32 devices in a mesh: grp: 2 (over x), blk: 16 (over z, y, core).
Axes of the slice: x: 2, y: 2, z: 4, core: 2. Of those that a mesh axis runs over, the one named last changes fastest.
Arguments:
- features: bfloat16 [512, 64, 256], P(('grp', 'blk')), parts along dimension 0, may hold values from -6 to 6
- occupancy: int32 [512, 64], P(('grp', 'blk')), parts along dimension 0, may hold values 0 or 1
- neighbors: int32 [512, 6], P(('grp', 'blk')), parts along dimension 0, may hold values from -1 to 15
- previous: bfloat16 [512, 64, 256], P(('grp', 'blk')), parts along dimension 0, may hold values from -6 to 6
- old_owner: int32 [512, 1], P(('grp', 'blk')), parts along dimension 0, may hold values from 0 to 15; in each aligned block of 16 rows (0 to 15, 16 to 31, ...) at most 2 rows name the same one
- old_slot: int32 [512], P(('grp', 'blk')), parts along dimension 0, may hold values from 0 to 15
- conv_weight: bfloat16 [27, 256, 256], replicated, may hold values from -0.078125 to 0.078125
- norm_scale: float32 [256], replicated, may hold values from 0.1 to 1.9
- norm_shift: float32 [256], replicated, may hold values from -3 to 3
- prev_weight: bfloat16 [256, 256], replicated, may hold values from -0.375 to 0.375
Outputs:
- merged: bfloat16 [512, 64, 256], P(('grp', 'blk')), parts along dimension 0
The draws below stay inside these ranges and needn't reach their ends.
There are 2 independent parts, one for each index of `grp`. The reference program is written for one: setup_inputs(seed, part) draws one part's arguments, and reference() takes and returns one part's arrays. A program takes and returns all parts, laid end to end along the dimension named above; an argument that names none is the same for every part. Nothing has to cross between parts.
Inputs may be any that keep to these rules, and one draw needn't show every extreme that they name: `old_owner`: among the 16 block slots of one device, at most 2 name the same old owner.
All inputs are finite; a program needn't handle non-finite values. No bound on the sum of `occupancy` on one device may be relied on, other than what follows from the above.
Results may differ from the reference program's by a relative error of at most 0.0034.
Values may be sent and summed in bfloat16 or wider, within the bound.
A program may use at most 128 MiB of HBM per device.

```python
import math
import jax
import jax.numpy as jnp
import numpy as np
from jax import lax

C = 256
EDGE = 4
TAPS = 27
B_DEV = 16
CAP = 2
VOX = 64
BLOCKS = 256
N_BLK = 16


def set_ends(values, rng, low, high):
    spot = [jax.random.randint(jax.random.fold_in(rng, axis), (), 0, length) for axis, length in enumerate(values.shape)]
    longest = values.shape.index(max(values.shape))
    next_to = spot[:longest] + [(spot[longest] + 1) % values.shape[longest]] + spot[longest + 1:]
    return values.at[tuple(spot)].set(low).at[tuple(next_to)].set(high)


def block_scale(key, dims, pieces, smallest, top_value):
    loudness, own = 1.0, jax.random.fold_in(key, 6)
    for axis_at, parts in pieces:
        draws = jnp.exp(jax.random.uniform(jax.random.fold_in(own, axis_at), (parts,), jnp.float32, smallest / len(pieces), top_value / len(pieces)))
        loudness = loudness * jnp.repeat(draws, dims[axis_at] // parts).reshape([-1 if axis == axis_at else 1 for axis in range(len(dims))])
    return loudness


def deal_out(rng, own, number, rows, count, top, most, slope):
    ranking = jax.random.permutation(rng, count)
    heavy_load, ordinary = load_shares(count, rows * top, most, slope, True), load_shares(count, rows * top, most, slope, False)
    places = jnp.arange(count)

    def named(sizes, rotation):
        used = int((sizes > 0).sum())
        fixed = max(1, used // 4)
        shifted = fixed + (places - fixed + rotation * (used - fixed)) % max(1, count - fixed)
        return jnp.zeros((count,), jnp.int32).at[ranking[jnp.where(places < fixed, places, shifted)]].set(jnp.asarray(sizes, jnp.int32))

    sizes = jnp.where(number % 4 == 0, named(heavy_load, number // 4), named(ordinary, number - number // 4 - 1))
    mixed = jax.random.permutation(jax.random.fold_in(own, 3), count)
    donor, receiver = mixed[0:count // 2 * 2:2], mixed[1:count // 2 * 2:2]
    room = jnp.minimum(sizes[donor] - 1, most - sizes[receiver]) // 2
    room = jnp.where((donor == ranking[0]) | (receiver == ranking[0]) | (sizes[receiver] == 0), 0, jnp.maximum(room, 0))
    shifted = jax.random.randint(jax.random.fold_in(own, 4), (count // 2,), 0, 1 << 20) % (room + 1)
    sizes = sizes.at[donor].add(-shifted).at[receiver].add(shifted)
    labels = jnp.searchsorted(jnp.cumsum(sizes), jnp.arange(rows * top), side="right").astype(jnp.int32)
    grid = labels.reshape(top, rows).T
    grid = grid[jax.random.permutation(jax.random.fold_in(own, 1), rows)]
    rotation = jax.random.randint(jax.random.fold_in(own, 2), (rows, 1), 0, top)
    return jnp.take_along_axis(grid, (jnp.arange(top)[None, :] + rotation) % top, axis=1)


def load_shares(amount, total, limit, lean, full):
    loads = [(1 << 20) // math.isqrt(rank ** lean) + 1 for rank in range(1, amount + 1)]
    largest = limit if full else min(limit, max(-(-total // amount), total * loads[0] // sum(loads)))
    least = 1 if total - largest >= amount - 1 else 0
    counts, surplus = [largest] + [least] * (amount - 1), total - largest - least * (amount - 1)
    while surplus > 0:
        free = [i for i in range(1, amount) if counts[i] < largest] or [i for i in range(1, amount) if counts[i] < limit]
        whole, remaining = sum([loads[i] for i in free]), surplus
        for i in free:
            more = min(limit - counts[i], max(1, remaining * loads[i] // whole), surplus)
            counts[i] = counts[i] + more
            surplus = surplus - more
    return np.array(counts)


def centred(own_key, dims, width, bound, shards=(), dtype=jnp.bfloat16):
    factor_of = block_scale(own_key, dims, shards, -0.22, 0.18) if shards else 1.0
    result = jax.random.normal(own_key, dims, jnp.float32) * width * factor_of
    return jnp.minimum(jnp.maximum(result, -bound), bound).astype(dtype)


def setup_inputs(seed: int = 0, part: int = 0) -> dict:
    key_of = jax.random.split(jax.random.key(seed), 11)
    own_keys = jax.random.split(jax.random.fold_in(key_of[10], part), 11)
    features = centred(own_keys[0], (BLOCKS, VOX, C), 1.0, 6.0, ((0, 16),))
    occupancy = set_ends((jax.random.randint(own_keys[1], (BLOCKS, VOX), 0, 4) < 3).astype(jnp.int32), jax.random.fold_in(own_keys[1], 1), 0, 1)
    neighbors = set_ends(jax.random.randint(own_keys[2], (BLOCKS, 6), -1, B_DEV), jax.random.fold_in(own_keys[2], 1), -1, B_DEV - 1).astype(jnp.int32)
    previous = centred(own_keys[3], (BLOCKS, VOX, C), 1.0, 6.0, ((0, 16),))
    old_owner_keys = jax.random.split(jax.random.fold_in(own_keys[4], 1), BLOCKS // B_DEV)
    old_owner_turns = jax.random.permutation(jax.random.fold_in(own_keys[4], 3), BLOCKS // B_DEV)
    old_owner = jax.vmap(lambda own, number: deal_out(jax.random.fold_in(own_keys[4], 2), own, number, B_DEV, N_BLK, 1, CAP, 2))(old_owner_keys, old_owner_turns).reshape((BLOCKS, 1))
    old_slot = set_ends(jax.random.randint(own_keys[5], (BLOCKS,), 0, B_DEV), jax.random.fold_in(own_keys[5], 1), 0, B_DEV - 1).astype(jnp.int32)
    conv_weight = centred(key_of[6], (TAPS, C, C), (TAPS * C) ** -0.5, 0.078125)
    norm_scale = jnp.clip(1.0 + 0.18 * jax.random.normal(key_of[7], (C,), jnp.float32), 0.1, 1.9)
    norm_shift = centred(key_of[8], (C,), 0.5, 3.0, (), jnp.float32)
    prev_weight = centred(key_of[9], (C, C), C ** -0.5, 0.375)
    return {"features": features, "occupancy": occupancy, "neighbors": neighbors, "previous": previous, "old_owner": old_owner, "old_slot": old_slot, "conv_weight": conv_weight, "norm_scale": norm_scale, "norm_shift": norm_shift, "prev_weight": prev_weight}


def face_layers(cube, slots, device_shift, layer, axis_pos):
    block_total = cube.shape[0]
    positions = jnp.arange(block_total).astype(jnp.int32)
    owner_dev = positions // B_DEV + device_shift
    valid = (slots >= 0) & (owner_dev >= 0) & (owner_dev < N_BLK)
    source = jnp.clip(owner_dev * B_DEV + slots, 0, block_total - 1).astype(jnp.int32)
    layers = jnp.take(cube, layer, axis=axis_pos)[source]
    return layers * valid.astype(jnp.bfloat16)[:, None, None, None]


def reference(features, occupancy, neighbors, previous, old_owner, old_slot, conv_weight, norm_scale, norm_shift, prev_weight):
    block_total = features.shape[0]
    occ_mask = occupancy.astype(jnp.bfloat16)[:, :, None]
    masked = features * occ_mask
    cube = masked.reshape(block_total, EDGE, EDGE, EDGE, C)
    volume = jnp.zeros((block_total, EDGE + 2, EDGE + 2, EDGE + 2, C), jnp.bfloat16)
    volume = volume.at[:, 1:EDGE + 1, 1:EDGE + 1, 1:EDGE + 1].set(cube)
    volume = volume.at[:, 0, 1:EDGE + 1, 1:EDGE + 1].set(face_layers(cube, neighbors[:, 0], -1, EDGE - 1, 1))
    volume = volume.at[:, EDGE + 1, 1:EDGE + 1, 1:EDGE + 1].set(face_layers(cube, neighbors[:, 1], 1, 0, 1))
    volume = volume.at[:, 1:EDGE + 1, 0, 1:EDGE + 1].set(face_layers(cube, neighbors[:, 2], 0, EDGE - 1, 2))
    volume = volume.at[:, 1:EDGE + 1, EDGE + 1, 1:EDGE + 1].set(face_layers(cube, neighbors[:, 3], 0, 0, 2))
    volume = volume.at[:, 1:EDGE + 1, 1:EDGE + 1, 0].set(face_layers(cube, neighbors[:, 4], 0, EDGE - 1, 3))
    volume = volume.at[:, 1:EDGE + 1, 1:EDGE + 1, EDGE + 1].set(face_layers(cube, neighbors[:, 5], 0, 0, 3))
    conv_out = jnp.zeros((block_total * EDGE * EDGE * EDGE, C), jnp.float32)
    for shift_a in range(3):
        for shift_b in range(3):
            for shift_c in range(3):
                window = volume[:, shift_a:shift_a + EDGE, shift_b:shift_b + EDGE, shift_c:shift_c + EDGE]
                conv_out = conv_out + jnp.dot(window.reshape(-1, C), conv_weight[(3 * shift_a + shift_b) * 3 + shift_c], preferred_element_type=jnp.float32)
    hidden = jnp.maximum(conv_out * norm_scale[None, :] + norm_shift[None, :], 0.0)
    source = (old_owner[:, 0] * B_DEV + old_slot).astype(jnp.int32)
    moved = previous[source]
    projected = jnp.dot(moved.reshape(-1, C), prev_weight, preferred_element_type=jnp.float32).astype(jnp.bfloat16)
    projected = lax.optimization_barrier(projected)
    occ_float = occupancy.astype(jnp.float32).reshape(-1, 1)
    merged = (hidden + projected.astype(jnp.float32)) * occ_float
    return merged.reshape(block_total, EDGE * EDGE * EDGE, C).astype(jnp.bfloat16)
```

```python
import functools

import jax
import jax.numpy as jnp
from jax import lax
from jax.experimental import pallas as pl
from jax.experimental.pallas import tpu as pltpu
from jax.sharding import PartitionSpec as P

EDGE = 4
FACE = EDGE * EDGE
VOX = EDGE * FACE
CAP = 2
LANES = 128
EXTRA = 2
TABLE = 4
MESH = pl.DeviceIdType.MESH
F32 = jnp.float32
BF16 = jnp.bfloat16


def iota(shape, dim):
    return lax.broadcasted_iota(jnp.int32, shape, dim)


def one_hot(hit):
    return jnp.where(hit, 1.0, 0.0).astype(BF16)


def kernel_full(
    count,
    slots,
    channels,
    owner_hbm,
    slot_hbm,
    nb_hbm,
    scale_hbm,
    shift_hbm,
    feat_hbm,
    prev_hbm,
    occ_hbm,
    w_hbm,
    pw_hbm,
    out_ref,
    owner_s,
    slot_s,
    nb_ref,
    occ_ref,
    scale_ref,
    shift_ref,
    feat,
    prev,
    weight,
    pweight,
    proj,
    table,
    reqs,
    reqs_s,
    sendbuf,
    recv,
    low_layer,
    high_layer,
    low_occ,
    high_occ,
    volume,
    acc,
    mask,
    base,
    small_sem,
    local_sem,
    halo_send,
    halo_recv,
    rq_send,
    rq_recv,
    rp_send,
    rp_recv,
):
    me = lax.axis_index("blk")
    layer_rows = FACE * slots
    barrier = pltpu.get_barrier_semaphore()

    @pl.loop(1, count)
    def _(i):
        peer = lax.rem(me + i, count)
        pl.semaphore_signal(barrier, inc=1, device_id={"blk": peer}, device_id_type=MESH)

    small = [
        pltpu.make_async_copy(owner_hbm, owner_s, small_sem.at[0]),
        pltpu.make_async_copy(slot_hbm, slot_s, small_sem.at[1]),
        pltpu.make_async_copy(occ_hbm, occ_ref, small_sem.at[2]),
        pltpu.make_async_copy(nb_hbm, nb_ref, small_sem.at[3]),
        pltpu.make_async_copy(scale_hbm, scale_ref, small_sem.at[4]),
        pltpu.make_async_copy(shift_hbm, shift_ref, small_sem.at[5]),
    ]
    for load in small:
        load.start()
    loads = [
        pltpu.make_async_copy(prev_hbm, prev, local_sem.at[0]),
        pltpu.make_async_copy(pw_hbm, pweight, local_sem.at[1]),
        pltpu.make_async_copy(feat_hbm, feat, local_sem.at[2]),
        pltpu.make_async_copy(w_hbm, weight, local_sem.at[3]),
    ]
    for load in loads:
        load.start()

    small[0].wait()
    small[1].wait()

    lane = iota((1, LANES), 1)
    first = jnp.zeros((1, LANES), jnp.int32)
    last = jnp.zeros((1, LANES), jnp.int32)
    for s in range(slots):
        last = jnp.where(lane == owner_s[s], slot_s[s], last)
        t = slots - 1 - s
        first = jnp.where(lane == owner_s[t], slot_s[t], first)
    row = iota((CAP, LANES), 0)
    table[...] = jnp.where(row == 0, first, last)

    def layer_occ(occ, x):
        spread = one_hot(iota((VOX, layer_rows), 0) == x * FACE + iota((VOX, layer_rows), 1) % FACE)
        rows = jnp.dot(occ, spread, preferred_element_type=F32)
        own = iota((slots, layer_rows), 0) == iota((slots, layer_rows), 1) // FACE
        return jnp.sum(jnp.where(own, rows, 0.0), axis=0, keepdims=True).astype(BF16)

    pl.semaphore_wait(barrier, count - 1)

    def request(i):
        return pltpu.make_async_remote_copy(
            src_ref=table,
            dst_ref=reqs.at[me],
            send_sem=rq_send.at[i],
            recv_sem=rq_recv.at[i],
            device_id={"blk": lax.rem(me + i, count)},
            device_id_type=MESH,
        )

    @pl.loop(1, count)
    def _(i):
        request(i).start()

    up = lax.rem(me + 1, count)
    down = lax.rem(me + count - 1, count)

    def halo(k):
        if k < 2:
            src = feat_hbm.at[:, pl.ds((EDGE - 1) * FACE, FACE), :] if k == 0 else occ_hbm
            dst = low_layer if k == 0 else low_occ
            peer = up
        else:
            src = feat_hbm.at[:, pl.ds(0, FACE), :] if k == 2 else occ_hbm
            dst = high_layer if k == 2 else high_occ
            peer = down
        return pltpu.make_async_remote_copy(
            src_ref=src,
            dst_ref=dst,
            send_sem=halo_send.at[k],
            recv_sem=halo_recv.at[k],
            device_id={"blk": peer},
            device_id_type=MESH,
        )

    @pl.when(me < count - 1)
    def _():
        halo(0).start()
        halo(1).start()

    @pl.when(me > 0)
    def _():
        halo(2).start()
        halo(3).start()

    @pl.when(me == 0)
    def _():
        low_layer[...] = jnp.zeros_like(low_layer)
        low_occ[...] = jnp.zeros_like(low_occ)

    @pl.when(me == count - 1)
    def _():
        high_layer[...] = jnp.zeros_like(high_layer)
        high_occ[...] = jnp.zeros_like(high_occ)

    loads[0].wait()
    loads[1].wait()

    blocks = layer_rows // VOX
    for s in range(0, slots, blocks):
        rows = prev[s : s + blocks].reshape(layer_rows, channels)
        part = jnp.dot(rows, pweight[...], preferred_element_type=F32).astype(BF16)
        proj[s : s + blocks] = part.reshape(blocks, VOX, channels)

    reqs_s_copy = pltpu.make_async_copy(reqs, reqs_s, local_sem.at[4])

    def reply(i):
        return pltpu.make_async_remote_copy(
            src_ref=sendbuf.at[i],
            dst_ref=recv.at[me],
            send_sem=rp_send.at[i],
            recv_sem=rp_recv.at[i],
            device_id={"blk": lax.rem(me + i, count)},
            device_id_type=MESH,
        )

    reqs[me] = table[...]

    @pl.loop(1, count)
    def _(i):
        request(i).wait_recv()

    reqs_s_copy.start()
    reqs_s_copy.wait()

    def far_first(k):
        step = (k + 1) // 2
        return count // 2 + step * (2 * (k % 2) - 1)

    @pl.loop(0, count - 1)
    def _(k):
        i = far_first(k)
        peer = lax.rem(me + i, count)
        sendbuf[i, 0] = proj[reqs_s[peer, 0, me]]
        sendbuf[i, 1] = proj[reqs_s[peer, 1, me]]

    @pl.loop(0, count - 1)
    def _(k):
        reply(far_first(k)).start()

    recv[me, 0] = proj[reqs_s[me, 0, me]]
    recv[me, 1] = proj[reqs_s[me, 1, me]]

    for load in small[2:]:
        load.wait()
    occ = occ_ref[...].astype(BF16)
    volume[...] = jnp.zeros_like(volume)
    loads[2].wait()
    col = iota((layer_rows, layer_rows), 1)
    line = iota((layer_rows, layer_rows), 0)
    select_own = one_hot(col == (line % slots) * FACE + line // slots)
    spread = one_hot(iota((layer_rows, slots), 0) % slots == iota((layer_rows, slots), 1))
    nb = lax.dot_general(
        spread,
        nb_ref[...].astype(F32).astype(BF16),
        (((1,), (1,)), ((), ())),
        preferred_element_type=F32,
    ).astype(jnp.int32)
    side_rows = EDGE * slots
    scol = iota((side_rows, layer_rows), 1)
    sline = iota((side_rows, 1), 0) // slots

    def side(f, fixed, step):
        wanted = nb[:side_rows, f : f + 1]
        target = jnp.where(wanted >= 0, wanted * FACE + fixed + sline * step, -1)
        return one_hot(scol == target)

    sides = [
        side(2, (EDGE - 1) * EDGE, 1),
        side(3, 0, 1),
        side(4, EDGE - 1, EDGE),
        side(5, 0, EDGE),
    ]
    select = jnp.concatenate([select_own] + sides, axis=0)
    for x in range(EDGE):
        layer = feat[:, x * FACE : (x + 1) * FACE, :].reshape(layer_rows, channels)
        part = jnp.dot(select * layer_occ(occ, x), layer, preferred_element_type=F32).astype(BF16)
        volume[x + 1, 1 : EDGE + 1, 1 : EDGE + 1] = part[:layer_rows].reshape(
            EDGE, EDGE, slots, channels
        )
        faces = part[layer_rows:].reshape(4, EDGE, slots, channels)
        volume[x + 1, 0, 1 : EDGE + 1] = faces[0]
        volume[x + 1, EDGE + 1, 1 : EDGE + 1] = faces[1]
        volume[x + 1, 1 : EDGE + 1, 0] = faces[2]
        volume[x + 1, 1 : EDGE + 1, EDGE + 1] = faces[3]

    @pl.when(me > 0)
    def _():
        pltpu.make_async_remote_copy(
            src_ref=feat_hbm.at[:, pl.ds(0, FACE), :],
            dst_ref=low_layer,
            send_sem=halo_send.at[0],
            recv_sem=halo_recv.at[0],
            device_id={"blk": up},
            device_id_type=MESH,
        ).wait_recv()
        halo(1).wait_recv()

    @pl.when(me < count - 1)
    def _():
        halo(2).wait_recv()
        halo(3).wait_recv()

    def x_face(f, layer_ref, other_occ, x):
        wanted = nb[:, f : f + 1]
        target = jnp.where(wanted >= 0, wanted * FACE + iota((layer_rows, 1), 0) // slots, -1)
        pick = one_hot(col == target) * layer_occ(other_occ[...].astype(BF16), x)
        layer = layer_ref[...].reshape(layer_rows, channels)
        part = jnp.dot(pick, layer, preferred_element_type=F32).astype(BF16)
        return part.reshape(EDGE, EDGE, slots, channels)

    volume[0, 1 : EDGE + 1, 1 : EDGE + 1] = x_face(0, low_layer, low_occ, EDGE - 1)
    volume[EDGE + 1, 1 : EDGE + 1, 1 : EDGE + 1] = x_face(1, high_layer, high_occ, 0)

    loads[3].wait()
    scale = scale_ref[...]
    shift = shift_ref[...]

    @pl.loop(0, EDGE)
    def _(x):
        total = jnp.zeros((layer_rows, channels), F32)
        for tap in range(27):
            a, b, c = tap // 9, (tap // 3) % 3, tap % 3
            window = volume[x + a, b : b + EDGE, c : c + EDGE].reshape(layer_rows, channels)
            total = total + jnp.dot(window, weight[tap], preferred_element_type=F32)
        hidden = jnp.maximum(total * scale + shift, 0.0)
        for k in range(channels // LANES):
            acc[k, pl.ds(x * layer_rows, layer_rows), :] = hidden[:, k * LANES : (k + 1) * LANES]

    @pl.loop(0, slots)
    def _(s):
        mine = jnp.where(iota((VOX, VOX), 0) == iota((VOX, VOX), 1), occ_ref[pl.ds(s, 1), :], 0)
        mask[pl.ds(s * VOX, VOX), :] = jnp.dot(
            mine.astype(BF16), jnp.ones((VOX, channels), BF16), preferred_element_type=F32
        )

    picks = []
    for s in range(slots):
        rank = jnp.int32(0)
        for t in range(s):
            rank = jnp.where(owner_s[t] == owner_s[s], 1, rank)
        picks.append(rank)
        hidden = jnp.concatenate(
            [acc[k, pl.ds(s, VOX, stride=slots), :] for k in range(channels // LANES)],
            axis=1,
        )
        base[s] = hidden * mask[s * VOX : (s + 1) * VOX, :]

    @pl.loop(1, count)
    def _(i):
        reply(i).wait_recv()

    for s in range(slots):
        moved = recv[owner_s[s], picks[s]].astype(F32)
        out_ref[s] = (base[s] + moved * mask[s * VOX : (s + 1) * VOX, :]).astype(BF16)

    @pl.loop(1, count)
    def _(i):
        request(i).wait_send()
        reply(i).wait_send()

    @pl.when(me < count - 1)
    def _():
        halo(0).wait_send()
        halo(1).wait_send()

    @pl.when(me > 0)
    def _():
        halo(2).wait_send()
        halo(3).wait_send()


def merge_full(
    features,
    occupancy,
    neighbors,
    previous,
    old_owner,
    old_slot,
    conv_weight,
    norm_scale,
    norm_shift,
    prev_weight,
):
    slots, vox, channels = features.shape
    count = lax.axis_size("blk")
    hbm = pl.BlockSpec(memory_space=pl.ANY)
    volume_shape = (EDGE + 2, EDGE + 2, EDGE + 2, slots, channels)
    dma = pltpu.SemaphoreType.DMA
    return pl.pallas_call(
        functools.partial(kernel_full, count, slots, channels),
        out_shape=pltpu.VMEM(features.shape, BF16),
        in_specs=[hbm] * 10,
        out_specs=pl.BlockSpec(memory_space=pltpu.VMEM),
        scratch_shapes=[
            pltpu.SMEM((slots,), jnp.int32),
            pltpu.SMEM((slots,), jnp.int32),
            pltpu.VMEM((6, slots), jnp.int32),
            pltpu.VMEM((slots, vox), jnp.int32),
            pltpu.VMEM((1, channels), F32),
            pltpu.VMEM((1, channels), F32),
            pltpu.VMEM(features.shape, BF16),
            pltpu.VMEM(previous.shape, BF16),
            pltpu.VMEM(conv_weight.shape, BF16),
            pltpu.VMEM(prev_weight.shape, BF16),
            pltpu.VMEM(previous.shape, BF16),
            pltpu.VMEM((CAP, LANES), jnp.int32),
            pltpu.VMEM((count, CAP, LANES), jnp.int32),
            pltpu.SMEM((count, CAP, LANES), jnp.int32),
            pltpu.VMEM((count, CAP, vox, channels), BF16),
            pltpu.VMEM((count, CAP, vox, channels), BF16),
            pltpu.VMEM((slots, FACE, channels), BF16),
            pltpu.VMEM((slots, FACE, channels), BF16),
            pltpu.VMEM((slots, vox), jnp.int32),
            pltpu.VMEM((slots, vox), jnp.int32),
            pltpu.VMEM(volume_shape, BF16),
            pltpu.VMEM((channels // LANES, slots * vox, LANES), F32),
            pltpu.VMEM((slots * vox, channels), F32),
            pltpu.VMEM(features.shape, F32),
            dma((6,)),
            dma((6,)),
            dma((4,)),
            dma((4,)),
            dma((count,)),
            dma((count,)),
            dma((count,)),
            dma((count,)),
        ],
        compiler_params=pltpu.CompilerParams(
            collective_id=1, has_side_effects=True, vmem_limit_bytes=66_000_000
        ),
        name="merge_full",
    )(
        old_owner[:, 0],
        old_slot,
        neighbors.T,
        norm_scale[None, :],
        norm_shift[None, :],
        features,
        previous,
        occupancy,
        conv_weight,
        prev_weight,
    )


def kernel(
    count,
    groups,
    slots,
    channels,
    owner_hbm,
    slot_hbm,
    nb_hbm,
    scale_hbm,
    shift_hbm,
    feat_hbm,
    prev_hbm,
    occ_hbm,
    w_hbm,
    pw_hbm,
    out_ref,
    over_ref,
    owner_s,
    slot_s,
    nb_ref,
    occ_ref,
    scale_ref,
    shift_ref,
    feat,
    prev,
    weight,
    pweight,
    proj,
    table,
    reqs,
    reqs_s,
    place_s,
    over,
    overs,
    overs_s,
    send_first,
    send_row,
    send_z,
    send_x,
    relay_z,
    relay_x,
    relay_out,
    recv,
    low_layer,
    high_layer,
    low_occ,
    high_occ,
    volume,
    acc,
    mask,
    base,
    small_sem,
    local_sem,
    halo_send,
    halo_recv,
    rq_send,
    rq_recv,
    first_send,
    first_recv,
    row_send,
    row_recv,
    z_send,
    z_recv,
    x_send,
    x_recv,
    out_send,
    out_recv,
    over_send,
    over_recv,
):
    me = lax.axis_index("blk")
    grp = lax.axis_index("grp")
    half, row = count // 2, count // 4
    half_base = me // half * half
    row_base = me // row * row
    half_at, row_at = me - half_base, me - row_base
    other_half = half - half_base
    other_row = 2 * half_base + row - row_base
    across = lax.rem(me + half, count)
    beside = other_row + row_at
    row_part, z_part, x_part = count, count + row, count + row + EXTRA
    layer_rows = FACE * slots
    barrier = pltpu.get_barrier_semaphore()

    @pl.loop(1, count)
    def _(i):
        peer = lax.rem(me + i, count)
        pl.semaphore_signal(barrier, inc=1, device_id={"blk": peer}, device_id_type=MESH)

    for i in range(1, groups):
        there = lax.rem(grp + i, groups)
        pl.semaphore_signal(barrier, inc=1, device_id={"grp": there}, device_id_type=MESH)

    small = [
        pltpu.make_async_copy(owner_hbm, owner_s, small_sem.at[0]),
        pltpu.make_async_copy(slot_hbm, slot_s, small_sem.at[1]),
        pltpu.make_async_copy(occ_hbm, occ_ref, small_sem.at[2]),
        pltpu.make_async_copy(nb_hbm, nb_ref, small_sem.at[3]),
        pltpu.make_async_copy(scale_hbm, scale_ref, small_sem.at[4]),
        pltpu.make_async_copy(shift_hbm, shift_ref, small_sem.at[5]),
    ]
    for load in small:
        load.start()
    loads = [
        pltpu.make_async_copy(prev_hbm, prev, local_sem.at[0]),
        pltpu.make_async_copy(pw_hbm, pweight, local_sem.at[1]),
        pltpu.make_async_copy(feat_hbm, feat, local_sem.at[2]),
        pltpu.make_async_copy(w_hbm, weight, local_sem.at[3]),
    ]
    for load in loads:
        load.start()

    small[0].wait()
    small[1].wait()

    lane = iota((1, LANES), 1)
    first = jnp.zeros((1, LANES), jnp.int32)
    last = jnp.zeros((1, LANES), jnp.int32)
    for s in range(slots):
        last = jnp.where(lane == owner_s[s], slot_s[s], last)
        t = slots - 1 - s
        first = jnp.where(lane == owner_s[t], slot_s[t], first)
    zero = jnp.int32(0)
    x_count, z_count = zero, zero
    x_owner, z_owner = [zero] * EXTRA, [zero] * EXTRA
    for s in range(slots):
        owner = owner_s[s]
        again = zero
        for t in range(s):
            again = jnp.where(owner_s[t] == owner, 1, again)
        far = jnp.where((owner < half_base) | (owner >= half_base + half), again, 0)
        near = jnp.where((owner >= other_row) & (owner < other_row + row), again, 0)
        for e in range(EXTRA):
            x_owner[e] = jnp.where((far == 1) & (x_count == e), owner - other_half, x_owner[e])
            z_owner[e] = jnp.where((near == 1) & (z_count == e), owner - other_row, z_owner[e])
        at = jnp.where(again == 1, row_part + owner - row_base, owner)
        at = jnp.where(near == 1, z_part + jnp.minimum(z_count, EXTRA - 1), at)
        place_s[s] = jnp.where(far == 1, x_part + jnp.minimum(x_count, EXTRA - 1), at)
        x_count = x_count + far
        z_count = z_count + near
    notes = jnp.where(lane == 2 * EXTRA, jnp.where((x_count > EXTRA) | (z_count > EXTRA), 1, 0), 0)
    for e in range(EXTRA):
        notes = jnp.where(lane == e, x_owner[e], notes)
        notes = jnp.where(lane == EXTRA + e, z_owner[e], notes)
    line = iota((TABLE, LANES), 0)
    table[...] = jnp.where(line == 0, first, jnp.where(line == 1, last, notes))

    def layer_occ(occ, x):
        spread = one_hot(iota((VOX, layer_rows), 0) == x * FACE + iota((VOX, layer_rows), 1) % FACE)
        rows = jnp.dot(occ, spread, preferred_element_type=F32)
        own = iota((slots, layer_rows), 0) == iota((slots, layer_rows), 1) // FACE
        return jnp.sum(jnp.where(own, rows, 0.0), axis=0, keepdims=True).astype(BF16)

    pl.semaphore_wait(barrier, count + groups - 2)

    def request(i):
        return pltpu.make_async_remote_copy(
            src_ref=table,
            dst_ref=reqs.at[me],
            send_sem=rq_send.at[i],
            recv_sem=rq_recv.at[i],
            device_id={"blk": lax.rem(me + i, count)},
            device_id_type=MESH,
        )

    @pl.loop(1, count)
    def _(i):
        request(i).start()

    up = lax.rem(me + 1, count)
    down = lax.rem(me + count - 1, count)

    def halo(k):
        if k < 2:
            src = feat_hbm.at[:, pl.ds((EDGE - 1) * FACE, FACE), :] if k == 0 else occ_hbm
            dst = low_layer if k == 0 else low_occ
            peer = up
        else:
            src = feat_hbm.at[:, pl.ds(0, FACE), :] if k == 2 else occ_hbm
            dst = high_layer if k == 2 else high_occ
            peer = down
        return pltpu.make_async_remote_copy(
            src_ref=src,
            dst_ref=dst,
            send_sem=halo_send.at[k],
            recv_sem=halo_recv.at[k],
            device_id={"blk": peer},
            device_id_type=MESH,
        )

    @pl.when(me < count - 1)
    def _():
        halo(0).start()
        halo(1).start()

    @pl.when(me > 0)
    def _():
        halo(2).start()
        halo(3).start()

    @pl.when(me == 0)
    def _():
        low_layer[...] = jnp.zeros_like(low_layer)
        low_occ[...] = jnp.zeros_like(low_occ)

    @pl.when(me == count - 1)
    def _():
        high_layer[...] = jnp.zeros_like(high_layer)
        high_occ[...] = jnp.zeros_like(high_occ)

    loads[0].wait()
    loads[1].wait()

    blocks = layer_rows // VOX
    for s in range(0, slots, blocks):
        rows = prev[s : s + blocks].reshape(layer_rows, channels)
        part = jnp.dot(rows, pweight[...], preferred_element_type=F32).astype(BF16)
        proj[s : s + blocks] = part.reshape(blocks, VOX, channels)

    reqs[me] = table[...]
    reqs_s_copy = pltpu.make_async_copy(reqs, reqs_s, local_sem.at[4])

    def in_half(i):
        return half_base + lax.rem(half_at + i, half)

    def in_row(i):
        return row_base + lax.rem(row_at + i, row)

    def first_to(i):
        return pltpu.make_async_remote_copy(
            src_ref=send_first.at[i],
            dst_ref=recv.at[me],
            send_sem=first_send.at[i],
            recv_sem=first_recv.at[i],
            device_id={"blk": lax.rem(me + i, count)},
            device_id_type=MESH,
        )

    def row_to(i):
        return pltpu.make_async_remote_copy(
            src_ref=send_row.at[i],
            dst_ref=recv.at[row_part + row_at],
            send_sem=row_send.at[i],
            recv_sem=row_recv.at[i],
            device_id={"blk": in_row(i)},
            device_id_type=MESH,
        )

    def z_to(i):
        return pltpu.make_async_remote_copy(
            src_ref=send_z.at[i],
            dst_ref=relay_z.at[row_at],
            send_sem=z_send.at[i],
            recv_sem=z_recv.at[i],
            device_id={"blk": in_row(i)},
            device_id_type=MESH,
        )

    def x_to(i):
        return pltpu.make_async_remote_copy(
            src_ref=send_x.at[i],
            dst_ref=relay_x.at[half_at],
            send_sem=x_send.at[i],
            recv_sem=x_recv.at[i],
            device_id={"blk": in_half(i)},
            device_id_type=MESH,
        )

    def relay(k):
        part, peer = ((x_part, across), (z_part, beside))[k]
        return pltpu.make_async_remote_copy(
            src_ref=relay_out.at[pl.ds(k * EXTRA, EXTRA)],
            dst_ref=recv.at[pl.ds(part, EXTRA)],
            send_sem=out_send.at[k],
            recv_sem=out_recv.at[k],
            device_id={"blk": peer},
            device_id_type=MESH,
        )

    def over_to(i):
        return pltpu.make_async_remote_copy(
            src_ref=over,
            dst_ref=overs.at[grp],
            send_sem=over_send.at[i],
            recv_sem=over_recv.at[i],
            device_id={"grp": lax.rem(grp + i, groups)},
            device_id_type=MESH,
        )

    @pl.loop(1, count)
    def _(i):
        request(i).wait_recv()

    reqs_s_copy.start()
    reqs_s_copy.wait()

    @pl.loop(1, half)
    def _(i):
        send_x[i] = proj[reqs_s[lax.rem(in_half(i) + half, count), 1, me]]
        x_to(i).start()

    @pl.loop(1, row)
    def _(i):
        send_z[i] = proj[reqs_s[other_row + lax.rem(row_at + i, row), 1, me]]
        z_to(i).start()

    def far_first(k):
        step = (k + 1) // 2
        return count // 2 + step * (2 * (k % 2) - 1)

    @pl.loop(0, count - 1)
    def _(k):
        i = far_first(k)
        send_first[i] = proj[reqs_s[lax.rem(me + i, count), 0, me]]
        first_to(i).start()

    @pl.loop(1, row)
    def _(i):
        send_row[i] = proj[reqs_s[in_row(i), 1, me]]
        row_to(i).start()

    recv[me] = proj[reqs_s[me, 0, me]]
    recv[row_part + row_at] = proj[reqs_s[me, 1, me]]
    relay_x[half_at] = proj[reqs_s[across, 1, me]]
    relay_z[row_at] = proj[reqs_s[beside, 1, me]]

    any_over = zero
    for d in range(count):
        any_over = any_over + reqs_s[d, 2, 2 * EXTRA]
    over[...] = jnp.zeros_like(over) + any_over
    for i in range(1, groups):
        over_to(i).start()

    for load in small[2:]:
        load.wait()
    occ = occ_ref[...].astype(BF16)
    volume[...] = jnp.zeros_like(volume)
    loads[2].wait()
    col = iota((layer_rows, layer_rows), 1)
    line = iota((layer_rows, layer_rows), 0)
    select_own = one_hot(col == (line % slots) * FACE + line // slots)
    spread = one_hot(iota((layer_rows, slots), 0) % slots == iota((layer_rows, slots), 1))
    nb = lax.dot_general(
        spread,
        nb_ref[...].astype(F32).astype(BF16),
        (((1,), (1,)), ((), ())),
        preferred_element_type=F32,
    ).astype(jnp.int32)
    side_rows = EDGE * slots
    scol = iota((side_rows, layer_rows), 1)
    sline = iota((side_rows, 1), 0) // slots

    def side(f, fixed, step):
        wanted = nb[:side_rows, f : f + 1]
        target = jnp.where(wanted >= 0, wanted * FACE + fixed + sline * step, -1)
        return one_hot(scol == target)

    sides = [
        side(2, (EDGE - 1) * EDGE, 1),
        side(3, 0, 1),
        side(4, EDGE - 1, EDGE),
        side(5, 0, EDGE),
    ]
    select = jnp.concatenate([select_own] + sides, axis=0)
    for x in range(EDGE):
        layer = feat[:, x * FACE : (x + 1) * FACE, :].reshape(layer_rows, channels)
        part = jnp.dot(select * layer_occ(occ, x), layer, preferred_element_type=F32).astype(BF16)
        volume[x + 1, 1 : EDGE + 1, 1 : EDGE + 1] = part[:layer_rows].reshape(
            EDGE, EDGE, slots, channels
        )
        faces = part[layer_rows:].reshape(4, EDGE, slots, channels)
        volume[x + 1, 0, 1 : EDGE + 1] = faces[0]
        volume[x + 1, EDGE + 1, 1 : EDGE + 1] = faces[1]
        volume[x + 1, 1 : EDGE + 1, 0] = faces[2]
        volume[x + 1, 1 : EDGE + 1, EDGE + 1] = faces[3]

    @pl.when(me > 0)
    def _():
        pltpu.make_async_remote_copy(
            src_ref=feat_hbm.at[:, pl.ds(0, FACE), :],
            dst_ref=low_layer,
            send_sem=halo_send.at[0],
            recv_sem=halo_recv.at[0],
            device_id={"blk": up},
            device_id_type=MESH,
        ).wait_recv()
        halo(1).wait_recv()

    @pl.when(me < count - 1)
    def _():
        halo(2).wait_recv()
        halo(3).wait_recv()

    def x_face(f, layer_ref, other_occ, x):
        wanted = nb[:, f : f + 1]
        target = jnp.where(wanted >= 0, wanted * FACE + iota((layer_rows, 1), 0) // slots, -1)
        pick = one_hot(col == target) * layer_occ(other_occ[...].astype(BF16), x)
        layer = layer_ref[...].reshape(layer_rows, channels)
        part = jnp.dot(pick, layer, preferred_element_type=F32).astype(BF16)
        return part.reshape(EDGE, EDGE, slots, channels)

    volume[0, 1 : EDGE + 1, 1 : EDGE + 1] = x_face(0, low_layer, low_occ, EDGE - 1)
    volume[EDGE + 1, 1 : EDGE + 1, 1 : EDGE + 1] = x_face(1, high_layer, high_occ, 0)

    @pl.loop(1, half)
    def _(i):
        x_to(i).wait_recv()

    @pl.loop(1, row)
    def _(i):
        z_to(i).wait_recv()

    for e in range(EXTRA):
        relay_out[e] = relay_x[reqs_s[across, 2, e]]
        relay_out[EXTRA + e] = relay_z[reqs_s[beside, 2, EXTRA + e]]
    relay(0).start()
    relay(1).start()

    loads[3].wait()
    scale = scale_ref[...]
    shift = shift_ref[...]

    @pl.loop(0, EDGE)
    def _(x):
        total = jnp.zeros((layer_rows, channels), F32)
        for tap in range(27):
            a, b, c = tap // 9, (tap // 3) % 3, tap % 3
            window = volume[x + a, b : b + EDGE, c : c + EDGE].reshape(layer_rows, channels)
            total = total + jnp.dot(window, weight[tap], preferred_element_type=F32)
        hidden = jnp.maximum(total * scale + shift, 0.0)
        for k in range(channels // LANES):
            acc[k, pl.ds(x * layer_rows, layer_rows), :] = hidden[:, k * LANES : (k + 1) * LANES]

    @pl.loop(0, slots)
    def _(s):
        mine = jnp.where(iota((VOX, VOX), 0) == iota((VOX, VOX), 1), occ_ref[pl.ds(s, 1), :], 0)
        mask[pl.ds(s * VOX, VOX), :] = jnp.dot(
            mine.astype(BF16), jnp.ones((VOX, channels), BF16), preferred_element_type=F32
        )

    for s in range(slots):
        hidden = jnp.concatenate(
            [acc[k, pl.ds(s, VOX, stride=slots), :] for k in range(channels // LANES)],
            axis=1,
        )
        base[s] = hidden * mask[s * VOX : (s + 1) * VOX, :]

    overs[grp] = over[...]
    for i in range(1, groups):
        over_to(i).wait_recv()
    overs_s_copy = pltpu.make_async_copy(overs, overs_s, local_sem.at[5])
    overs_s_copy.start()
    overs_s_copy.wait()
    total_over = zero
    for g in range(groups):
        total_over = total_over + overs_s[g, 0, 0]
    over_ref[0] = total_over

    @pl.loop(1, count)
    def _(i):
        first_to(i).wait_recv()

    @pl.loop(1, row)
    def _(i):
        row_to(i).wait_recv()

    relay(0).wait_recv()
    relay(1).wait_recv()

    for s in range(slots):
        moved = recv[place_s[s]].astype(F32)
        out_ref[s] = (base[s] + moved * mask[s * VOX : (s + 1) * VOX, :]).astype(BF16)

    @pl.loop(1, count)
    def _(i):
        request(i).wait_send()
        first_to(i).wait_send()

    @pl.loop(1, half)
    def _(i):
        x_to(i).wait_send()

    @pl.loop(1, row)
    def _(i):
        row_to(i).wait_send()
        z_to(i).wait_send()

    relay(0).wait_send()
    relay(1).wait_send()
    for i in range(1, groups):
        over_to(i).wait_send()

    @pl.when(me < count - 1)
    def _():
        halo(0).wait_send()
        halo(1).wait_send()

    @pl.when(me > 0)
    def _():
        halo(2).wait_send()
        halo(3).wait_send()


def per_device(
    features,
    occupancy,
    neighbors,
    previous,
    old_owner,
    old_slot,
    conv_weight,
    norm_scale,
    norm_shift,
    prev_weight,
):
    slots, vox, channels = features.shape
    count = lax.axis_size("blk")
    groups = lax.axis_size("grp")
    half, row = count // 2, count // 4
    hbm = pl.BlockSpec(memory_space=pl.ANY)
    volume_shape = (EDGE + 2, EDGE + 2, EDGE + 2, slots, channels)
    dma = pltpu.SemaphoreType.DMA
    return pl.pallas_call(
        functools.partial(kernel, count, groups, slots, channels),
        out_shape=[
            pltpu.VMEM(features.shape, BF16),
            jax.ShapeDtypeStruct((1,), jnp.int32),
        ],
        in_specs=[hbm] * 10,
        out_specs=[
            pl.BlockSpec(memory_space=pltpu.VMEM),
            pl.BlockSpec(memory_space=pltpu.SMEM),
        ],
        scratch_shapes=[
            pltpu.SMEM((slots,), jnp.int32),
            pltpu.SMEM((slots,), jnp.int32),
            pltpu.VMEM((6, slots), jnp.int32),
            pltpu.VMEM((slots, vox), jnp.int32),
            pltpu.VMEM((1, channels), F32),
            pltpu.VMEM((1, channels), F32),
            pltpu.VMEM(features.shape, BF16),
            pltpu.VMEM(previous.shape, BF16),
            pltpu.VMEM(conv_weight.shape, BF16),
            pltpu.VMEM(prev_weight.shape, BF16),
            pltpu.VMEM(previous.shape, BF16),
            pltpu.VMEM((TABLE, LANES), jnp.int32),
            pltpu.VMEM((count, TABLE, LANES), jnp.int32),
            pltpu.SMEM((count, TABLE, LANES), jnp.int32),
            pltpu.SMEM((slots,), jnp.int32),
            pltpu.VMEM((TABLE, LANES), jnp.int32),
            pltpu.VMEM((groups, TABLE, LANES), jnp.int32),
            pltpu.SMEM((groups, TABLE, LANES), jnp.int32),
            pltpu.VMEM((count, vox, channels), BF16),
            pltpu.VMEM((row, vox, channels), BF16),
            pltpu.VMEM((row, vox, channels), BF16),
            pltpu.VMEM((half, vox, channels), BF16),
            pltpu.VMEM((row, vox, channels), BF16),
            pltpu.VMEM((half, vox, channels), BF16),
            pltpu.VMEM((2 * EXTRA, vox, channels), BF16),
            pltpu.VMEM((count + row + 2 * EXTRA, vox, channels), BF16),
            pltpu.VMEM((slots, FACE, channels), BF16),
            pltpu.VMEM((slots, FACE, channels), BF16),
            pltpu.VMEM((slots, vox), jnp.int32),
            pltpu.VMEM((slots, vox), jnp.int32),
            pltpu.VMEM(volume_shape, BF16),
            pltpu.VMEM((channels // LANES, slots * vox, LANES), F32),
            pltpu.VMEM((slots * vox, channels), F32),
            pltpu.VMEM(features.shape, F32),
            dma((6,)),
            dma((6,)),
            dma((4,)),
            dma((4,)),
            dma((count,)),
            dma((count,)),
            dma((count,)),
            dma((count,)),
            dma((row,)),
            dma((row,)),
            dma((row,)),
            dma((row,)),
            dma((half,)),
            dma((half,)),
            dma((2,)),
            dma((2,)),
            dma((groups,)),
            dma((groups,)),
        ],
        compiler_params=pltpu.CompilerParams(
            collective_id=0, has_side_effects=True, vmem_limit_bytes=66_000_000
        ),
        name="merge_blocks",
    )(
        old_owner[:, 0],
        old_slot,
        neighbors.T,
        norm_scale[None, :],
        norm_shift[None, :],
        features,
        previous,
        occupancy,
        conv_weight,
        prev_weight,
    )


def merge(*arrays):
    merged, over = per_device(*arrays)
    return lax.cond(over[0] > 0, lambda: merge_full(*arrays), lambda: merged)


def solution(mesh):
    in_specs = (
        P(("grp", "blk"), None, None),
        P(("grp", "blk"), None),
        P(("grp", "blk"), None),
        P(("grp", "blk"), None, None),
        P(("grp", "blk"), None),
        P(("grp", "blk")),
        P(),
        P(),
        P(),
        P(),
    )
    out_specs = P(("grp", "blk"), None, None)
    return jax.shard_map(
        merge, mesh=mesh, in_specs=in_specs, out_specs=out_specs, check_vma=False
    )
```

```python
import functools

import jax
import jax.numpy as jnp
from jax import lax
from jax.experimental import pallas as pl
from jax.experimental.pallas import tpu as pltpu
from jax.sharding import PartitionSpec as P

EDGE = 4
FACE = EDGE * EDGE
VOX = EDGE * FACE
CAP = 2
LANES = 128
EXTRA = 2
PACK = 1 << 16
MESH = pl.DeviceIdType.MESH
F32 = jnp.float32
BF16 = jnp.bfloat16


def iota(shape, dim):
    return lax.broadcasted_iota(jnp.int32, shape, dim)


def one_hot(hit):
    return jnp.where(hit, 1.0, 0.0).astype(BF16)


def kernel_full(
    count,
    slots,
    channels,
    owner_hbm,
    slot_hbm,
    nb_hbm,
    scale_hbm,
    shift_hbm,
    feat_hbm,
    prev_hbm,
    occ_hbm,
    w_hbm,
    pw_hbm,
    out_ref,
    owner_s,
    slot_s,
    nb_ref,
    occ_ref,
    scale_ref,
    shift_ref,
    feat,
    prev,
    weight,
    pweight,
    proj,
    table,
    reqs,
    reqs_s,
    sendbuf,
    recv,
    low_layer,
    high_layer,
    low_occ,
    high_occ,
    volume,
    acc,
    mask,
    base,
    small_sem,
    local_sem,
    halo_send,
    halo_recv,
    rq_send,
    rq_recv,
    rp_send,
    rp_recv,
):
    me = lax.axis_index("blk")
    layer_rows = FACE * slots
    barrier = pltpu.get_barrier_semaphore()

    @pl.loop(1, count)
    def _(i):
        peer = lax.rem(me + i, count)
        pl.semaphore_signal(barrier, inc=1, device_id={"blk": peer}, device_id_type=MESH)

    small = [
        pltpu.make_async_copy(owner_hbm, owner_s, small_sem.at[0]),
        pltpu.make_async_copy(slot_hbm, slot_s, small_sem.at[1]),
        pltpu.make_async_copy(occ_hbm, occ_ref, small_sem.at[2]),
        pltpu.make_async_copy(nb_hbm, nb_ref, small_sem.at[3]),
        pltpu.make_async_copy(scale_hbm, scale_ref, small_sem.at[4]),
        pltpu.make_async_copy(shift_hbm, shift_ref, small_sem.at[5]),
    ]
    for load in small:
        load.start()
    loads = [
        pltpu.make_async_copy(prev_hbm, prev, local_sem.at[0]),
        pltpu.make_async_copy(pw_hbm, pweight, local_sem.at[1]),
        pltpu.make_async_copy(feat_hbm, feat, local_sem.at[2]),
        pltpu.make_async_copy(w_hbm, weight, local_sem.at[3]),
    ]
    for load in loads:
        load.start()

    small[0].wait()
    small[1].wait()

    lane = iota((1, LANES), 1)
    first = jnp.zeros((1, LANES), jnp.int32)
    last = jnp.zeros((1, LANES), jnp.int32)
    for s in range(slots):
        last = jnp.where(lane == owner_s[s], slot_s[s], last)
        t = slots - 1 - s
        first = jnp.where(lane == owner_s[t], slot_s[t], first)
    row = iota((CAP, LANES), 0)
    table[...] = jnp.where(row == 0, first, last)

    def layer_occ(occ, x):
        spread = one_hot(iota((VOX, layer_rows), 0) == x * FACE + iota((VOX, layer_rows), 1) % FACE)
        rows = jnp.dot(occ, spread, preferred_element_type=F32)
        own = iota((slots, layer_rows), 0) == iota((slots, layer_rows), 1) // FACE
        return jnp.sum(jnp.where(own, rows, 0.0), axis=0, keepdims=True).astype(BF16)

    pl.semaphore_wait(barrier, count - 1)

    def request(i):
        return pltpu.make_async_remote_copy(
            src_ref=table,
            dst_ref=reqs.at[me],
            send_sem=rq_send.at[i],
            recv_sem=rq_recv.at[i],
            device_id={"blk": lax.rem(me + i, count)},
            device_id_type=MESH,
        )

    @pl.loop(1, count)
    def _(i):
        request(i).start()

    up = lax.rem(me + 1, count)
    down = lax.rem(me + count - 1, count)

    def halo(k):
        if k < 2:
            src = feat_hbm.at[:, pl.ds((EDGE - 1) * FACE, FACE), :] if k == 0 else occ_hbm
            dst = low_layer if k == 0 else low_occ
            peer = up
        else:
            src = feat_hbm.at[:, pl.ds(0, FACE), :] if k == 2 else occ_hbm
            dst = high_layer if k == 2 else high_occ
            peer = down
        return pltpu.make_async_remote_copy(
            src_ref=src,
            dst_ref=dst,
            send_sem=halo_send.at[k],
            recv_sem=halo_recv.at[k],
            device_id={"blk": peer},
            device_id_type=MESH,
        )

    @pl.when(me < count - 1)
    def _():
        halo(0).start()
        halo(1).start()

    @pl.when(me > 0)
    def _():
        halo(2).start()
        halo(3).start()

    @pl.when(me == 0)
    def _():
        low_layer[...] = jnp.zeros_like(low_layer)
        low_occ[...] = jnp.zeros_like(low_occ)

    @pl.when(me == count - 1)
    def _():
        high_layer[...] = jnp.zeros_like(high_layer)
        high_occ[...] = jnp.zeros_like(high_occ)

    loads[0].wait()
    loads[1].wait()

    blocks = layer_rows // VOX
    for s in range(0, slots, blocks):
        rows = prev[s : s + blocks].reshape(layer_rows, channels)
        part = jnp.dot(rows, pweight[...], preferred_element_type=F32).astype(BF16)
        proj[s : s + blocks] = part.reshape(blocks, VOX, channels)

    reqs_s_copy = pltpu.make_async_copy(reqs, reqs_s, local_sem.at[4])

    def reply(i):
        return pltpu.make_async_remote_copy(
            src_ref=sendbuf.at[i],
            dst_ref=recv.at[me],
            send_sem=rp_send.at[i],
            recv_sem=rp_recv.at[i],
            device_id={"blk": lax.rem(me + i, count)},
            device_id_type=MESH,
        )

    reqs[me] = table[...]

    @pl.loop(1, count)
    def _(i):
        request(i).wait_recv()

    reqs_s_copy.start()
    reqs_s_copy.wait()

    def far_first(k):
        step = (k + 1) // 2
        return count // 2 + step * (2 * (k % 2) - 1)

    @pl.loop(0, count - 1)
    def _(k):
        i = far_first(k)
        peer = lax.rem(me + i, count)
        sendbuf[i, 0] = proj[reqs_s[peer, 0, me]]
        sendbuf[i, 1] = proj[reqs_s[peer, 1, me]]

    @pl.loop(0, count - 1)
    def _(k):
        reply(far_first(k)).start()

    recv[me, 0] = proj[reqs_s[me, 0, me]]
    recv[me, 1] = proj[reqs_s[me, 1, me]]

    for load in small[2:]:
        load.wait()
    occ = occ_ref[...].astype(BF16)
    volume[...] = jnp.zeros_like(volume)
    loads[2].wait()
    col = iota((layer_rows, layer_rows), 1)
    line = iota((layer_rows, layer_rows), 0)
    select_own = one_hot(col == (line % slots) * FACE + line // slots)
    spread = one_hot(iota((layer_rows, slots), 0) % slots == iota((layer_rows, slots), 1))
    nb = lax.dot_general(
        spread,
        nb_ref[...].astype(F32).astype(BF16),
        (((1,), (1,)), ((), ())),
        preferred_element_type=F32,
    ).astype(jnp.int32)
    side_rows = EDGE * slots
    scol = iota((side_rows, layer_rows), 1)
    sline = iota((side_rows, 1), 0) // slots

    def side(f, fixed, step):
        wanted = nb[:side_rows, f : f + 1]
        target = jnp.where(wanted >= 0, wanted * FACE + fixed + sline * step, -1)
        return one_hot(scol == target)

    sides = [
        side(2, (EDGE - 1) * EDGE, 1),
        side(3, 0, 1),
        side(4, EDGE - 1, EDGE),
        side(5, 0, EDGE),
    ]
    select = jnp.concatenate([select_own] + sides, axis=0)
    for x in range(EDGE):
        layer = feat[:, x * FACE : (x + 1) * FACE, :].reshape(layer_rows, channels)
        part = jnp.dot(select * layer_occ(occ, x), layer, preferred_element_type=F32).astype(BF16)
        volume[x + 1, 1 : EDGE + 1, 1 : EDGE + 1] = part[:layer_rows].reshape(
            EDGE, EDGE, slots, channels
        )
        faces = part[layer_rows:].reshape(4, EDGE, slots, channels)
        volume[x + 1, 0, 1 : EDGE + 1] = faces[0]
        volume[x + 1, EDGE + 1, 1 : EDGE + 1] = faces[1]
        volume[x + 1, 1 : EDGE + 1, 0] = faces[2]
        volume[x + 1, 1 : EDGE + 1, EDGE + 1] = faces[3]

    @pl.when(me > 0)
    def _():
        pltpu.make_async_remote_copy(
            src_ref=feat_hbm.at[:, pl.ds(0, FACE), :],
            dst_ref=low_layer,
            send_sem=halo_send.at[0],
            recv_sem=halo_recv.at[0],
            device_id={"blk": up},
            device_id_type=MESH,
        ).wait_recv()
        halo(1).wait_recv()

    @pl.when(me < count - 1)
    def _():
        halo(2).wait_recv()
        halo(3).wait_recv()

    def x_face(f, layer_ref, other_occ, x):
        wanted = nb[:, f : f + 1]
        target = jnp.where(wanted >= 0, wanted * FACE + iota((layer_rows, 1), 0) // slots, -1)
        pick = one_hot(col == target) * layer_occ(other_occ[...].astype(BF16), x)
        layer = layer_ref[...].reshape(layer_rows, channels)
        part = jnp.dot(pick, layer, preferred_element_type=F32).astype(BF16)
        return part.reshape(EDGE, EDGE, slots, channels)

    volume[0, 1 : EDGE + 1, 1 : EDGE + 1] = x_face(0, low_layer, low_occ, EDGE - 1)
    volume[EDGE + 1, 1 : EDGE + 1, 1 : EDGE + 1] = x_face(1, high_layer, high_occ, 0)

    loads[3].wait()
    scale = scale_ref[...]
    shift = shift_ref[...]

    @pl.loop(0, EDGE)
    def _(x):
        total = jnp.zeros((layer_rows, channels), F32)
        for tap in range(27):
            a, b, c = tap // 9, (tap // 3) % 3, tap % 3
            window = volume[x + a, b : b + EDGE, c : c + EDGE].reshape(layer_rows, channels)
            total = total + jnp.dot(window, weight[tap], preferred_element_type=F32)
        hidden = jnp.maximum(total * scale + shift, 0.0)
        for k in range(channels // LANES):
            acc[k, pl.ds(x * layer_rows, layer_rows), :] = hidden[:, k * LANES : (k + 1) * LANES]

    @pl.loop(0, slots)
    def _(s):
        mine = jnp.where(iota((VOX, VOX), 0) == iota((VOX, VOX), 1), occ_ref[pl.ds(s, 1), :], 0)
        mask[pl.ds(s * VOX, VOX), :] = jnp.dot(
            mine.astype(BF16), jnp.ones((VOX, channels), BF16), preferred_element_type=F32
        )

    picks = []
    for s in range(slots):
        rank = jnp.int32(0)
        for t in range(s):
            rank = jnp.where(owner_s[t] == owner_s[s], 1, rank)
        picks.append(rank)
        hidden = jnp.concatenate(
            [acc[k, pl.ds(s, VOX, stride=slots), :] for k in range(channels // LANES)],
            axis=1,
        )
        base[s] = hidden * mask[s * VOX : (s + 1) * VOX, :]

    @pl.loop(1, count)
    def _(i):
        reply(i).wait_recv()

    for s in range(slots):
        moved = recv[owner_s[s], picks[s]].astype(F32)
        out_ref[s] = (base[s] + moved * mask[s * VOX : (s + 1) * VOX, :]).astype(BF16)

    @pl.loop(1, count)
    def _(i):
        request(i).wait_send()
        reply(i).wait_send()

    @pl.when(me < count - 1)
    def _():
        halo(0).wait_send()
        halo(1).wait_send()

    @pl.when(me > 0)
    def _():
        halo(2).wait_send()
        halo(3).wait_send()


def merge_full(
    features,
    occupancy,
    neighbors,
    previous,
    old_owner,
    old_slot,
    conv_weight,
    norm_scale,
    norm_shift,
    prev_weight,
):
    slots, vox, channels = features.shape
    count = lax.axis_size("blk")
    hbm = pl.BlockSpec(memory_space=pl.ANY)
    volume_shape = (EDGE + 2, EDGE + 2, EDGE + 2, slots, channels)
    dma = pltpu.SemaphoreType.DMA
    return pl.pallas_call(
        functools.partial(kernel_full, count, slots, channels),
        out_shape=pltpu.VMEM(features.shape, BF16),
        in_specs=[hbm] * 10,
        out_specs=pl.BlockSpec(memory_space=pltpu.VMEM),
        scratch_shapes=[
            pltpu.SMEM((slots,), jnp.int32),
            pltpu.SMEM((slots,), jnp.int32),
            pltpu.VMEM((6, slots), jnp.int32),
            pltpu.VMEM((slots, vox), jnp.int32),
            pltpu.VMEM((1, channels), F32),
            pltpu.VMEM((1, channels), F32),
            pltpu.VMEM(features.shape, BF16),
            pltpu.VMEM(previous.shape, BF16),
            pltpu.VMEM(conv_weight.shape, BF16),
            pltpu.VMEM(prev_weight.shape, BF16),
            pltpu.VMEM(previous.shape, BF16),
            pltpu.VMEM((CAP, LANES), jnp.int32),
            pltpu.VMEM((count, CAP, LANES), jnp.int32),
            pltpu.SMEM((count, CAP, LANES), jnp.int32),
            pltpu.VMEM((count, CAP, vox, channels), BF16),
            pltpu.VMEM((count, CAP, vox, channels), BF16),
            pltpu.VMEM((slots, FACE, channels), BF16),
            pltpu.VMEM((slots, FACE, channels), BF16),
            pltpu.VMEM((slots, vox), jnp.int32),
            pltpu.VMEM((slots, vox), jnp.int32),
            pltpu.VMEM(volume_shape, BF16),
            pltpu.VMEM((channels // LANES, slots * vox, LANES), F32),
            pltpu.VMEM((slots * vox, channels), F32),
            pltpu.VMEM(features.shape, F32),
            dma((6,)),
            dma((6,)),
            dma((4,)),
            dma((4,)),
            dma((count,)),
            dma((count,)),
            dma((count,)),
            dma((count,)),
        ],
        compiler_params=pltpu.CompilerParams(
            collective_id=1, has_side_effects=True, vmem_limit_bytes=66_000_000
        ),
        name="merge_full",
    )(
        old_owner[:, 0],
        old_slot,
        neighbors.T,
        norm_scale[None, :],
        norm_shift[None, :],
        features,
        previous,
        occupancy,
        conv_weight,
        prev_weight,
    )


def kernel(
    count,
    groups,
    slots,
    channels,
    owner_hbm,
    slot_hbm,
    nb_hbm,
    scale_hbm,
    shift_hbm,
    feat_hbm,
    prev_hbm,
    occ_hbm,
    w_hbm,
    pw_hbm,
    out_ref,
    over_ref,
    owner_s,
    slot_s,
    nb_ref,
    occ_ref,
    scale_ref,
    shift_ref,
    feat,
    prev,
    weight,
    pweight,
    proj,
    table,
    reqs,
    first_s,
    last_s,
    place_s,
    over,
    overs,
    send_first,
    send_row,
    send_z,
    send_x,
    relay_z,
    relay_x,
    relay_out,
    recv,
    low_layer,
    high_layer,
    low_occ,
    high_occ,
    volume,
    acc,
    mask,
    base,
    small_sem,
    local_sem,
    halo_send,
    halo_recv,
    rq_send,
    rq_recv,
    first_send,
    first_recv,
    row_send,
    row_recv,
    z_send,
    z_recv,
    x_send,
    x_recv,
    out_send,
    out_recv,
    over_send,
    over_recv,
):
    me = lax.axis_index("blk")
    grp = lax.axis_index("grp")
    half, row = count // 2, count // 4
    half_base = me // half * half
    row_base = me // row * row
    half_at, row_at = me - half_base, me - row_base
    other_half = half - half_base
    other_row = 2 * half_base + row - row_base
    across = lax.rem(me + half, count)
    beside = other_row + row_at
    row_part, z_part, x_part = count, count + row, count + row + EXTRA
    layer_rows = FACE * slots
    barrier = pltpu.get_barrier_semaphore()

    @pl.loop(1, count)
    def _(i):
        peer = lax.rem(me + i, count)
        pl.semaphore_signal(barrier, inc=1, device_id={"blk": peer}, device_id_type=MESH)

    for i in range(1, groups):
        there = lax.rem(grp + i, groups)
        pl.semaphore_signal(barrier, inc=1, device_id={"grp": there}, device_id_type=MESH)

    small = [
        pltpu.make_async_copy(owner_hbm, owner_s, small_sem.at[0]),
        pltpu.make_async_copy(slot_hbm, slot_s, small_sem.at[1]),
        pltpu.make_async_copy(occ_hbm, occ_ref, small_sem.at[2]),
        pltpu.make_async_copy(nb_hbm, nb_ref, small_sem.at[3]),
        pltpu.make_async_copy(scale_hbm, scale_ref, small_sem.at[4]),
        pltpu.make_async_copy(shift_hbm, shift_ref, small_sem.at[5]),
    ]
    for load in small:
        load.start()
    loads = [
        pltpu.make_async_copy(prev_hbm, prev, local_sem.at[0]),
        pltpu.make_async_copy(pw_hbm, pweight, local_sem.at[1]),
        pltpu.make_async_copy(feat_hbm, feat, local_sem.at[2]),
        pltpu.make_async_copy(w_hbm, weight, local_sem.at[3]),
    ]
    for load in loads:
        load.start()

    small[0].wait()
    small[1].wait()

    lane = iota((1, LANES), 1)
    first = jnp.zeros((1, LANES), jnp.int32)
    last = jnp.zeros((1, LANES), jnp.int32)
    for s in range(slots):
        last = jnp.where(lane == owner_s[s], slot_s[s], last)
        t = slots - 1 - s
        first = jnp.where(lane == owner_s[t], slot_s[t], first)
    zero = jnp.int32(0)
    x_count, z_count = zero, zero
    x_owner, z_owner = [zero] * EXTRA, [zero] * EXTRA
    for s in range(slots):
        owner = owner_s[s]
        again = zero
        for t in range(s):
            again = jnp.where(owner_s[t] == owner, 1, again)
        far = jnp.where((owner < half_base) | (owner >= half_base + half), again, 0)
        near = jnp.where((owner >= other_row) & (owner < other_row + row), again, 0)
        for e in range(EXTRA):
            x_owner[e] = jnp.where((far == 1) & (x_count == e), owner - other_half, x_owner[e])
            z_owner[e] = jnp.where((near == 1) & (z_count == e), owner - other_row, z_owner[e])
        at = jnp.where(again == 1, row_part + owner - row_base, owner)
        at = jnp.where(near == 1, z_part + jnp.minimum(z_count, EXTRA - 1), at)
        place_s[s] = jnp.where(far == 1, x_part + jnp.minimum(x_count, EXTRA - 1), at)
        x_count = x_count + far
        z_count = z_count + near
    notes = jnp.where(
        lane == count + 2 * EXTRA, jnp.where((x_count > EXTRA) | (z_count > EXTRA), 1, 0), first + last * PACK
    )
    for e in range(EXTRA):
        notes = jnp.where(lane == count + e, x_owner[e], notes)
        notes = jnp.where(lane == count + EXTRA + e, z_owner[e], notes)
    table[...] = notes

    def layer_occ(occ, x):
        spread = one_hot(iota((VOX, layer_rows), 0) == x * FACE + iota((VOX, layer_rows), 1) % FACE)
        rows = jnp.dot(occ, spread, preferred_element_type=F32)
        own = iota((slots, layer_rows), 0) == iota((slots, layer_rows), 1) // FACE
        return jnp.sum(jnp.where(own, rows, 0.0), axis=0, keepdims=True).astype(BF16)

    pl.semaphore_wait(barrier, count + groups - 2)

    def request(i):
        return pltpu.make_async_remote_copy(
            src_ref=table,
            dst_ref=reqs.at[me],
            send_sem=rq_send.at[i],
            recv_sem=rq_recv.at[i],
            device_id={"blk": lax.rem(me + i, count)},
            device_id_type=MESH,
        )

    @pl.loop(1, count)
    def _(i):
        request(i).start()

    up = lax.rem(me + 1, count)
    down = lax.rem(me + count - 1, count)

    def halo(k):
        if k < 2:
            src = feat_hbm.at[:, pl.ds((EDGE - 1) * FACE, FACE), :] if k == 0 else occ_hbm
            dst = low_layer if k == 0 else low_occ
            peer = up
        else:
            src = feat_hbm.at[:, pl.ds(0, FACE), :] if k == 2 else occ_hbm
            dst = high_layer if k == 2 else high_occ
            peer = down
        return pltpu.make_async_remote_copy(
            src_ref=src,
            dst_ref=dst,
            send_sem=halo_send.at[k],
            recv_sem=halo_recv.at[k],
            device_id={"blk": peer},
            device_id_type=MESH,
        )

    @pl.when(me < count - 1)
    def _():
        halo(0).start()
        halo(1).start()

    @pl.when(me > 0)
    def _():
        halo(2).start()
        halo(3).start()

    @pl.when(me == 0)
    def _():
        low_layer[...] = jnp.zeros_like(low_layer)
        low_occ[...] = jnp.zeros_like(low_occ)

    @pl.when(me == count - 1)
    def _():
        high_layer[...] = jnp.zeros_like(high_layer)
        high_occ[...] = jnp.zeros_like(high_occ)

    loads[0].wait()
    loads[1].wait()

    blocks = layer_rows // VOX
    for s in range(0, slots, blocks):
        rows = prev[s : s + blocks].reshape(layer_rows, channels)
        part = jnp.dot(rows, pweight[...], preferred_element_type=F32).astype(BF16)
        proj[s : s + blocks] = part.reshape(blocks, VOX, channels)

    reqs[me] = table[...]

    def in_half(i):
        return half_base + lax.rem(half_at + i, half)

    def in_row(i):
        return row_base + lax.rem(row_at + i, row)

    def first_to(i):
        return pltpu.make_async_remote_copy(
            src_ref=send_first.at[i],
            dst_ref=recv.at[me],
            send_sem=first_send.at[i],
            recv_sem=first_recv.at[i],
            device_id={"blk": lax.rem(me + i, count)},
            device_id_type=MESH,
        )

    def row_to(i):
        return pltpu.make_async_remote_copy(
            src_ref=send_row.at[i],
            dst_ref=recv.at[row_part + row_at],
            send_sem=row_send.at[i],
            recv_sem=row_recv.at[i],
            device_id={"blk": in_row(i)},
            device_id_type=MESH,
        )

    def z_to(i):
        return pltpu.make_async_remote_copy(
            src_ref=send_z.at[i],
            dst_ref=relay_z.at[row_at],
            send_sem=z_send.at[i],
            recv_sem=z_recv.at[i],
            device_id={"blk": in_row(i)},
            device_id_type=MESH,
        )

    def x_to(i):
        return pltpu.make_async_remote_copy(
            src_ref=send_x.at[i],
            dst_ref=relay_x.at[half_at],
            send_sem=x_send.at[i],
            recv_sem=x_recv.at[i],
            device_id={"blk": in_half(i)},
            device_id_type=MESH,
        )

    def relay(k):
        part, peer = ((x_part, across), (z_part, beside))[k]
        return pltpu.make_async_remote_copy(
            src_ref=relay_out.at[pl.ds(k * EXTRA, EXTRA)],
            dst_ref=recv.at[pl.ds(part, EXTRA)],
            send_sem=out_send.at[k],
            recv_sem=out_recv.at[k],
            device_id={"blk": peer},
            device_id_type=MESH,
        )

    def over_to(i):
        return pltpu.make_async_remote_copy(
            src_ref=over,
            dst_ref=overs.at[grp],
            send_sem=over_send.at[i],
            recv_sem=over_recv.at[i],
            device_id={"grp": lax.rem(grp + i, groups)},
            device_id_type=MESH,
        )

    @pl.loop(1, count)
    def _(i):
        request(i).wait_recv()

    def entry(peer, at):
        return jnp.sum(jnp.where(lane == at, reqs[peer], 0))

    for d in range(count):
        wanted = entry(d, me)
        first_s[d] = wanted % PACK
        last_s[d] = wanted // PACK

    @pl.loop(1, half)
    def _(i):
        send_x[i] = proj[last_s[lax.rem(in_half(i) + half, count)]]
        x_to(i).start()

    @pl.loop(1, row)
    def _(i):
        send_z[i] = proj[last_s[other_row + lax.rem(row_at + i, row)]]
        z_to(i).start()

    def far_first(k):
        step = (k + 1) // 2
        return count // 2 + step * (2 * (k % 2) - 1)

    @pl.loop(0, count - 1)
    def _(k):
        i = far_first(k)
        send_first[i] = proj[first_s[lax.rem(me + i, count)]]
        first_to(i).start()

    @pl.loop(1, row)
    def _(i):
        send_row[i] = proj[last_s[in_row(i)]]
        row_to(i).start()

    recv[me] = proj[first_s[me]]
    recv[row_part + row_at] = proj[last_s[me]]
    relay_x[half_at] = proj[last_s[across]]
    relay_z[row_at] = proj[last_s[beside]]

    over[...] = jnp.sum(jnp.where(lane == count + 2 * EXTRA, reqs[...].reshape(count, LANES), 0), axis=0, keepdims=True)
    for i in range(1, groups):
        over_to(i).start()

    for load in small[2:]:
        load.wait()
    occ = occ_ref[...].astype(BF16)
    volume[...] = jnp.zeros_like(volume)
    loads[2].wait()
    col = iota((layer_rows, layer_rows), 1)
    line = iota((layer_rows, layer_rows), 0)
    select_own = one_hot(col == (line % slots) * FACE + line // slots)
    spread = one_hot(iota((layer_rows, slots), 0) % slots == iota((layer_rows, slots), 1))
    nb = lax.dot_general(
        spread,
        nb_ref[...].astype(F32).astype(BF16),
        (((1,), (1,)), ((), ())),
        preferred_element_type=F32,
    ).astype(jnp.int32)
    side_rows = EDGE * slots
    scol = iota((side_rows, layer_rows), 1)
    sline = iota((side_rows, 1), 0) // slots

    def side(f, fixed, step):
        wanted = nb[:side_rows, f : f + 1]
        target = jnp.where(wanted >= 0, wanted * FACE + fixed + sline * step, -1)
        return one_hot(scol == target)

    sides = [
        side(2, (EDGE - 1) * EDGE, 1),
        side(3, 0, 1),
        side(4, EDGE - 1, EDGE),
        side(5, 0, EDGE),
    ]
    select = jnp.concatenate([select_own] + sides, axis=0)
    for x in range(EDGE):
        layer = feat[:, x * FACE : (x + 1) * FACE, :].reshape(layer_rows, channels)
        part = jnp.dot(select * layer_occ(occ, x), layer, preferred_element_type=F32).astype(BF16)
        volume[x + 1, 1 : EDGE + 1, 1 : EDGE + 1] = part[:layer_rows].reshape(
            EDGE, EDGE, slots, channels
        )
        faces = part[layer_rows:].reshape(4, EDGE, slots, channels)
        volume[x + 1, 0, 1 : EDGE + 1] = faces[0]
        volume[x + 1, EDGE + 1, 1 : EDGE + 1] = faces[1]
        volume[x + 1, 1 : EDGE + 1, 0] = faces[2]
        volume[x + 1, 1 : EDGE + 1, EDGE + 1] = faces[3]

    @pl.when(me > 0)
    def _():
        pltpu.make_async_remote_copy(
            src_ref=feat_hbm.at[:, pl.ds(0, FACE), :],
            dst_ref=low_layer,
            send_sem=halo_send.at[0],
            recv_sem=halo_recv.at[0],
            device_id={"blk": up},
            device_id_type=MESH,
        ).wait_recv()
        halo(1).wait_recv()

    @pl.when(me < count - 1)
    def _():
        halo(2).wait_recv()
        halo(3).wait_recv()

    def x_face(f, layer_ref, other_occ, x):
        wanted = nb[:, f : f + 1]
        target = jnp.where(wanted >= 0, wanted * FACE + iota((layer_rows, 1), 0) // slots, -1)
        pick = one_hot(col == target) * layer_occ(other_occ[...].astype(BF16), x)
        layer = layer_ref[...].reshape(layer_rows, channels)
        part = jnp.dot(pick, layer, preferred_element_type=F32).astype(BF16)
        return part.reshape(EDGE, EDGE, slots, channels)

    volume[0, 1 : EDGE + 1, 1 : EDGE + 1] = x_face(0, low_layer, low_occ, EDGE - 1)
    volume[EDGE + 1, 1 : EDGE + 1, 1 : EDGE + 1] = x_face(1, high_layer, high_occ, 0)

    @pl.loop(1, half)
    def _(i):
        x_to(i).wait_recv()

    @pl.loop(1, row)
    def _(i):
        z_to(i).wait_recv()

    for e in range(EXTRA):
        relay_out[e] = relay_x[entry(across, count + e)]
        relay_out[EXTRA + e] = relay_z[entry(beside, count + EXTRA + e)]
    relay(0).start()
    relay(1).start()

    loads[3].wait()
    scale = scale_ref[...]
    shift = shift_ref[...]

    @pl.loop(0, EDGE)
    def _(x):
        total = jnp.zeros((layer_rows, channels), F32)
        for tap in range(27):
            a, b, c = tap // 9, (tap // 3) % 3, tap % 3
            window = volume[x + a, b : b + EDGE, c : c + EDGE].reshape(layer_rows, channels)
            total = total + jnp.dot(window, weight[tap], preferred_element_type=F32)
        hidden = jnp.maximum(total * scale + shift, 0.0)
        for k in range(channels // LANES):
            acc[k, pl.ds(x * layer_rows, layer_rows), :] = hidden[:, k * LANES : (k + 1) * LANES]

    @pl.loop(0, slots)
    def _(s):
        mine = jnp.where(iota((VOX, VOX), 0) == iota((VOX, VOX), 1), occ_ref[pl.ds(s, 1), :], 0)
        mask[pl.ds(s * VOX, VOX), :] = jnp.dot(
            mine.astype(BF16), jnp.ones((VOX, channels), BF16), preferred_element_type=F32
        )

    for s in range(slots):
        hidden = jnp.concatenate(
            [acc[k, pl.ds(s, VOX, stride=slots), :] for k in range(channels // LANES)],
            axis=1,
        )
        base[s] = hidden * mask[s * VOX : (s + 1) * VOX, :]

    overs[grp] = over[...]
    for i in range(1, groups):
        over_to(i).wait_recv()
    over_ref[0] = jnp.sum(overs[...])

    @pl.loop(1, count)
    def _(i):
        first_to(i).wait_recv()

    @pl.loop(1, row)
    def _(i):
        row_to(i).wait_recv()

    relay(0).wait_recv()
    relay(1).wait_recv()

    for s in range(slots):
        moved = recv[place_s[s]].astype(F32)
        out_ref[s] = (base[s] + moved * mask[s * VOX : (s + 1) * VOX, :]).astype(BF16)

    @pl.loop(1, count)
    def _(i):
        request(i).wait_send()
        first_to(i).wait_send()

    @pl.loop(1, half)
    def _(i):
        x_to(i).wait_send()

    @pl.loop(1, row)
    def _(i):
        row_to(i).wait_send()
        z_to(i).wait_send()

    relay(0).wait_send()
    relay(1).wait_send()
    for i in range(1, groups):
        over_to(i).wait_send()

    @pl.when(me < count - 1)
    def _():
        halo(0).wait_send()
        halo(1).wait_send()

    @pl.when(me > 0)
    def _():
        halo(2).wait_send()
        halo(3).wait_send()


def per_device(
    features,
    occupancy,
    neighbors,
    previous,
    old_owner,
    old_slot,
    conv_weight,
    norm_scale,
    norm_shift,
    prev_weight,
):
    slots, vox, channels = features.shape
    count = lax.axis_size("blk")
    groups = lax.axis_size("grp")
    half, row = count // 2, count // 4
    hbm = pl.BlockSpec(memory_space=pl.ANY)
    volume_shape = (EDGE + 2, EDGE + 2, EDGE + 2, slots, channels)
    dma = pltpu.SemaphoreType.DMA
    return pl.pallas_call(
        functools.partial(kernel, count, groups, slots, channels),
        out_shape=[
            pltpu.VMEM(features.shape, BF16),
            jax.ShapeDtypeStruct((1,), jnp.int32),
        ],
        in_specs=[hbm] * 10,
        out_specs=[
            pl.BlockSpec(memory_space=pltpu.VMEM),
            pl.BlockSpec(memory_space=pltpu.SMEM),
        ],
        scratch_shapes=[
            pltpu.SMEM((slots,), jnp.int32),
            pltpu.SMEM((slots,), jnp.int32),
            pltpu.VMEM((6, slots), jnp.int32),
            pltpu.VMEM((slots, vox), jnp.int32),
            pltpu.VMEM((1, channels), F32),
            pltpu.VMEM((1, channels), F32),
            pltpu.VMEM(features.shape, BF16),
            pltpu.VMEM(previous.shape, BF16),
            pltpu.VMEM(conv_weight.shape, BF16),
            pltpu.VMEM(prev_weight.shape, BF16),
            pltpu.VMEM(previous.shape, BF16),
            pltpu.VMEM((1, LANES), jnp.int32),
            pltpu.VMEM((count, 1, LANES), jnp.int32),
            pltpu.SMEM((count,), jnp.int32),
            pltpu.SMEM((count,), jnp.int32),
            pltpu.SMEM((slots,), jnp.int32),
            pltpu.VMEM((1, LANES), jnp.int32),
            pltpu.VMEM((groups, 1, LANES), jnp.int32),
            pltpu.VMEM((count, vox, channels), BF16),
            pltpu.VMEM((row, vox, channels), BF16),
            pltpu.VMEM((row, vox, channels), BF16),
            pltpu.VMEM((half, vox, channels), BF16),
            pltpu.VMEM((row, vox, channels), BF16),
            pltpu.VMEM((half, vox, channels), BF16),
            pltpu.VMEM((2 * EXTRA, vox, channels), BF16),
            pltpu.VMEM((count + row + 2 * EXTRA, vox, channels), BF16),
            pltpu.VMEM((slots, FACE, channels), BF16),
            pltpu.VMEM((slots, FACE, channels), BF16),
            pltpu.VMEM((slots, vox), jnp.int32),
            pltpu.VMEM((slots, vox), jnp.int32),
            pltpu.VMEM(volume_shape, BF16),
            pltpu.VMEM((channels // LANES, slots * vox, LANES), F32),
            pltpu.VMEM((slots * vox, channels), F32),
            pltpu.VMEM(features.shape, F32),
            dma((6,)),
            dma((6,)),
            dma((4,)),
            dma((4,)),
            dma((count,)),
            dma((count,)),
            dma((count,)),
            dma((count,)),
            dma((row,)),
            dma((row,)),
            dma((row,)),
            dma((row,)),
            dma((half,)),
            dma((half,)),
            dma((2,)),
            dma((2,)),
            dma((groups,)),
            dma((groups,)),
        ],
        compiler_params=pltpu.CompilerParams(
            collective_id=0, has_side_effects=True, vmem_limit_bytes=66_000_000
        ),
        name="merge_blocks",
    )(
        old_owner[:, 0],
        old_slot,
        neighbors.T,
        norm_scale[None, :],
        norm_shift[None, :],
        features,
        previous,
        occupancy,
        conv_weight,
        prev_weight,
    )


def merge(*arrays):
    merged, over = per_device(*arrays)
    return lax.cond(over[0] > 0, lambda: merge_full(*arrays), lambda: merged)


def solution(mesh):
    in_specs = (
        P(("grp", "blk"), None, None),
        P(("grp", "blk"), None),
        P(("grp", "blk"), None),
        P(("grp", "blk"), None, None),
        P(("grp", "blk"), None),
        P(("grp", "blk")),
        P(),
        P(),
        P(),
        P(),
    )
    out_specs = P(("grp", "blk"), None, None)
    return jax.shard_map(
        merge, mesh=mesh, in_specs=in_specs, out_specs=out_specs, check_vma=False
    )
```

```python
import functools

import jax
import jax.numpy as jnp
from jax import lax
from jax.experimental import pallas as pl
from jax.experimental.pallas import tpu as pltpu
from jax.sharding import PartitionSpec as P

EDGE = 4
FACE = EDGE * EDGE
VOX = EDGE * FACE
CAP = 2
LANES = 128
EXTRA = 2
PACK = 1 << 16
MESH = pl.DeviceIdType.MESH
F32 = jnp.float32
BF16 = jnp.bfloat16


def iota(shape, dim):
    return lax.broadcasted_iota(jnp.int32, shape, dim)


def one_hot(hit):
    return jnp.where(hit, 1.0, 0.0).astype(BF16)


def kernel_full(
    count,
    slots,
    channels,
    owner_hbm,
    slot_hbm,
    nb_hbm,
    scale_hbm,
    shift_hbm,
    feat_hbm,
    prev_hbm,
    occ_hbm,
    w_hbm,
    pw_hbm,
    out_ref,
    owner_s,
    slot_s,
    nb_ref,
    occ_ref,
    scale_ref,
    shift_ref,
    feat,
    prev,
    weight,
    pweight,
    proj,
    table,
    reqs,
    reqs_s,
    sendbuf,
    recv,
    low_layer,
    high_layer,
    low_occ,
    high_occ,
    volume,
    acc,
    mask,
    base,
    small_sem,
    local_sem,
    halo_send,
    halo_recv,
    rq_send,
    rq_recv,
    rp_send,
    rp_recv,
):
    me = lax.axis_index("blk")
    layer_rows = FACE * slots
    barrier = pltpu.get_barrier_semaphore()

    @pl.loop(1, count)
    def _(i):
        peer = lax.rem(me + i, count)
        pl.semaphore_signal(barrier, inc=1, device_id={"blk": peer}, device_id_type=MESH)

    small = [
        pltpu.make_async_copy(owner_hbm, owner_s, small_sem.at[0]),
        pltpu.make_async_copy(slot_hbm, slot_s, small_sem.at[1]),
        pltpu.make_async_copy(occ_hbm, occ_ref, small_sem.at[2]),
        pltpu.make_async_copy(nb_hbm, nb_ref, small_sem.at[3]),
        pltpu.make_async_copy(scale_hbm, scale_ref, small_sem.at[4]),
        pltpu.make_async_copy(shift_hbm, shift_ref, small_sem.at[5]),
    ]
    for load in small:
        load.start()
    loads = [
        pltpu.make_async_copy(prev_hbm, prev, local_sem.at[0]),
        pltpu.make_async_copy(pw_hbm, pweight, local_sem.at[1]),
        pltpu.make_async_copy(feat_hbm, feat, local_sem.at[2]),
        pltpu.make_async_copy(w_hbm, weight, local_sem.at[3]),
    ]
    for load in loads:
        load.start()

    small[0].wait()
    small[1].wait()

    lane = iota((1, LANES), 1)
    first = jnp.zeros((1, LANES), jnp.int32)
    last = jnp.zeros((1, LANES), jnp.int32)
    for s in range(slots):
        last = jnp.where(lane == owner_s[s], slot_s[s], last)
        t = slots - 1 - s
        first = jnp.where(lane == owner_s[t], slot_s[t], first)
    row = iota((CAP, LANES), 0)
    table[...] = jnp.where(row == 0, first, last)

    def layer_occ(occ, x):
        spread = one_hot(iota((VOX, layer_rows), 0) == x * FACE + iota((VOX, layer_rows), 1) % FACE)
        rows = jnp.dot(occ, spread, preferred_element_type=F32)
        own = iota((slots, layer_rows), 0) == iota((slots, layer_rows), 1) // FACE
        return jnp.sum(jnp.where(own, rows, 0.0), axis=0, keepdims=True).astype(BF16)

    pl.semaphore_wait(barrier, count - 1)

    def request(i):
        return pltpu.make_async_remote_copy(
            src_ref=table,
            dst_ref=reqs.at[me],
            send_sem=rq_send.at[i],
            recv_sem=rq_recv.at[i],
            device_id={"blk": lax.rem(me + i, count)},
            device_id_type=MESH,
        )

    @pl.loop(1, count)
    def _(i):
        request(i).start()

    up = lax.rem(me + 1, count)
    down = lax.rem(me + count - 1, count)

    def halo(k):
        if k < 2:
            src = feat_hbm.at[:, pl.ds((EDGE - 1) * FACE, FACE), :] if k == 0 else occ_hbm
            dst = low_layer if k == 0 else low_occ
            peer = up
        else:
            src = feat_hbm.at[:, pl.ds(0, FACE), :] if k == 2 else occ_hbm
            dst = high_layer if k == 2 else high_occ
            peer = down
        return pltpu.make_async_remote_copy(
            src_ref=src,
            dst_ref=dst,
            send_sem=halo_send.at[k],
            recv_sem=halo_recv.at[k],
            device_id={"blk": peer},
            device_id_type=MESH,
        )

    @pl.when(me < count - 1)
    def _():
        halo(0).start()
        halo(1).start()

    @pl.when(me > 0)
    def _():
        halo(2).start()
        halo(3).start()

    @pl.when(me == 0)
    def _():
        low_layer[...] = jnp.zeros_like(low_layer)
        low_occ[...] = jnp.zeros_like(low_occ)

    @pl.when(me == count - 1)
    def _():
        high_layer[...] = jnp.zeros_like(high_layer)
        high_occ[...] = jnp.zeros_like(high_occ)

    loads[0].wait()
    loads[1].wait()

    blocks = layer_rows // VOX
    for s in range(0, slots, blocks):
        rows = prev[s : s + blocks].reshape(layer_rows, channels)
        part = jnp.dot(rows, pweight[...], preferred_element_type=F32).astype(BF16)
        proj[s : s + blocks] = part.reshape(blocks, VOX, channels)

    reqs_s_copy = pltpu.make_async_copy(reqs, reqs_s, local_sem.at[4])

    def reply(i):
        return pltpu.make_async_remote_copy(
            src_ref=sendbuf.at[i],
            dst_ref=recv.at[me],
            send_sem=rp_send.at[i],
            recv_sem=rp_recv.at[i],
            device_id={"blk": lax.rem(me + i, count)},
            device_id_type=MESH,
        )

    reqs[me] = table[...]

    @pl.loop(1, count)
    def _(i):
        request(i).wait_recv()

    reqs_s_copy.start()
    reqs_s_copy.wait()

    def far_first(k):
        step = (k + 1) // 2
        return count // 2 + step * (2 * (k % 2) - 1)

    @pl.loop(0, count - 1)
    def _(k):
        i = far_first(k)
        peer = lax.rem(me + i, count)
        sendbuf[i, 0] = proj[reqs_s[peer, 0, me]]
        sendbuf[i, 1] = proj[reqs_s[peer, 1, me]]

    @pl.loop(0, count - 1)
    def _(k):
        reply(far_first(k)).start()

    recv[me, 0] = proj[reqs_s[me, 0, me]]
    recv[me, 1] = proj[reqs_s[me, 1, me]]

    for load in small[2:]:
        load.wait()
    occ = occ_ref[...].astype(BF16)
    volume[...] = jnp.zeros_like(volume)
    loads[2].wait()
    col = iota((layer_rows, layer_rows), 1)
    line = iota((layer_rows, layer_rows), 0)
    select_own = one_hot(col == (line % slots) * FACE + line // slots)
    spread = one_hot(iota((layer_rows, slots), 0) % slots == iota((layer_rows, slots), 1))
    nb = lax.dot_general(
        spread,
        nb_ref[...].astype(F32).astype(BF16),
        (((1,), (1,)), ((), ())),
        preferred_element_type=F32,
    ).astype(jnp.int32)
    side_rows = EDGE * slots
    scol = iota((side_rows, layer_rows), 1)
    sline = iota((side_rows, 1), 0) // slots

    def side(f, fixed, step):
        wanted = nb[:side_rows, f : f + 1]
        target = jnp.where(wanted >= 0, wanted * FACE + fixed + sline * step, -1)
        return one_hot(scol == target)

    sides = [
        side(2, (EDGE - 1) * EDGE, 1),
        side(3, 0, 1),
        side(4, EDGE - 1, EDGE),
        side(5, 0, EDGE),
    ]
    select = jnp.concatenate([select_own] + sides, axis=0)
    for x in range(EDGE):
        layer = feat[:, x * FACE : (x + 1) * FACE, :].reshape(layer_rows, channels)
        part = jnp.dot(select * layer_occ(occ, x), layer, preferred_element_type=F32).astype(BF16)
        volume[x + 1, 1 : EDGE + 1, 1 : EDGE + 1] = part[:layer_rows].reshape(
            EDGE, EDGE, slots, channels
        )
        faces = part[layer_rows:].reshape(4, EDGE, slots, channels)
        volume[x + 1, 0, 1 : EDGE + 1] = faces[0]
        volume[x + 1, EDGE + 1, 1 : EDGE + 1] = faces[1]
        volume[x + 1, 1 : EDGE + 1, 0] = faces[2]
        volume[x + 1, 1 : EDGE + 1, EDGE + 1] = faces[3]

    @pl.when(me > 0)
    def _():
        pltpu.make_async_remote_copy(
            src_ref=feat_hbm.at[:, pl.ds(0, FACE), :],
            dst_ref=low_layer,
            send_sem=halo_send.at[0],
            recv_sem=halo_recv.at[0],
            device_id={"blk": up},
            device_id_type=MESH,
        ).wait_recv()
        halo(1).wait_recv()

    @pl.when(me < count - 1)
    def _():
        halo(2).wait_recv()
        halo(3).wait_recv()

    def x_face(f, layer_ref, other_occ, x):
        wanted = nb[:, f : f + 1]
        target = jnp.where(wanted >= 0, wanted * FACE + iota((layer_rows, 1), 0) // slots, -1)
        pick = one_hot(col == target) * layer_occ(other_occ[...].astype(BF16), x)
        layer = layer_ref[...].reshape(layer_rows, channels)
        part = jnp.dot(pick, layer, preferred_element_type=F32).astype(BF16)
        return part.reshape(EDGE, EDGE, slots, channels)

    volume[0, 1 : EDGE + 1, 1 : EDGE + 1] = x_face(0, low_layer, low_occ, EDGE - 1)
    volume[EDGE + 1, 1 : EDGE + 1, 1 : EDGE + 1] = x_face(1, high_layer, high_occ, 0)

    loads[3].wait()
    scale = scale_ref[...]
    shift = shift_ref[...]

    @pl.loop(0, EDGE)
    def _(x):
        total = jnp.zeros((layer_rows, channels), F32)
        for tap in range(27):
            a, b, c = tap // 9, (tap // 3) % 3, tap % 3
            window = volume[x + a, b : b + EDGE, c : c + EDGE].reshape(layer_rows, channels)
            total = total + jnp.dot(window, weight[tap], preferred_element_type=F32)
        hidden = jnp.maximum(total * scale + shift, 0.0)
        for k in range(channels // LANES):
            acc[k, pl.ds(x * layer_rows, layer_rows), :] = hidden[:, k * LANES : (k + 1) * LANES]

    @pl.loop(0, slots)
    def _(s):
        mine = jnp.where(iota((VOX, VOX), 0) == iota((VOX, VOX), 1), occ_ref[pl.ds(s, 1), :], 0)
        mask[pl.ds(s * VOX, VOX), :] = jnp.dot(
            mine.astype(BF16), jnp.ones((VOX, channels), BF16), preferred_element_type=F32
        )

    picks = []
    for s in range(slots):
        rank = jnp.int32(0)
        for t in range(s):
            rank = jnp.where(owner_s[t] == owner_s[s], 1, rank)
        picks.append(rank)
        hidden = jnp.concatenate(
            [acc[k, pl.ds(s, VOX, stride=slots), :] for k in range(channels // LANES)],
            axis=1,
        )
        base[s] = hidden * mask[s * VOX : (s + 1) * VOX, :]

    @pl.loop(1, count)
    def _(i):
        reply(i).wait_recv()

    for s in range(slots):
        moved = recv[owner_s[s], picks[s]].astype(F32)
        out_ref[s] = (base[s] + moved * mask[s * VOX : (s + 1) * VOX, :]).astype(BF16)

    @pl.loop(1, count)
    def _(i):
        request(i).wait_send()
        reply(i).wait_send()

    @pl.when(me < count - 1)
    def _():
        halo(0).wait_send()
        halo(1).wait_send()

    @pl.when(me > 0)
    def _():
        halo(2).wait_send()
        halo(3).wait_send()


def merge_full(
    features,
    occupancy,
    neighbors,
    previous,
    old_owner,
    old_slot,
    conv_weight,
    norm_scale,
    norm_shift,
    prev_weight,
):
    slots, vox, channels = features.shape
    count = lax.axis_size("blk")
    hbm = pl.BlockSpec(memory_space=pl.ANY)
    volume_shape = (EDGE + 2, EDGE + 2, EDGE + 2, slots, channels)
    dma = pltpu.SemaphoreType.DMA
    return pl.pallas_call(
        functools.partial(kernel_full, count, slots, channels),
        out_shape=pltpu.VMEM(features.shape, BF16),
        in_specs=[hbm] * 10,
        out_specs=pl.BlockSpec(memory_space=pltpu.VMEM),
        scratch_shapes=[
            pltpu.SMEM((slots,), jnp.int32),
            pltpu.SMEM((slots,), jnp.int32),
            pltpu.VMEM((6, slots), jnp.int32),
            pltpu.VMEM((slots, vox), jnp.int32),
            pltpu.VMEM((1, channels), F32),
            pltpu.VMEM((1, channels), F32),
            pltpu.VMEM(features.shape, BF16),
            pltpu.VMEM(previous.shape, BF16),
            pltpu.VMEM(conv_weight.shape, BF16),
            pltpu.VMEM(prev_weight.shape, BF16),
            pltpu.VMEM(previous.shape, BF16),
            pltpu.VMEM((CAP, LANES), jnp.int32),
            pltpu.VMEM((count, CAP, LANES), jnp.int32),
            pltpu.SMEM((count, CAP, LANES), jnp.int32),
            pltpu.VMEM((count, CAP, vox, channels), BF16),
            pltpu.VMEM((count, CAP, vox, channels), BF16),
            pltpu.VMEM((slots, FACE, channels), BF16),
            pltpu.VMEM((slots, FACE, channels), BF16),
            pltpu.VMEM((slots, vox), jnp.int32),
            pltpu.VMEM((slots, vox), jnp.int32),
            pltpu.VMEM(volume_shape, BF16),
            pltpu.VMEM((channels // LANES, slots * vox, LANES), F32),
            pltpu.VMEM((slots * vox, channels), F32),
            pltpu.VMEM(features.shape, F32),
            dma((6,)),
            dma((6,)),
            dma((4,)),
            dma((4,)),
            dma((count,)),
            dma((count,)),
            dma((count,)),
            dma((count,)),
        ],
        compiler_params=pltpu.CompilerParams(
            collective_id=1, has_side_effects=True, vmem_limit_bytes=66_000_000
        ),
        name="merge_full",
    )(
        old_owner[:, 0],
        old_slot,
        neighbors.T,
        norm_scale[None, :],
        norm_shift[None, :],
        features,
        previous,
        occupancy,
        conv_weight,
        prev_weight,
    )


def kernel(
    count,
    groups,
    slots,
    channels,
    owner_hbm,
    slot_hbm,
    nb_hbm,
    scale_hbm,
    shift_hbm,
    feat_hbm,
    prev_hbm,
    occ_hbm,
    w_hbm,
    pw_hbm,
    out_ref,
    over_ref,
    owner_s,
    slot_s,
    nb_ref,
    occ_ref,
    scale_ref,
    shift_ref,
    feat,
    prev,
    weight,
    pweight,
    proj,
    table,
    reqs,
    first_s,
    last_s,
    place_s,
    over,
    overs,
    send_first,
    send_row,
    send_z,
    send_x,
    relay_z,
    relay_x,
    relay_out,
    recv,
    low_layer,
    high_layer,
    low_occ,
    high_occ,
    volume,
    acc,
    mask,
    base,
    small_sem,
    local_sem,
    halo_send,
    halo_recv,
    rq_send,
    rq_recv,
    first_send,
    first_recv,
    row_send,
    row_recv,
    z_send,
    z_recv,
    x_send,
    x_recv,
    out_send,
    out_recv,
    over_send,
    over_recv,
):
    me = lax.axis_index("blk")
    grp = lax.axis_index("grp")
    half, row = count // 2, count // 4
    half_base = me // half * half
    row_base = me // row * row
    half_at, row_at = me - half_base, me - row_base
    other_half = half - half_base
    other_row = 2 * half_base + row - row_base
    across = lax.rem(me + half, count)
    beside = other_row + row_at
    row_part, z_part, x_part = count, count + row, count + row + EXTRA
    layer_rows = FACE * slots
    barrier = pltpu.get_barrier_semaphore()

    @pl.loop(1, count)
    def _(i):
        peer = lax.rem(me + i, count)
        pl.semaphore_signal(barrier, inc=1, device_id={"blk": peer}, device_id_type=MESH)

    for i in range(1, groups):
        there = lax.rem(grp + i, groups)
        pl.semaphore_signal(barrier, inc=1, device_id={"grp": there}, device_id_type=MESH)

    small = [
        pltpu.make_async_copy(owner_hbm, owner_s, small_sem.at[0]),
        pltpu.make_async_copy(slot_hbm, slot_s, small_sem.at[1]),
        pltpu.make_async_copy(occ_hbm, occ_ref, small_sem.at[2]),
        pltpu.make_async_copy(nb_hbm, nb_ref, small_sem.at[3]),
        pltpu.make_async_copy(scale_hbm, scale_ref, small_sem.at[4]),
        pltpu.make_async_copy(shift_hbm, shift_ref, small_sem.at[5]),
    ]
    for load in small:
        load.start()
    loads = [
        pltpu.make_async_copy(prev_hbm, prev, local_sem.at[0]),
        pltpu.make_async_copy(pw_hbm, pweight, local_sem.at[1]),
        pltpu.make_async_copy(feat_hbm, feat, local_sem.at[2]),
        pltpu.make_async_copy(w_hbm, weight, local_sem.at[3]),
    ]
    for load in loads:
        load.start()

    small[0].wait()
    small[1].wait()

    lane = iota((1, LANES), 1)
    first = jnp.zeros((1, LANES), jnp.int32)
    last = jnp.zeros((1, LANES), jnp.int32)
    for s in range(slots):
        last = jnp.where(lane == owner_s[s], slot_s[s], last)
        t = slots - 1 - s
        first = jnp.where(lane == owner_s[t], slot_s[t], first)
    zero = jnp.int32(0)
    x_count, z_count = zero, zero
    x_owner, z_owner = [zero] * EXTRA, [zero] * EXTRA
    for s in range(slots):
        owner = owner_s[s]
        again = zero
        for t in range(s):
            again = jnp.where(owner_s[t] == owner, 1, again)
        far = jnp.where((owner < half_base) | (owner >= half_base + half), again, 0)
        near = jnp.where((owner >= other_row) & (owner < other_row + row), again, 0)
        for e in range(EXTRA):
            x_owner[e] = jnp.where((far == 1) & (x_count == e), owner - other_half, x_owner[e])
            z_owner[e] = jnp.where((near == 1) & (z_count == e), owner - other_row, z_owner[e])
        at = jnp.where(again == 1, row_part + owner - row_base, owner)
        at = jnp.where(near == 1, z_part + jnp.minimum(z_count, EXTRA - 1), at)
        place_s[s] = jnp.where(far == 1, x_part + jnp.minimum(x_count, EXTRA - 1), at)
        x_count = x_count + far
        z_count = z_count + near
    notes = jnp.where(
        lane == count + 2 * EXTRA, jnp.where((x_count > EXTRA) | (z_count > EXTRA), 1, 0), first + last * PACK
    )
    for e in range(EXTRA):
        notes = jnp.where(lane == count + e, x_owner[e], notes)
        notes = jnp.where(lane == count + EXTRA + e, z_owner[e], notes)
    table[...] = notes

    def layer_occ(occ, x):
        spread = one_hot(iota((VOX, layer_rows), 0) == x * FACE + iota((VOX, layer_rows), 1) % FACE)
        rows = jnp.dot(occ, spread, preferred_element_type=F32)
        own = iota((slots, layer_rows), 0) == iota((slots, layer_rows), 1) // FACE
        return jnp.sum(jnp.where(own, rows, 0.0), axis=0, keepdims=True).astype(BF16)

    pl.semaphore_wait(barrier, count + groups - 2)

    def request(i):
        return pltpu.make_async_remote_copy(
            src_ref=table,
            dst_ref=reqs.at[me],
            send_sem=rq_send.at[i],
            recv_sem=rq_recv.at[i],
            device_id={"blk": lax.rem(me + i, count)},
            device_id_type=MESH,
        )

    @pl.loop(1, count)
    def _(i):
        request(i).start()

    up = lax.rem(me + 1, count)
    down = lax.rem(me + count - 1, count)

    def halo(k):
        if k < 2:
            src = feat_hbm.at[:, pl.ds((EDGE - 1) * FACE, FACE), :] if k == 0 else occ_hbm
            dst = low_layer if k == 0 else low_occ
            peer = up
        else:
            src = feat_hbm.at[:, pl.ds(0, FACE), :] if k == 2 else occ_hbm
            dst = high_layer if k == 2 else high_occ
            peer = down
        return pltpu.make_async_remote_copy(
            src_ref=src,
            dst_ref=dst,
            send_sem=halo_send.at[k],
            recv_sem=halo_recv.at[k],
            device_id={"blk": peer},
            device_id_type=MESH,
        )

    @pl.when(me < count - 1)
    def _():
        halo(0).start()
        halo(1).start()

    @pl.when(me > 0)
    def _():
        halo(2).start()
        halo(3).start()

    @pl.when(me == 0)
    def _():
        low_layer[...] = jnp.zeros_like(low_layer)
        low_occ[...] = jnp.zeros_like(low_occ)

    @pl.when(me == count - 1)
    def _():
        high_layer[...] = jnp.zeros_like(high_layer)
        high_occ[...] = jnp.zeros_like(high_occ)

    loads[0].wait()
    loads[1].wait()

    blocks = layer_rows // VOX
    for s in range(0, slots, blocks):
        rows = prev[s : s + blocks].reshape(layer_rows, channels)
        part = jnp.dot(rows, pweight[...], preferred_element_type=F32).astype(BF16)
        proj[s : s + blocks] = part.reshape(blocks, VOX, channels)

    reqs[me] = table[...]

    def in_half(i):
        return half_base + lax.rem(half_at + i, half)

    def in_row(i):
        return row_base + lax.rem(row_at + i, row)

    def first_to(i):
        return pltpu.make_async_remote_copy(
            src_ref=send_first.at[i],
            dst_ref=recv.at[me],
            send_sem=first_send.at[i],
            recv_sem=first_recv.at[i],
            device_id={"blk": lax.rem(me + i, count)},
            device_id_type=MESH,
        )

    def row_to(i):
        return pltpu.make_async_remote_copy(
            src_ref=send_row.at[i],
            dst_ref=recv.at[row_part + row_at],
            send_sem=row_send.at[i],
            recv_sem=row_recv.at[i],
            device_id={"blk": in_row(i)},
            device_id_type=MESH,
        )

    def z_to(i):
        return pltpu.make_async_remote_copy(
            src_ref=send_z.at[i],
            dst_ref=relay_z.at[row_at],
            send_sem=z_send.at[i],
            recv_sem=z_recv.at[i],
            device_id={"blk": in_row(i)},
            device_id_type=MESH,
        )

    def x_to(i):
        return pltpu.make_async_remote_copy(
            src_ref=send_x.at[i],
            dst_ref=relay_x.at[half_at],
            send_sem=x_send.at[i],
            recv_sem=x_recv.at[i],
            device_id={"blk": in_half(i)},
            device_id_type=MESH,
        )

    def relay(k):
        part, peer = ((x_part, across), (z_part, beside))[k]
        return pltpu.make_async_remote_copy(
            src_ref=relay_out.at[pl.ds(k * EXTRA, EXTRA)],
            dst_ref=recv.at[pl.ds(part, EXTRA)],
            send_sem=out_send.at[k],
            recv_sem=out_recv.at[k],
            device_id={"blk": peer},
            device_id_type=MESH,
        )

    def over_to(i):
        return pltpu.make_async_remote_copy(
            src_ref=over,
            dst_ref=overs.at[grp],
            send_sem=over_send.at[i],
            recv_sem=over_recv.at[i],
            device_id={"grp": lax.rem(grp + i, groups)},
            device_id_type=MESH,
        )

    @pl.loop(1, count)
    def _(i):
        request(i).wait_recv()

    def entry(peer, at):
        return jnp.sum(jnp.where(lane == at, reqs[peer], 0))

    for d in range(count):
        wanted = entry(d, me)
        first_s[d] = wanted % PACK
        last_s[d] = wanted // PACK

    @pl.loop(1, half)
    def _(i):
        send_x[i] = proj[last_s[lax.rem(in_half(i) + half, count)]]
        x_to(i).start()

    @pl.loop(1, row)
    def _(i):
        send_z[i] = proj[last_s[other_row + lax.rem(row_at + i, row)]]
        z_to(i).start()

    def far_first(k):
        step = (k + 1) // 2
        return count // 2 + step * (2 * (k % 2) - 1)

    @pl.loop(0, count - 1)
    def _(k):
        i = far_first(k)
        send_first[i] = proj[first_s[lax.rem(me + i, count)]]
        first_to(i).start()

    @pl.loop(1, row)
    def _(i):
        send_row[i] = proj[last_s[in_row(i)]]
        row_to(i).start()

    recv[me] = proj[first_s[me]]
    recv[row_part + row_at] = proj[last_s[me]]
    relay_x[half_at] = proj[last_s[across]]
    relay_z[row_at] = proj[last_s[beside]]

    over[...] = jnp.sum(jnp.where(lane == count + 2 * EXTRA, reqs[...].reshape(count, LANES), 0), axis=0, keepdims=True)
    for i in range(1, groups):
        over_to(i).start()

    for load in small[2:]:
        load.wait()
    occ = occ_ref[...].astype(BF16)
    volume[...] = jnp.zeros_like(volume)
    loads[2].wait()
    col = iota((layer_rows, layer_rows), 1)
    line = iota((layer_rows, layer_rows), 0)
    select_own = one_hot(col == (line % slots) * FACE + line // slots)
    spread = one_hot(iota((layer_rows, slots), 0) % slots == iota((layer_rows, slots), 1))
    nb = lax.dot_general(
        spread,
        nb_ref[...].astype(F32).astype(BF16),
        (((1,), (1,)), ((), ())),
        preferred_element_type=F32,
    ).astype(jnp.int32)
    side_rows = EDGE * slots
    scol = iota((side_rows, layer_rows), 1)
    sline = iota((side_rows, 1), 0) // slots

    def side(f, fixed, step):
        wanted = nb[:side_rows, f : f + 1]
        target = jnp.where(wanted >= 0, wanted * FACE + fixed + sline * step, -1)
        return one_hot(scol == target)

    sides = [
        side(2, (EDGE - 1) * EDGE, 1),
        side(3, 0, 1),
        side(4, EDGE - 1, EDGE),
        side(5, 0, EDGE),
    ]
    select = jnp.concatenate([select_own] + sides, axis=0)
    for x in range(EDGE):
        layer = feat[:, x * FACE : (x + 1) * FACE, :].reshape(layer_rows, channels)
        part = jnp.dot(select * layer_occ(occ, x), layer, preferred_element_type=F32).astype(BF16)
        volume[x + 1, 1 : EDGE + 1, 1 : EDGE + 1] = part[:layer_rows].reshape(
            EDGE, EDGE, slots, channels
        )
        faces = part[layer_rows:].reshape(4, EDGE, slots, channels)
        volume[x + 1, 0, 1 : EDGE + 1] = faces[0]
        volume[x + 1, EDGE + 1, 1 : EDGE + 1] = faces[1]
        volume[x + 1, 1 : EDGE + 1, 0] = faces[2]
        volume[x + 1, 1 : EDGE + 1, EDGE + 1] = faces[3]

    @pl.when(me > 0)
    def _():
        pltpu.make_async_remote_copy(
            src_ref=feat_hbm.at[:, pl.ds(0, FACE), :],
            dst_ref=low_layer,
            send_sem=halo_send.at[0],
            recv_sem=halo_recv.at[0],
            device_id={"blk": up},
            device_id_type=MESH,
        ).wait_recv()
        halo(1).wait_recv()

    @pl.when(me < count - 1)
    def _():
        halo(2).wait_recv()
        halo(3).wait_recv()

    def x_face(f, layer_ref, other_occ, x):
        wanted = nb[:, f : f + 1]
        target = jnp.where(wanted >= 0, wanted * FACE + iota((layer_rows, 1), 0) // slots, -1)
        pick = one_hot(col == target) * layer_occ(other_occ[...].astype(BF16), x)
        layer = layer_ref[...].reshape(layer_rows, channels)
        part = jnp.dot(pick, layer, preferred_element_type=F32).astype(BF16)
        return part.reshape(EDGE, EDGE, slots, channels)

    volume[0, 1 : EDGE + 1, 1 : EDGE + 1] = x_face(0, low_layer, low_occ, EDGE - 1)
    volume[EDGE + 1, 1 : EDGE + 1, 1 : EDGE + 1] = x_face(1, high_layer, high_occ, 0)

    @pl.loop(1, half)
    def _(i):
        x_to(i).wait_recv()

    @pl.loop(1, row)
    def _(i):
        z_to(i).wait_recv()

    for e in range(EXTRA):
        relay_out[e] = relay_x[entry(across, count + e)]
        relay_out[EXTRA + e] = relay_z[entry(beside, count + EXTRA + e)]
    relay(0).start()
    relay(1).start()

    loads[3].wait()
    scale = scale_ref[...]
    shift = shift_ref[...]

    @pl.loop(0, EDGE)
    def _(x):
        total = jnp.zeros((layer_rows, channels), F32)
        for tap in range(27):
            a, b, c = tap // 9, (tap // 3) % 3, tap % 3
            window = volume[x + a, b : b + EDGE, c : c + EDGE].reshape(layer_rows, channels)
            total = total + jnp.dot(window, weight[tap], preferred_element_type=F32)
        hidden = jnp.maximum(total * scale + shift, 0.0)
        for k in range(channels // LANES):
            acc[k, pl.ds(x * layer_rows, layer_rows), :] = hidden[:, k * LANES : (k + 1) * LANES]

    @pl.loop(0, slots)
    def _(s):
        mine = jnp.where(iota((VOX, VOX), 0) == iota((VOX, VOX), 1), occ_ref[pl.ds(s, 1), :], 0)
        mask[pl.ds(s * VOX, VOX), :] = jnp.dot(
            mine.astype(BF16), jnp.ones((VOX, channels), BF16), preferred_element_type=F32
        )

    for s in range(slots):
        hidden = jnp.concatenate(
            [acc[k, pl.ds(s, VOX, stride=slots), :] for k in range(channels // LANES)],
            axis=1,
        )
        base[s] = hidden * mask[s * VOX : (s + 1) * VOX, :]

    overs[grp] = over[...]
    for i in range(1, groups):
        over_to(i).wait_recv()
    over_ref[0] = jnp.sum(overs[...])

    @pl.loop(1, count)
    def _(i):
        request(i).wait_send()
        first_to(i).wait_send()

    @pl.loop(1, half)
    def _(i):
        x_to(i).wait_send()

    @pl.loop(1, row)
    def _(i):
        row_to(i).wait_send()
        z_to(i).wait_send()

    relay(0).wait_send()
    relay(1).wait_send()
    for i in range(1, groups):
        over_to(i).wait_send()

    @pl.when(me < count - 1)
    def _():
        halo(0).wait_send()
        halo(1).wait_send()

    @pl.when(me > 0)
    def _():
        halo(2).wait_send()
        halo(3).wait_send()

    @pl.loop(1, count)
    def _(i):
        first_to(i).wait_recv()

    @pl.loop(1, row)
    def _(i):
        row_to(i).wait_recv()

    relay(0).wait_recv()
    relay(1).wait_recv()

    for s in range(slots):
        moved = recv[place_s[s]].astype(F32)
        out_ref[s] = (base[s] + moved * mask[s * VOX : (s + 1) * VOX, :]).astype(BF16)


def per_device(
    features,
    occupancy,
    neighbors,
    previous,
    old_owner,
    old_slot,
    conv_weight,
    norm_scale,
    norm_shift,
    prev_weight,
):
    slots, vox, channels = features.shape
    count = lax.axis_size("blk")
    groups = lax.axis_size("grp")
    half, row = count // 2, count // 4
    hbm = pl.BlockSpec(memory_space=pl.ANY)
    volume_shape = (EDGE + 2, EDGE + 2, EDGE + 2, slots, channels)
    dma = pltpu.SemaphoreType.DMA
    return pl.pallas_call(
        functools.partial(kernel, count, groups, slots, channels),
        out_shape=[
            pltpu.VMEM(features.shape, BF16),
            pltpu.SMEM((1,), jnp.int32),
        ],
        in_specs=[hbm] * 10,
        out_specs=[
            pl.BlockSpec(memory_space=pltpu.VMEM),
            pl.BlockSpec(memory_space=pltpu.SMEM),
        ],
        scratch_shapes=[
            pltpu.SMEM((slots,), jnp.int32),
            pltpu.SMEM((slots,), jnp.int32),
            pltpu.VMEM((6, slots), jnp.int32),
            pltpu.VMEM((slots, vox), jnp.int32),
            pltpu.VMEM((1, channels), F32),
            pltpu.VMEM((1, channels), F32),
            pltpu.VMEM(features.shape, BF16),
            pltpu.VMEM(previous.shape, BF16),
            pltpu.VMEM(conv_weight.shape, BF16),
            pltpu.VMEM(prev_weight.shape, BF16),
            pltpu.VMEM(previous.shape, BF16),
            pltpu.VMEM((1, LANES), jnp.int32),
            pltpu.VMEM((count, 1, LANES), jnp.int32),
            pltpu.SMEM((count,), jnp.int32),
            pltpu.SMEM((count,), jnp.int32),
            pltpu.SMEM((slots,), jnp.int32),
            pltpu.VMEM((1, LANES), jnp.int32),
            pltpu.VMEM((groups, 1, LANES), jnp.int32),
            pltpu.VMEM((count, vox, channels), BF16),
            pltpu.VMEM((row, vox, channels), BF16),
            pltpu.VMEM((row, vox, channels), BF16),
            pltpu.VMEM((half, vox, channels), BF16),
            pltpu.VMEM((row, vox, channels), BF16),
            pltpu.VMEM((half, vox, channels), BF16),
            pltpu.VMEM((2 * EXTRA, vox, channels), BF16),
            pltpu.VMEM((count + row + 2 * EXTRA, vox, channels), BF16),
            pltpu.VMEM((slots, FACE, channels), BF16),
            pltpu.VMEM((slots, FACE, channels), BF16),
            pltpu.VMEM((slots, vox), jnp.int32),
            pltpu.VMEM((slots, vox), jnp.int32),
            pltpu.VMEM(volume_shape, BF16),
            pltpu.VMEM((channels // LANES, slots * vox, LANES), F32),
            pltpu.VMEM((slots * vox, channels), F32),
            pltpu.VMEM(features.shape, F32),
            dma((6,)),
            dma((6,)),
            dma((4,)),
            dma((4,)),
            dma((count,)),
            dma((count,)),
            dma((count,)),
            dma((count,)),
            dma((row,)),
            dma((row,)),
            dma((row,)),
            dma((row,)),
            dma((half,)),
            dma((half,)),
            dma((2,)),
            dma((2,)),
            dma((groups,)),
            dma((groups,)),
        ],
        compiler_params=pltpu.CompilerParams(
            collective_id=0, has_side_effects=True, vmem_limit_bytes=66_000_000
        ),
        name="merge_blocks",
    )(
        old_owner[:, 0],
        old_slot,
        neighbors.T,
        norm_scale[None, :],
        norm_shift[None, :],
        features,
        previous,
        occupancy,
        conv_weight,
        prev_weight,
    )


def merge(*arrays):
    merged, over = per_device(*arrays)
    return lax.switch(over[0], [lambda: merged, lambda: merge_full(*arrays)])


def solution(mesh):
    in_specs = (
        P(("grp", "blk"), None, None),
        P(("grp", "blk"), None),
        P(("grp", "blk"), None),
        P(("grp", "blk"), None, None),
        P(("grp", "blk"), None),
        P(("grp", "blk")),
        P(),
        P(),
        P(),
        P(),
    )
    out_specs = P(("grp", "blk"), None, None)
    return jax.shard_map(
        merge, mesh=mesh, in_specs=in_specs, out_specs=out_specs, check_vma=False
    )
```

```python
import functools

import jax
import jax.numpy as jnp
from jax import lax
from jax.experimental import pallas as pl
from jax.experimental.pallas import tpu as pltpu
from jax.sharding import PartitionSpec as P

EDGE = 4
FACE = EDGE * EDGE
VOX = EDGE * FACE
CAP = 2
LANES = 128
EXTRA = 2
PACK = 1 << 16
MESH = pl.DeviceIdType.MESH
F32 = jnp.float32
BF16 = jnp.bfloat16


def iota(shape, dim):
    return lax.broadcasted_iota(jnp.int32, shape, dim)


def one_hot(hit):
    return jnp.where(hit, 1.0, 0.0).astype(BF16)


def kernel_full(
    count,
    slots,
    channels,
    owner_hbm,
    slot_hbm,
    nb_hbm,
    scale_hbm,
    shift_hbm,
    feat_hbm,
    prev_hbm,
    occ_hbm,
    w_hbm,
    pw_hbm,
    out_ref,
    owner_s,
    slot_s,
    nb_ref,
    occ_ref,
    scale_ref,
    shift_ref,
    feat,
    prev,
    weight,
    pweight,
    proj,
    table,
    reqs,
    reqs_s,
    sendbuf,
    recv,
    low_layer,
    high_layer,
    low_occ,
    high_occ,
    volume,
    acc,
    mask,
    base,
    small_sem,
    local_sem,
    halo_send,
    halo_recv,
    rq_send,
    rq_recv,
    rp_send,
    rp_recv,
):
    me = lax.axis_index("blk")
    layer_rows = FACE * slots
    barrier = pltpu.get_barrier_semaphore()

    @pl.loop(1, count)
    def _(i):
        peer = lax.rem(me + i, count)
        pl.semaphore_signal(barrier, inc=1, device_id={"blk": peer}, device_id_type=MESH)

    small = [
        pltpu.make_async_copy(owner_hbm, owner_s, small_sem.at[0]),
        pltpu.make_async_copy(slot_hbm, slot_s, small_sem.at[1]),
        pltpu.make_async_copy(occ_hbm, occ_ref, small_sem.at[2]),
        pltpu.make_async_copy(nb_hbm, nb_ref, small_sem.at[3]),
        pltpu.make_async_copy(scale_hbm, scale_ref, small_sem.at[4]),
        pltpu.make_async_copy(shift_hbm, shift_ref, small_sem.at[5]),
    ]
    for load in small:
        load.start()
    loads = [
        pltpu.make_async_copy(prev_hbm, prev, local_sem.at[0]),
        pltpu.make_async_copy(pw_hbm, pweight, local_sem.at[1]),
        pltpu.make_async_copy(feat_hbm, feat, local_sem.at[2]),
        pltpu.make_async_copy(w_hbm, weight, local_sem.at[3]),
    ]
    for load in loads:
        load.start()

    small[0].wait()
    small[1].wait()

    lane = iota((1, LANES), 1)
    first = jnp.zeros((1, LANES), jnp.int32)
    last = jnp.zeros((1, LANES), jnp.int32)
    for s in range(slots):
        last = jnp.where(lane == owner_s[s], slot_s[s], last)
        t = slots - 1 - s
        first = jnp.where(lane == owner_s[t], slot_s[t], first)
    row = iota((CAP, LANES), 0)
    table[...] = jnp.where(row == 0, first, last)

    def layer_occ(occ, x):
        spread = one_hot(iota((VOX, layer_rows), 0) == x * FACE + iota((VOX, layer_rows), 1) % FACE)
        rows = jnp.dot(occ, spread, preferred_element_type=F32)
        own = iota((slots, layer_rows), 0) == iota((slots, layer_rows), 1) // FACE
        return jnp.sum(jnp.where(own, rows, 0.0), axis=0, keepdims=True).astype(BF16)

    pl.semaphore_wait(barrier, count - 1)

    def request(i):
        return pltpu.make_async_remote_copy(
            src_ref=table,
            dst_ref=reqs.at[me],
            send_sem=rq_send.at[i],
            recv_sem=rq_recv.at[i],
            device_id={"blk": lax.rem(me + i, count)},
            device_id_type=MESH,
        )

    @pl.loop(1, count)
    def _(i):
        request(i).start()

    up = lax.rem(me + 1, count)
    down = lax.rem(me + count - 1, count)

    def halo(k):
        if k < 2:
            src = feat_hbm.at[:, pl.ds((EDGE - 1) * FACE, FACE), :] if k == 0 else occ_hbm
            dst = low_layer if k == 0 else low_occ
            peer = up
        else:
            src = feat_hbm.at[:, pl.ds(0, FACE), :] if k == 2 else occ_hbm
            dst = high_layer if k == 2 else high_occ
            peer = down
        return pltpu.make_async_remote_copy(
            src_ref=src,
            dst_ref=dst,
            send_sem=halo_send.at[k],
            recv_sem=halo_recv.at[k],
            device_id={"blk": peer},
            device_id_type=MESH,
        )

    @pl.when(me < count - 1)
    def _():
        halo(0).start()
        halo(1).start()

    @pl.when(me > 0)
    def _():
        halo(2).start()
        halo(3).start()

    @pl.when(me == 0)
    def _():
        low_layer[...] = jnp.zeros_like(low_layer)
        low_occ[...] = jnp.zeros_like(low_occ)

    @pl.when(me == count - 1)
    def _():
        high_layer[...] = jnp.zeros_like(high_layer)
        high_occ[...] = jnp.zeros_like(high_occ)

    loads[0].wait()
    loads[1].wait()

    blocks = layer_rows // VOX
    for s in range(0, slots, blocks):
        rows = prev[s : s + blocks].reshape(layer_rows, channels)
        part = jnp.dot(rows, pweight[...], preferred_element_type=F32).astype(BF16)
        proj[s : s + blocks] = part.reshape(blocks, VOX, channels)

    reqs_s_copy = pltpu.make_async_copy(reqs, reqs_s, local_sem.at[4])

    def reply(i):
        return pltpu.make_async_remote_copy(
            src_ref=sendbuf.at[i],
            dst_ref=recv.at[me],
            send_sem=rp_send.at[i],
            recv_sem=rp_recv.at[i],
            device_id={"blk": lax.rem(me + i, count)},
            device_id_type=MESH,
        )

    reqs[me] = table[...]

    @pl.loop(1, count)
    def _(i):
        request(i).wait_recv()

    reqs_s_copy.start()
    reqs_s_copy.wait()

    def far_first(k):
        step = (k + 1) // 2
        return count // 2 + step * (2 * (k % 2) - 1)

    @pl.loop(0, count - 1)
    def _(k):
        i = far_first(k)
        peer = lax.rem(me + i, count)
        sendbuf[i, 0] = proj[reqs_s[peer, 0, me]]
        sendbuf[i, 1] = proj[reqs_s[peer, 1, me]]

    @pl.loop(0, count - 1)
    def _(k):
        reply(far_first(k)).start()

    recv[me, 0] = proj[reqs_s[me, 0, me]]
    recv[me, 1] = proj[reqs_s[me, 1, me]]

    for load in small[2:]:
        load.wait()
    occ = occ_ref[...].astype(BF16)
    volume[...] = jnp.zeros_like(volume)
    loads[2].wait()
    col = iota((layer_rows, layer_rows), 1)
    line = iota((layer_rows, layer_rows), 0)
    select_own = one_hot(col == (line % slots) * FACE + line // slots)
    spread = one_hot(iota((layer_rows, slots), 0) % slots == iota((layer_rows, slots), 1))
    nb = lax.dot_general(
        spread,
        nb_ref[...].astype(F32).astype(BF16),
        (((1,), (1,)), ((), ())),
        preferred_element_type=F32,
    ).astype(jnp.int32)
    side_rows = EDGE * slots
    scol = iota((side_rows, layer_rows), 1)
    sline = iota((side_rows, 1), 0) // slots

    def side(f, fixed, step):
        wanted = nb[:side_rows, f : f + 1]
        target = jnp.where(wanted >= 0, wanted * FACE + fixed + sline * step, -1)
        return one_hot(scol == target)

    sides = [
        side(2, (EDGE - 1) * EDGE, 1),
        side(3, 0, 1),
        side(4, EDGE - 1, EDGE),
        side(5, 0, EDGE),
    ]
    select = jnp.concatenate([select_own] + sides, axis=0)
    for x in range(EDGE):
        layer = feat[:, x * FACE : (x + 1) * FACE, :].reshape(layer_rows, channels)
        part = jnp.dot(select * layer_occ(occ, x), layer, preferred_element_type=F32).astype(BF16)
        volume[x + 1, 1 : EDGE + 1, 1 : EDGE + 1] = part[:layer_rows].reshape(
            EDGE, EDGE, slots, channels
        )
        faces = part[layer_rows:].reshape(4, EDGE, slots, channels)
        volume[x + 1, 0, 1 : EDGE + 1] = faces[0]
        volume[x + 1, EDGE + 1, 1 : EDGE + 1] = faces[1]
        volume[x + 1, 1 : EDGE + 1, 0] = faces[2]
        volume[x + 1, 1 : EDGE + 1, EDGE + 1] = faces[3]

    @pl.when(me > 0)
    def _():
        pltpu.make_async_remote_copy(
            src_ref=feat_hbm.at[:, pl.ds(0, FACE), :],
            dst_ref=low_layer,
            send_sem=halo_send.at[0],
            recv_sem=halo_recv.at[0],
            device_id={"blk": up},
            device_id_type=MESH,
        ).wait_recv()
        halo(1).wait_recv()

    @pl.when(me < count - 1)
    def _():
        halo(2).wait_recv()
        halo(3).wait_recv()

    def x_face(f, layer_ref, other_occ, x):
        wanted = nb[:, f : f + 1]
        target = jnp.where(wanted >= 0, wanted * FACE + iota((layer_rows, 1), 0) // slots, -1)
        pick = one_hot(col == target) * layer_occ(other_occ[...].astype(BF16), x)
        layer = layer_ref[...].reshape(layer_rows, channels)
        part = jnp.dot(pick, layer, preferred_element_type=F32).astype(BF16)
        return part.reshape(EDGE, EDGE, slots, channels)

    volume[0, 1 : EDGE + 1, 1 : EDGE + 1] = x_face(0, low_layer, low_occ, EDGE - 1)
    volume[EDGE + 1, 1 : EDGE + 1, 1 : EDGE + 1] = x_face(1, high_layer, high_occ, 0)

    loads[3].wait()
    scale = scale_ref[...]
    shift = shift_ref[...]

    @pl.loop(0, EDGE)
    def _(x):
        total = jnp.zeros((layer_rows, channels), F32)
        for tap in range(27):
            a, b, c = tap // 9, (tap // 3) % 3, tap % 3
            window = volume[x + a, b : b + EDGE, c : c + EDGE].reshape(layer_rows, channels)
            total = total + jnp.dot(window, weight[tap], preferred_element_type=F32)
        hidden = jnp.maximum(total * scale + shift, 0.0)
        for k in range(channels // LANES):
            acc[k, pl.ds(x * layer_rows, layer_rows), :] = hidden[:, k * LANES : (k + 1) * LANES]

    @pl.loop(0, slots)
    def _(s):
        mine = jnp.where(iota((VOX, VOX), 0) == iota((VOX, VOX), 1), occ_ref[pl.ds(s, 1), :], 0)
        mask[pl.ds(s * VOX, VOX), :] = jnp.dot(
            mine.astype(BF16), jnp.ones((VOX, channels), BF16), preferred_element_type=F32
        )

    picks = []
    for s in range(slots):
        rank = jnp.int32(0)
        for t in range(s):
            rank = jnp.where(owner_s[t] == owner_s[s], 1, rank)
        picks.append(rank)
        hidden = jnp.concatenate(
            [acc[k, pl.ds(s, VOX, stride=slots), :] for k in range(channels // LANES)],
            axis=1,
        )
        base[s] = hidden * mask[s * VOX : (s + 1) * VOX, :]

    @pl.loop(1, count)
    def _(i):
        reply(i).wait_recv()

    for s in range(slots):
        moved = recv[owner_s[s], picks[s]].astype(F32)
        out_ref[s] = (base[s] + moved * mask[s * VOX : (s + 1) * VOX, :]).astype(BF16)

    @pl.loop(1, count)
    def _(i):
        request(i).wait_send()
        reply(i).wait_send()

    @pl.when(me < count - 1)
    def _():
        halo(0).wait_send()
        halo(1).wait_send()

    @pl.when(me > 0)
    def _():
        halo(2).wait_send()
        halo(3).wait_send()


def merge_full(
    features,
    occupancy,
    neighbors,
    previous,
    old_owner,
    old_slot,
    conv_weight,
    norm_scale,
    norm_shift,
    prev_weight,
):
    slots, vox, channels = features.shape
    count = lax.axis_size("blk")
    hbm = pl.BlockSpec(memory_space=pl.ANY)
    volume_shape = (EDGE + 2, EDGE + 2, EDGE + 2, slots, channels)
    dma = pltpu.SemaphoreType.DMA
    return pl.pallas_call(
        functools.partial(kernel_full, count, slots, channels),
        out_shape=pltpu.VMEM(features.shape, BF16),
        in_specs=[hbm] * 10,
        out_specs=pl.BlockSpec(memory_space=pltpu.VMEM),
        scratch_shapes=[
            pltpu.SMEM((slots,), jnp.int32),
            pltpu.SMEM((slots,), jnp.int32),
            pltpu.VMEM((6, slots), jnp.int32),
            pltpu.VMEM((slots, vox), jnp.int32),
            pltpu.VMEM((1, channels), F32),
            pltpu.VMEM((1, channels), F32),
            pltpu.VMEM(features.shape, BF16),
            pltpu.VMEM(previous.shape, BF16),
            pltpu.VMEM(conv_weight.shape, BF16),
            pltpu.VMEM(prev_weight.shape, BF16),
            pltpu.VMEM(previous.shape, BF16),
            pltpu.VMEM((CAP, LANES), jnp.int32),
            pltpu.VMEM((count, CAP, LANES), jnp.int32),
            pltpu.SMEM((count, CAP, LANES), jnp.int32),
            pltpu.VMEM((count, CAP, vox, channels), BF16),
            pltpu.VMEM((count, CAP, vox, channels), BF16),
            pltpu.VMEM((slots, FACE, channels), BF16),
            pltpu.VMEM((slots, FACE, channels), BF16),
            pltpu.VMEM((slots, vox), jnp.int32),
            pltpu.VMEM((slots, vox), jnp.int32),
            pltpu.VMEM(volume_shape, BF16),
            pltpu.VMEM((channels // LANES, slots * vox, LANES), F32),
            pltpu.VMEM((slots * vox, channels), F32),
            pltpu.VMEM(features.shape, F32),
            dma((6,)),
            dma((6,)),
            dma((4,)),
            dma((4,)),
            dma((count,)),
            dma((count,)),
            dma((count,)),
            dma((count,)),
        ],
        compiler_params=pltpu.CompilerParams(
            collective_id=1, has_side_effects=True, vmem_limit_bytes=66_000_000
        ),
        name="merge_full",
    )(
        old_owner[:, 0],
        old_slot,
        neighbors.T,
        norm_scale[None, :],
        norm_shift[None, :],
        features,
        previous,
        occupancy,
        conv_weight,
        prev_weight,
    )


def kernel(
    count,
    groups,
    slots,
    channels,
    owner_hbm,
    slot_hbm,
    nb_hbm,
    scale_hbm,
    shift_hbm,
    feat_hbm,
    prev_hbm,
    occ_hbm,
    w_hbm,
    pw_hbm,
    out_ref,
    over_ref,
    owner_s,
    slot_s,
    nb_ref,
    occ_ref,
    scale_ref,
    shift_ref,
    feat,
    prev,
    weight,
    pweight,
    proj,
    table,
    near_reqs,
    far_reqs,
    first_s,
    last_s,
    place_s,
    over,
    overs,
    send_first,
    send_row,
    send_z,
    send_x,
    relay_z,
    relay_x,
    relay_out,
    recv,
    low_layer,
    high_layer,
    low_occ,
    high_occ,
    volume,
    acc,
    mask,
    base,
    small_sem,
    local_sem,
    halo_send,
    halo_recv,
    rq_send,
    rq_recv,
    first_send,
    first_recv,
    row_send,
    row_recv,
    z_send,
    z_recv,
    x_send,
    x_recv,
    out_send,
    out_recv,
    over_send,
    over_recv,
):
    me = lax.axis_index("blk")
    grp = lax.axis_index("grp")
    half, row = count // 2, count // 4
    half_base = me // half * half
    row_base = me // row * row
    half_at, row_at = me - half_base, me - row_base
    other_half = half - half_base
    other_row = 2 * half_base + row - row_base
    across = lax.rem(me + half, count)
    beside = other_row + row_at
    row_part, z_part, x_part = count, count + row, count + row + EXTRA
    layer_rows = FACE * slots
    barrier = pltpu.get_barrier_semaphore()

    @pl.loop(1, count)
    def _(i):
        peer = lax.rem(me + i, count)
        pl.semaphore_signal(barrier, inc=1, device_id={"blk": peer}, device_id_type=MESH)

    for i in range(1, groups):
        there = lax.rem(grp + i, groups)
        pl.semaphore_signal(barrier, inc=1, device_id={"grp": there}, device_id_type=MESH)

    small = [
        pltpu.make_async_copy(owner_hbm, owner_s, small_sem.at[0]),
        pltpu.make_async_copy(slot_hbm, slot_s, small_sem.at[1]),
        pltpu.make_async_copy(occ_hbm, occ_ref, small_sem.at[2]),
        pltpu.make_async_copy(nb_hbm, nb_ref, small_sem.at[3]),
        pltpu.make_async_copy(scale_hbm, scale_ref, small_sem.at[4]),
        pltpu.make_async_copy(shift_hbm, shift_ref, small_sem.at[5]),
    ]
    for load in small:
        load.start()
    loads = [
        pltpu.make_async_copy(prev_hbm, prev, local_sem.at[0]),
        pltpu.make_async_copy(pw_hbm, pweight, local_sem.at[1]),
        pltpu.make_async_copy(feat_hbm, feat, local_sem.at[2]),
        pltpu.make_async_copy(w_hbm, weight, local_sem.at[3]),
    ]
    for load in loads:
        load.start()

    small[0].wait()
    small[1].wait()

    lane = iota((1, LANES), 1)
    first = jnp.zeros((1, LANES), jnp.int32)
    last = jnp.zeros((1, LANES), jnp.int32)
    for s in range(slots):
        last = jnp.where(lane == owner_s[s], slot_s[s], last)
        t = slots - 1 - s
        first = jnp.where(lane == owner_s[t], slot_s[t], first)
    zero = jnp.int32(0)
    x_count, z_count = zero, zero
    x_owner, z_owner = [zero] * EXTRA, [zero] * EXTRA
    for s in range(slots):
        owner = owner_s[s]
        again = zero
        for t in range(s):
            again = jnp.where(owner_s[t] == owner, 1, again)
        far = jnp.where((owner < half_base) | (owner >= half_base + half), again, 0)
        near = jnp.where((owner >= other_row) & (owner < other_row + row), again, 0)
        for e in range(EXTRA):
            x_owner[e] = jnp.where((far == 1) & (x_count == e), owner - other_half, x_owner[e])
            z_owner[e] = jnp.where((near == 1) & (z_count == e), owner - other_row, z_owner[e])
        at = jnp.where(again == 1, row_part + owner - row_base, owner)
        at = jnp.where(near == 1, z_part + jnp.minimum(z_count, EXTRA - 1), at)
        place_s[s] = jnp.where(far == 1, x_part + jnp.minimum(x_count, EXTRA - 1), at)
        x_count = x_count + far
        z_count = z_count + near
    notes = jnp.where(
        lane == count + 2 * EXTRA, jnp.where((x_count > EXTRA) | (z_count > EXTRA), 1, 0), first + last * PACK
    )
    for e in range(EXTRA):
        notes = jnp.where(lane == count + e, x_owner[e], notes)
        notes = jnp.where(lane == count + EXTRA + e, z_owner[e], notes)
    table[...] = notes

    def layer_occ(occ, x):
        spread = one_hot(iota((VOX, layer_rows), 0) == x * FACE + iota((VOX, layer_rows), 1) % FACE)
        rows = jnp.dot(occ, spread, preferred_element_type=F32)
        own = iota((slots, layer_rows), 0) == iota((slots, layer_rows), 1) // FACE
        return jnp.sum(jnp.where(own, rows, 0.0), axis=0, keepdims=True).astype(BF16)

    pl.semaphore_wait(barrier, count + groups - 2)

    def in_half(i):
        return half_base + lax.rem(half_at + i, half)

    def in_other(i):
        return other_half + lax.rem(half_at + i, half)

    def in_row(i):
        return row_base + lax.rem(row_at + i, row)

    def request(i, far):
        return pltpu.make_async_remote_copy(
            src_ref=table,
            dst_ref=(far_reqs if far else near_reqs).at[half_at],
            send_sem=rq_send.at[far * half + i],
            recv_sem=rq_recv.at[far * half + i],
            device_id={"blk": in_other(i) if far else in_half(i)},
            device_id_type=MESH,
        )

    @pl.loop(0, half)
    def _(i):
        request(i, 1).start()

    @pl.loop(1, half)
    def _(i):
        request(i, 0).start()

    up = lax.rem(me + 1, count)
    down = lax.rem(me + count - 1, count)

    def halo(k):
        if k < 2:
            src = feat_hbm.at[:, pl.ds((EDGE - 1) * FACE, FACE), :] if k == 0 else occ_hbm
            dst = low_layer if k == 0 else low_occ
            peer = up
        else:
            src = feat_hbm.at[:, pl.ds(0, FACE), :] if k == 2 else occ_hbm
            dst = high_layer if k == 2 else high_occ
            peer = down
        return pltpu.make_async_remote_copy(
            src_ref=src,
            dst_ref=dst,
            send_sem=halo_send.at[k],
            recv_sem=halo_recv.at[k],
            device_id={"blk": peer},
            device_id_type=MESH,
        )

    @pl.when(me < count - 1)
    def _():
        halo(0).start()
        halo(1).start()

    @pl.when(me > 0)
    def _():
        halo(2).start()
        halo(3).start()

    @pl.when(me == 0)
    def _():
        low_layer[...] = jnp.zeros_like(low_layer)
        low_occ[...] = jnp.zeros_like(low_occ)

    @pl.when(me == count - 1)
    def _():
        high_layer[...] = jnp.zeros_like(high_layer)
        high_occ[...] = jnp.zeros_like(high_occ)

    loads[0].wait()
    loads[1].wait()

    blocks = layer_rows // VOX
    for s in range(0, slots, blocks):
        rows = prev[s : s + blocks].reshape(layer_rows, channels)
        part = jnp.dot(rows, pweight[...], preferred_element_type=F32).astype(BF16)
        proj[s : s + blocks] = part.reshape(blocks, VOX, channels)

    near_reqs[half_at] = table[...]

    def first_to(i, far):
        return pltpu.make_async_remote_copy(
            src_ref=send_first.at[far * half + i],
            dst_ref=recv.at[me],
            send_sem=first_send.at[far * half + i],
            recv_sem=first_recv.at[far * half + i],
            device_id={"blk": in_other(i) if far else in_half(i)},
            device_id_type=MESH,
        )

    def row_to(i):
        return pltpu.make_async_remote_copy(
            src_ref=send_row.at[i],
            dst_ref=recv.at[row_part + row_at],
            send_sem=row_send.at[i],
            recv_sem=row_recv.at[i],
            device_id={"blk": in_row(i)},
            device_id_type=MESH,
        )

    def z_to(i):
        return pltpu.make_async_remote_copy(
            src_ref=send_z.at[i],
            dst_ref=relay_z.at[row_at],
            send_sem=z_send.at[i],
            recv_sem=z_recv.at[i],
            device_id={"blk": in_row(i)},
            device_id_type=MESH,
        )

    def x_to(i):
        return pltpu.make_async_remote_copy(
            src_ref=send_x.at[i],
            dst_ref=relay_x.at[half_at],
            send_sem=x_send.at[i],
            recv_sem=x_recv.at[i],
            device_id={"blk": in_half(i)},
            device_id_type=MESH,
        )

    def relay(k):
        part, peer = ((x_part, across), (z_part, beside))[k]
        return pltpu.make_async_remote_copy(
            src_ref=relay_out.at[pl.ds(k * EXTRA, EXTRA)],
            dst_ref=recv.at[pl.ds(part, EXTRA)],
            send_sem=out_send.at[k],
            recv_sem=out_recv.at[k],
            device_id={"blk": peer},
            device_id_type=MESH,
        )

    def over_to(i):
        return pltpu.make_async_remote_copy(
            src_ref=over,
            dst_ref=overs.at[grp],
            send_sem=over_send.at[i],
            recv_sem=over_recv.at[i],
            device_id={"grp": lax.rem(grp + i, groups)},
            device_id_type=MESH,
        )

    def near_entry(peer, at):
        return jnp.sum(jnp.where(lane == at, near_reqs[peer - half_base], 0))

    def far_entry(peer, at):
        return jnp.sum(jnp.where(lane == at, far_reqs[peer - other_half], 0))

    def send_far(i):
        send_first[half + i] = proj[first_s[in_other(i)]]
        first_to(i, 1).start()

    def send_across(i):
        send_x[i] = proj[last_s[in_other(i)]]
        x_to(i).start()

    def send_near(i):
        send_first[i] = proj[first_s[in_half(i)]]
        first_to(i, 0).start()

    def send_beside(i):
        send_z[i] = proj[last_s[other_row + lax.rem(row_at + i, row)]]
        z_to(i).start()

    def send_second(i):
        send_row[i] = proj[last_s[in_row(i)]]
        row_to(i).start()

    @pl.loop(0, half)
    def _(i):
        request(i, 1).wait_recv()

    for d in range(half):
        wanted = far_entry(other_half + d, me)
        first_s[other_half + d] = wanted % PACK
        last_s[other_half + d] = wanted // PACK

    @pl.loop(0, 2)
    def _(i):
        send_far(i)

    @pl.loop(1, half)
    def _(i):
        send_across(i)

    @pl.loop(2, half)
    def _(i):
        send_far(i)

    @pl.loop(1, half)
    def _(i):
        request(i, 0).wait_recv()

    for d in range(half):
        wanted = near_entry(half_base + d, me)
        first_s[half_base + d] = wanted % PACK
        last_s[half_base + d] = wanted // PACK

    @pl.loop(1, row)
    def _(i):
        send_beside(i)

    @pl.loop(1, half)
    def _(i):
        send_near(i)

    @pl.loop(1, row)
    def _(i):
        send_second(i)

    recv[me] = proj[first_s[me]]
    recv[row_part + row_at] = proj[last_s[me]]
    relay_x[half_at] = proj[last_s[across]]
    relay_z[row_at] = proj[last_s[beside]]

    notes = near_reqs[...].reshape(half, LANES) + far_reqs[...].reshape(half, LANES)
    over[...] = jnp.sum(jnp.where(lane == count + 2 * EXTRA, notes, 0), axis=0, keepdims=True)
    for i in range(1, groups):
        over_to(i).start()

    for load in small[2:]:
        load.wait()
    occ = occ_ref[...].astype(BF16)
    volume[...] = jnp.zeros_like(volume)
    loads[2].wait()
    col = iota((layer_rows, layer_rows), 1)
    line = iota((layer_rows, layer_rows), 0)
    select_own = one_hot(col == (line % slots) * FACE + line // slots)
    spread = one_hot(iota((layer_rows, slots), 0) % slots == iota((layer_rows, slots), 1))
    nb = lax.dot_general(
        spread,
        nb_ref[...].astype(F32).astype(BF16),
        (((1,), (1,)), ((), ())),
        preferred_element_type=F32,
    ).astype(jnp.int32)
    side_rows = EDGE * slots
    scol = iota((side_rows, layer_rows), 1)
    sline = iota((side_rows, 1), 0) // slots

    def side(f, fixed, step):
        wanted = nb[:side_rows, f : f + 1]
        target = jnp.where(wanted >= 0, wanted * FACE + fixed + sline * step, -1)
        return one_hot(scol == target)

    sides = [
        side(2, (EDGE - 1) * EDGE, 1),
        side(3, 0, 1),
        side(4, EDGE - 1, EDGE),
        side(5, 0, EDGE),
    ]
    select = jnp.concatenate([select_own] + sides, axis=0)
    for x in range(EDGE):
        layer = feat[:, x * FACE : (x + 1) * FACE, :].reshape(layer_rows, channels)
        part = jnp.dot(select * layer_occ(occ, x), layer, preferred_element_type=F32).astype(BF16)
        volume[x + 1, 1 : EDGE + 1, 1 : EDGE + 1] = part[:layer_rows].reshape(
            EDGE, EDGE, slots, channels
        )
        faces = part[layer_rows:].reshape(4, EDGE, slots, channels)
        volume[x + 1, 0, 1 : EDGE + 1] = faces[0]
        volume[x + 1, EDGE + 1, 1 : EDGE + 1] = faces[1]
        volume[x + 1, 1 : EDGE + 1, 0] = faces[2]
        volume[x + 1, 1 : EDGE + 1, EDGE + 1] = faces[3]

    @pl.when(me > 0)
    def _():
        pltpu.make_async_remote_copy(
            src_ref=feat_hbm.at[:, pl.ds(0, FACE), :],
            dst_ref=low_layer,
            send_sem=halo_send.at[0],
            recv_sem=halo_recv.at[0],
            device_id={"blk": up},
            device_id_type=MESH,
        ).wait_recv()
        halo(1).wait_recv()

    @pl.when(me < count - 1)
    def _():
        halo(2).wait_recv()
        halo(3).wait_recv()

    def x_face(f, layer_ref, other_occ, x):
        wanted = nb[:, f : f + 1]
        target = jnp.where(wanted >= 0, wanted * FACE + iota((layer_rows, 1), 0) // slots, -1)
        pick = one_hot(col == target) * layer_occ(other_occ[...].astype(BF16), x)
        layer = layer_ref[...].reshape(layer_rows, channels)
        part = jnp.dot(pick, layer, preferred_element_type=F32).astype(BF16)
        return part.reshape(EDGE, EDGE, slots, channels)

    volume[0, 1 : EDGE + 1, 1 : EDGE + 1] = x_face(0, low_layer, low_occ, EDGE - 1)
    volume[EDGE + 1, 1 : EDGE + 1, 1 : EDGE + 1] = x_face(1, high_layer, high_occ, 0)

    loads[3].wait()
    scale = scale_ref[...]
    shift = shift_ref[...]

    @pl.loop(0, 1)
    def _(x):
        total = jnp.zeros((layer_rows, channels), F32)
        for tap in range(27):
            a, b, c = tap // 9, (tap // 3) % 3, tap % 3
            window = volume[x + a, b : b + EDGE, c : c + EDGE].reshape(layer_rows, channels)
            total = total + jnp.dot(window, weight[tap], preferred_element_type=F32)
        hidden = jnp.maximum(total * scale + shift, 0.0)
        for k in range(channels // LANES):
            acc[k, pl.ds(x * layer_rows, layer_rows), :] = hidden[:, k * LANES : (k + 1) * LANES]

    @pl.loop(1, half)
    def _(i):
        x_to(i).wait_recv()

    @pl.loop(1, row)
    def _(i):
        z_to(i).wait_recv()

    for e in range(EXTRA):
        relay_out[e] = relay_x[far_entry(across, count + e)]
        relay_out[EXTRA + e] = relay_z[near_entry(beside, count + EXTRA + e)]
    relay(0).start()
    relay(1).start()

    @pl.loop(1, EDGE)
    def _(x):
        total = jnp.zeros((layer_rows, channels), F32)
        for tap in range(27):
            a, b, c = tap // 9, (tap // 3) % 3, tap % 3
            window = volume[x + a, b : b + EDGE, c : c + EDGE].reshape(layer_rows, channels)
            total = total + jnp.dot(window, weight[tap], preferred_element_type=F32)
        hidden = jnp.maximum(total * scale + shift, 0.0)
        for k in range(channels // LANES):
            acc[k, pl.ds(x * layer_rows, layer_rows), :] = hidden[:, k * LANES : (k + 1) * LANES]

    @pl.loop(0, slots)
    def _(s):
        mine = jnp.where(iota((VOX, VOX), 0) == iota((VOX, VOX), 1), occ_ref[pl.ds(s, 1), :], 0)
        mask[pl.ds(s * VOX, VOX), :] = jnp.dot(
            mine.astype(BF16), jnp.ones((VOX, channels), BF16), preferred_element_type=F32
        )

    for s in range(slots):
        hidden = jnp.concatenate(
            [acc[k, pl.ds(s, VOX, stride=slots), :] for k in range(channels // LANES)],
            axis=1,
        )
        base[s] = hidden * mask[s * VOX : (s + 1) * VOX, :]

    overs[grp] = over[...]
    for i in range(1, groups):
        over_to(i).wait_recv()
    over_ref[0] = jnp.sum(overs[...])

    @pl.loop(0, half)
    def _(i):
        request(i, 1).wait_send()
        first_to(i, 1).wait_send()

    @pl.loop(1, half)
    def _(i):
        request(i, 0).wait_send()
        first_to(i, 0).wait_send()

    @pl.loop(1, half)
    def _(i):
        x_to(i).wait_send()

    @pl.loop(1, row)
    def _(i):
        row_to(i).wait_send()
        z_to(i).wait_send()

    relay(0).wait_send()
    relay(1).wait_send()
    for i in range(1, groups):
        over_to(i).wait_send()

    @pl.when(me < count - 1)
    def _():
        halo(0).wait_send()
        halo(1).wait_send()

    @pl.when(me > 0)
    def _():
        halo(2).wait_send()
        halo(3).wait_send()

    @pl.loop(0, half)
    def _(i):
        first_to(i, 1).wait_recv()

    @pl.loop(1, half)
    def _(i):
        first_to(i, 0).wait_recv()

    @pl.loop(1, row)
    def _(i):
        row_to(i).wait_recv()

    relay(0).wait_recv()
    relay(1).wait_recv()

    for s in range(slots):
        moved = recv[place_s[s]].astype(F32)
        out_ref[s] = (base[s] + moved * mask[s * VOX : (s + 1) * VOX, :]).astype(BF16)


def per_device(
    features,
    occupancy,
    neighbors,
    previous,
    old_owner,
    old_slot,
    conv_weight,
    norm_scale,
    norm_shift,
    prev_weight,
):
    slots, vox, channels = features.shape
    count = lax.axis_size("blk")
    groups = lax.axis_size("grp")
    half, row = count // 2, count // 4
    hbm = pl.BlockSpec(memory_space=pl.ANY)
    volume_shape = (EDGE + 2, EDGE + 2, EDGE + 2, slots, channels)
    dma = pltpu.SemaphoreType.DMA
    return pl.pallas_call(
        functools.partial(kernel, count, groups, slots, channels),
        out_shape=[
            pltpu.VMEM(features.shape, BF16),
            pltpu.SMEM((1,), jnp.int32),
        ],
        in_specs=[hbm] * 10,
        out_specs=[
            pl.BlockSpec(memory_space=pltpu.VMEM),
            pl.BlockSpec(memory_space=pltpu.SMEM),
        ],
        scratch_shapes=[
            pltpu.SMEM((slots,), jnp.int32),
            pltpu.SMEM((slots,), jnp.int32),
            pltpu.VMEM((6, slots), jnp.int32),
            pltpu.VMEM((slots, vox), jnp.int32),
            pltpu.VMEM((1, channels), F32),
            pltpu.VMEM((1, channels), F32),
            pltpu.VMEM(features.shape, BF16),
            pltpu.VMEM(previous.shape, BF16),
            pltpu.VMEM(conv_weight.shape, BF16),
            pltpu.VMEM(prev_weight.shape, BF16),
            pltpu.VMEM(previous.shape, BF16),
            pltpu.VMEM((1, LANES), jnp.int32),
            pltpu.VMEM((half, 1, LANES), jnp.int32),
            pltpu.VMEM((half, 1, LANES), jnp.int32),
            pltpu.SMEM((count,), jnp.int32),
            pltpu.SMEM((count,), jnp.int32),
            pltpu.SMEM((slots,), jnp.int32),
            pltpu.VMEM((1, LANES), jnp.int32),
            pltpu.VMEM((groups, 1, LANES), jnp.int32),
            pltpu.VMEM((count, vox, channels), BF16),
            pltpu.VMEM((row, vox, channels), BF16),
            pltpu.VMEM((row, vox, channels), BF16),
            pltpu.VMEM((half, vox, channels), BF16),
            pltpu.VMEM((row, vox, channels), BF16),
            pltpu.VMEM((half, vox, channels), BF16),
            pltpu.VMEM((2 * EXTRA, vox, channels), BF16),
            pltpu.VMEM((count + row + 2 * EXTRA, vox, channels), BF16),
            pltpu.VMEM((slots, FACE, channels), BF16),
            pltpu.VMEM((slots, FACE, channels), BF16),
            pltpu.VMEM((slots, vox), jnp.int32),
            pltpu.VMEM((slots, vox), jnp.int32),
            pltpu.VMEM(volume_shape, BF16),
            pltpu.VMEM((channels // LANES, slots * vox, LANES), F32),
            pltpu.VMEM((slots * vox, channels), F32),
            pltpu.VMEM(features.shape, F32),
            dma((6,)),
            dma((6,)),
            dma((4,)),
            dma((4,)),
            dma((count,)),
            dma((count,)),
            dma((count,)),
            dma((count,)),
            dma((row,)),
            dma((row,)),
            dma((row,)),
            dma((row,)),
            dma((half,)),
            dma((half,)),
            dma((2,)),
            dma((2,)),
            dma((groups,)),
            dma((groups,)),
        ],
        compiler_params=pltpu.CompilerParams(
            collective_id=0, has_side_effects=True, vmem_limit_bytes=66_000_000
        ),
        name="merge_blocks",
    )(
        old_owner[:, 0],
        old_slot,
        neighbors.T,
        norm_scale[None, :],
        norm_shift[None, :],
        features,
        previous,
        occupancy,
        conv_weight,
        prev_weight,
    )


def merge(*arrays):
    merged, over = per_device(*arrays)
    return lax.switch(over[0], [lambda: merged, lambda: merge_full(*arrays)])


def solution(mesh):
    in_specs = (
        P(("grp", "blk"), None, None),
        P(("grp", "blk"), None),
        P(("grp", "blk"), None),
        P(("grp", "blk"), None, None),
        P(("grp", "blk"), None),
        P(("grp", "blk")),
        P(),
        P(),
        P(),
        P(),
    )
    out_specs = P(("grp", "blk"), None, None)
    return jax.shard_map(
        merge, mesh=mesh, in_specs=in_specs, out_specs=out_specs, check_vma=False
    )
```

```python
import functools

import jax
import jax.numpy as jnp
from jax import lax
from jax.experimental import pallas as pl
from jax.experimental.pallas import tpu as pltpu
from jax.sharding import PartitionSpec as P

EDGE = 4
FACE = EDGE * EDGE
VOX = EDGE * FACE
CAP = 2
LANES = 128
EXTRA = 2
PACK = 1 << 16
MESH = pl.DeviceIdType.MESH
F32 = jnp.float32
BF16 = jnp.bfloat16


def iota(shape, dim):
    return lax.broadcasted_iota(jnp.int32, shape, dim)


def one_hot(hit):
    return jnp.where(hit, 1.0, 0.0).astype(BF16)


def kernel_full(
    count,
    slots,
    channels,
    owner_hbm,
    slot_hbm,
    nb_hbm,
    scale_hbm,
    shift_hbm,
    feat_hbm,
    prev_hbm,
    occ_hbm,
    w_hbm,
    pw_hbm,
    out_ref,
    owner_s,
    slot_s,
    nb_ref,
    occ_ref,
    scale_ref,
    shift_ref,
    feat,
    prev,
    weight,
    pweight,
    proj,
    table,
    reqs,
    reqs_s,
    sendbuf,
    recv,
    low_layer,
    high_layer,
    low_occ,
    high_occ,
    volume,
    acc,
    mask,
    base,
    small_sem,
    local_sem,
    halo_send,
    halo_recv,
    rq_send,
    rq_recv,
    rp_send,
    rp_recv,
):
    me = lax.axis_index("blk")
    layer_rows = FACE * slots
    barrier = pltpu.get_barrier_semaphore()

    @pl.loop(1, count)
    def _(i):
        peer = lax.rem(me + i, count)
        pl.semaphore_signal(barrier, inc=1, device_id={"blk": peer}, device_id_type=MESH)

    small = [
        pltpu.make_async_copy(owner_hbm, owner_s, small_sem.at[0]),
        pltpu.make_async_copy(slot_hbm, slot_s, small_sem.at[1]),
        pltpu.make_async_copy(occ_hbm, occ_ref, small_sem.at[2]),
        pltpu.make_async_copy(nb_hbm, nb_ref, small_sem.at[3]),
        pltpu.make_async_copy(scale_hbm, scale_ref, small_sem.at[4]),
        pltpu.make_async_copy(shift_hbm, shift_ref, small_sem.at[5]),
    ]
    for load in small:
        load.start()
    loads = [
        pltpu.make_async_copy(prev_hbm, prev, local_sem.at[0]),
        pltpu.make_async_copy(pw_hbm, pweight, local_sem.at[1]),
        pltpu.make_async_copy(feat_hbm, feat, local_sem.at[2]),
        pltpu.make_async_copy(w_hbm, weight, local_sem.at[3]),
    ]
    for load in loads:
        load.start()

    small[0].wait()
    small[1].wait()

    lane = iota((1, LANES), 1)
    first = jnp.zeros((1, LANES), jnp.int32)
    last = jnp.zeros((1, LANES), jnp.int32)
    for s in range(slots):
        last = jnp.where(lane == owner_s[s], slot_s[s], last)
        t = slots - 1 - s
        first = jnp.where(lane == owner_s[t], slot_s[t], first)
    row = iota((CAP, LANES), 0)
    table[...] = jnp.where(row == 0, first, last)

    def layer_occ(occ, x):
        spread = one_hot(iota((VOX, layer_rows), 0) == x * FACE + iota((VOX, layer_rows), 1) % FACE)
        rows = jnp.dot(occ, spread, preferred_element_type=F32)
        own = iota((slots, layer_rows), 0) == iota((slots, layer_rows), 1) // FACE
        return jnp.sum(jnp.where(own, rows, 0.0), axis=0, keepdims=True).astype(BF16)

    pl.semaphore_wait(barrier, count - 1)

    def request(i):
        return pltpu.make_async_remote_copy(
            src_ref=table,
            dst_ref=reqs.at[me],
            send_sem=rq_send.at[i],
            recv_sem=rq_recv.at[i],
            device_id={"blk": lax.rem(me + i, count)},
            device_id_type=MESH,
        )

    @pl.loop(1, count)
    def _(i):
        request(i).start()

    up = lax.rem(me + 1, count)
    down = lax.rem(me + count - 1, count)

    def halo(k):
        if k < 2:
            src = feat_hbm.at[:, pl.ds((EDGE - 1) * FACE, FACE), :] if k == 0 else occ_hbm
            dst = low_layer if k == 0 else low_occ
            peer = up
        else:
            src = feat_hbm.at[:, pl.ds(0, FACE), :] if k == 2 else occ_hbm
            dst = high_layer if k == 2 else high_occ
            peer = down
        return pltpu.make_async_remote_copy(
            src_ref=src,
            dst_ref=dst,
            send_sem=halo_send.at[k],
            recv_sem=halo_recv.at[k],
            device_id={"blk": peer},
            device_id_type=MESH,
        )

    @pl.when(me < count - 1)
    def _():
        halo(0).start()
        halo(1).start()

    @pl.when(me > 0)
    def _():
        halo(2).start()
        halo(3).start()

    @pl.when(me == 0)
    def _():
        low_layer[...] = jnp.zeros_like(low_layer)
        low_occ[...] = jnp.zeros_like(low_occ)

    @pl.when(me == count - 1)
    def _():
        high_layer[...] = jnp.zeros_like(high_layer)
        high_occ[...] = jnp.zeros_like(high_occ)

    loads[0].wait()
    loads[1].wait()

    blocks = layer_rows // VOX
    for s in range(0, slots, blocks):
        rows = prev[s : s + blocks].reshape(layer_rows, channels)
        part = jnp.dot(rows, pweight[...], preferred_element_type=F32).astype(BF16)
        proj[s : s + blocks] = part.reshape(blocks, VOX, channels)

    reqs_s_copy = pltpu.make_async_copy(reqs, reqs_s, local_sem.at[4])

    def reply(i):
        return pltpu.make_async_remote_copy(
            src_ref=sendbuf.at[i],
            dst_ref=recv.at[me],
            send_sem=rp_send.at[i],
            recv_sem=rp_recv.at[i],
            device_id={"blk": lax.rem(me + i, count)},
            device_id_type=MESH,
        )

    reqs[me] = table[...]

    @pl.loop(1, count)
    def _(i):
        request(i).wait_recv()

    reqs_s_copy.start()
    reqs_s_copy.wait()

    def far_first(k):
        step = (k + 1) // 2
        return count // 2 + step * (2 * (k % 2) - 1)

    @pl.loop(0, count - 1)
    def _(k):
        i = far_first(k)
        peer = lax.rem(me + i, count)
        sendbuf[i, 0] = proj[reqs_s[peer, 0, me]]
        sendbuf[i, 1] = proj[reqs_s[peer, 1, me]]

    @pl.loop(0, count - 1)
    def _(k):
        reply(far_first(k)).start()

    recv[me, 0] = proj[reqs_s[me, 0, me]]
    recv[me, 1] = proj[reqs_s[me, 1, me]]

    for load in small[2:]:
        load.wait()
    occ = occ_ref[...].astype(BF16)
    volume[...] = jnp.zeros_like(volume)
    loads[2].wait()
    col = iota((layer_rows, layer_rows), 1)
    line = iota((layer_rows, layer_rows), 0)
    select_own = one_hot(col == (line % slots) * FACE + line // slots)
    spread = one_hot(iota((layer_rows, slots), 0) % slots == iota((layer_rows, slots), 1))
    nb = lax.dot_general(
        spread,
        nb_ref[...].astype(F32).astype(BF16),
        (((1,), (1,)), ((), ())),
        preferred_element_type=F32,
    ).astype(jnp.int32)
    side_rows = EDGE * slots
    scol = iota((side_rows, layer_rows), 1)
    sline = iota((side_rows, 1), 0) // slots

    def side(f, fixed, step):
        wanted = nb[:side_rows, f : f + 1]
        target = jnp.where(wanted >= 0, wanted * FACE + fixed + sline * step, -1)
        return one_hot(scol == target)

    sides = [
        side(2, (EDGE - 1) * EDGE, 1),
        side(3, 0, 1),
        side(4, EDGE - 1, EDGE),
        side(5, 0, EDGE),
    ]
    select = jnp.concatenate([select_own] + sides, axis=0)
    for x in range(EDGE):
        layer = feat[:, x * FACE : (x + 1) * FACE, :].reshape(layer_rows, channels)
        part = jnp.dot(select * layer_occ(occ, x), layer, preferred_element_type=F32).astype(BF16)
        volume[x + 1, 1 : EDGE + 1, 1 : EDGE + 1] = part[:layer_rows].reshape(
            EDGE, EDGE, slots, channels
        )
        faces = part[layer_rows:].reshape(4, EDGE, slots, channels)
        volume[x + 1, 0, 1 : EDGE + 1] = faces[0]
        volume[x + 1, EDGE + 1, 1 : EDGE + 1] = faces[1]
        volume[x + 1, 1 : EDGE + 1, 0] = faces[2]
        volume[x + 1, 1 : EDGE + 1, EDGE + 1] = faces[3]

    @pl.when(me > 0)
    def _():
        pltpu.make_async_remote_copy(
            src_ref=feat_hbm.at[:, pl.ds(0, FACE), :],
            dst_ref=low_layer,
            send_sem=halo_send.at[0],
            recv_sem=halo_recv.at[0],
            device_id={"blk": up},
            device_id_type=MESH,
        ).wait_recv()
        halo(1).wait_recv()

    @pl.when(me < count - 1)
    def _():
        halo(2).wait_recv()
        halo(3).wait_recv()

    def x_face(f, layer_ref, other_occ, x):
        wanted = nb[:, f : f + 1]
        target = jnp.where(wanted >= 0, wanted * FACE + iota((layer_rows, 1), 0) // slots, -1)
        pick = one_hot(col == target) * layer_occ(other_occ[...].astype(BF16), x)
        layer = layer_ref[...].reshape(layer_rows, channels)
        part = jnp.dot(pick, layer, preferred_element_type=F32).astype(BF16)
        return part.reshape(EDGE, EDGE, slots, channels)

    volume[0, 1 : EDGE + 1, 1 : EDGE + 1] = x_face(0, low_layer, low_occ, EDGE - 1)
    volume[EDGE + 1, 1 : EDGE + 1, 1 : EDGE + 1] = x_face(1, high_layer, high_occ, 0)

    loads[3].wait()
    scale = scale_ref[...]
    shift = shift_ref[...]

    @pl.loop(0, EDGE)
    def _(x):
        total = jnp.zeros((layer_rows, channels), F32)
        for tap in range(27):
            a, b, c = tap // 9, (tap // 3) % 3, tap % 3
            window = volume[x + a, b : b + EDGE, c : c + EDGE].reshape(layer_rows, channels)
            total = total + jnp.dot(window, weight[tap], preferred_element_type=F32)
        hidden = jnp.maximum(total * scale + shift, 0.0)
        for k in range(channels // LANES):
            acc[k, pl.ds(x * layer_rows, layer_rows), :] = hidden[:, k * LANES : (k + 1) * LANES]

    @pl.loop(0, slots)
    def _(s):
        mine = jnp.where(iota((VOX, VOX), 0) == iota((VOX, VOX), 1), occ_ref[pl.ds(s, 1), :], 0)
        mask[pl.ds(s * VOX, VOX), :] = jnp.dot(
            mine.astype(BF16), jnp.ones((VOX, channels), BF16), preferred_element_type=F32
        )

    picks = []
    for s in range(slots):
        rank = jnp.int32(0)
        for t in range(s):
            rank = jnp.where(owner_s[t] == owner_s[s], 1, rank)
        picks.append(rank)
        hidden = jnp.concatenate(
            [acc[k, pl.ds(s, VOX, stride=slots), :] for k in range(channels // LANES)],
            axis=1,
        )
        base[s] = hidden * mask[s * VOX : (s + 1) * VOX, :]

    @pl.loop(1, count)
    def _(i):
        reply(i).wait_recv()

    for s in range(slots):
        moved = recv[owner_s[s], picks[s]].astype(F32)
        out_ref[s] = (base[s] + moved * mask[s * VOX : (s + 1) * VOX, :]).astype(BF16)

    @pl.loop(1, count)
    def _(i):
        request(i).wait_send()
        reply(i).wait_send()

    @pl.when(me < count - 1)
    def _():
        halo(0).wait_send()
        halo(1).wait_send()

    @pl.when(me > 0)
    def _():
        halo(2).wait_send()
        halo(3).wait_send()


def merge_full(
    features,
    occupancy,
    neighbors,
    previous,
    old_owner,
    old_slot,
    conv_weight,
    norm_scale,
    norm_shift,
    prev_weight,
):
    slots, vox, channels = features.shape
    count = lax.axis_size("blk")
    hbm = pl.BlockSpec(memory_space=pl.ANY)
    volume_shape = (EDGE + 2, EDGE + 2, EDGE + 2, slots, channels)
    dma = pltpu.SemaphoreType.DMA
    return pl.pallas_call(
        functools.partial(kernel_full, count, slots, channels),
        out_shape=pltpu.VMEM(features.shape, BF16),
        in_specs=[hbm] * 10,
        out_specs=pl.BlockSpec(memory_space=pltpu.VMEM),
        scratch_shapes=[
            pltpu.SMEM((slots,), jnp.int32),
            pltpu.SMEM((slots,), jnp.int32),
            pltpu.VMEM((6, slots), jnp.int32),
            pltpu.VMEM((slots, vox), jnp.int32),
            pltpu.VMEM((1, channels), F32),
            pltpu.VMEM((1, channels), F32),
            pltpu.VMEM(features.shape, BF16),
            pltpu.VMEM(previous.shape, BF16),
            pltpu.VMEM(conv_weight.shape, BF16),
            pltpu.VMEM(prev_weight.shape, BF16),
            pltpu.VMEM(previous.shape, BF16),
            pltpu.VMEM((CAP, LANES), jnp.int32),
            pltpu.VMEM((count, CAP, LANES), jnp.int32),
            pltpu.SMEM((count, CAP, LANES), jnp.int32),
            pltpu.VMEM((count, CAP, vox, channels), BF16),
            pltpu.VMEM((count, CAP, vox, channels), BF16),
            pltpu.VMEM((slots, FACE, channels), BF16),
            pltpu.VMEM((slots, FACE, channels), BF16),
            pltpu.VMEM((slots, vox), jnp.int32),
            pltpu.VMEM((slots, vox), jnp.int32),
            pltpu.VMEM(volume_shape, BF16),
            pltpu.VMEM((channels // LANES, slots * vox, LANES), F32),
            pltpu.VMEM((slots * vox, channels), F32),
            pltpu.VMEM(features.shape, F32),
            dma((6,)),
            dma((6,)),
            dma((4,)),
            dma((4,)),
            dma((count,)),
            dma((count,)),
            dma((count,)),
            dma((count,)),
        ],
        compiler_params=pltpu.CompilerParams(
            collective_id=1, has_side_effects=True, vmem_limit_bytes=66_000_000
        ),
        name="merge_full",
    )(
        old_owner[:, 0],
        old_slot,
        neighbors.T,
        norm_scale[None, :],
        norm_shift[None, :],
        features,
        previous,
        occupancy,
        conv_weight,
        prev_weight,
    )


def kernel(
    count,
    groups,
    slots,
    channels,
    owner_hbm,
    slot_hbm,
    nb_hbm,
    scale_hbm,
    shift_hbm,
    feat_hbm,
    prev_hbm,
    occ_hbm,
    w_hbm,
    pw_hbm,
    out_ref,
    over_ref,
    owner_s,
    slot_s,
    nb_ref,
    occ_ref,
    scale_ref,
    shift_ref,
    feat,
    prev,
    weight,
    pweight,
    proj,
    table,
    near_reqs,
    far_reqs,
    first_s,
    last_s,
    place_s,
    over,
    overs,
    send_first,
    send_row,
    send_z,
    send_x,
    relay_z,
    relay_x,
    relay_out,
    recv,
    low_layer,
    high_layer,
    low_occ,
    high_occ,
    volume,
    acc,
    mask,
    base,
    small_sem,
    local_sem,
    halo_send,
    halo_recv,
    rq_send,
    rq_recv,
    first_send,
    first_recv,
    row_send,
    row_recv,
    z_send,
    z_recv,
    x_send,
    x_recv,
    out_send,
    out_recv,
    late_sem,
    over_send,
    over_recv,
):
    me = lax.axis_index("blk")
    grp = lax.axis_index("grp")
    half, row = count // 2, count // 4
    half_base = me // half * half
    row_base = me // row * row
    half_at, row_at = me - half_base, me - row_base
    other_half = half - half_base
    other_row = 2 * half_base + row - row_base
    across = lax.rem(me + half, count)
    beside = other_row + row_at
    row_part, z_part, x_part = count, count + row, count + row + EXTRA
    layer_rows = FACE * slots
    barrier = pltpu.get_barrier_semaphore()

    upper = half_base > 0
    last_row = count - row
    late = me >= last_row

    def hello(peer):
        pl.semaphore_signal(barrier, inc=1, device_id={"blk": peer}, device_id_type=MESH)

    @pl.when(jnp.logical_not(late))
    def _():
        @pl.loop(1, count)
        def _(i):
            hello(lax.rem(me + i, count))

    @pl.when(late)
    def _():
        @pl.loop(1, row)
        def _(i):
            hello(row_base + lax.rem(row_at + i, row))

    for i in range(1, groups):
        there = lax.rem(grp + i, groups)
        pl.semaphore_signal(barrier, inc=1, device_id={"grp": there}, device_id_type=MESH)

    small = [
        pltpu.make_async_copy(owner_hbm, owner_s, small_sem.at[0]),
        pltpu.make_async_copy(slot_hbm, slot_s, small_sem.at[1]),
        pltpu.make_async_copy(occ_hbm, occ_ref, small_sem.at[2]),
        pltpu.make_async_copy(nb_hbm, nb_ref, small_sem.at[3]),
        pltpu.make_async_copy(scale_hbm, scale_ref, small_sem.at[4]),
        pltpu.make_async_copy(shift_hbm, shift_ref, small_sem.at[5]),
    ]
    for load in small:
        load.start()
    loads = [
        pltpu.make_async_copy(prev_hbm, prev, local_sem.at[0]),
        pltpu.make_async_copy(pw_hbm, pweight, local_sem.at[1]),
        pltpu.make_async_copy(feat_hbm, feat, local_sem.at[2]),
        pltpu.make_async_copy(w_hbm, weight, local_sem.at[3]),
    ]
    for load in loads:
        load.start()

    small[0].wait()
    small[1].wait()

    lane = iota((1, LANES), 1)
    first = jnp.zeros((1, LANES), jnp.int32)
    last = jnp.zeros((1, LANES), jnp.int32)
    for s in range(slots):
        last = jnp.where(lane == owner_s[s], slot_s[s], last)
        t = slots - 1 - s
        first = jnp.where(lane == owner_s[t], slot_s[t], first)
    zero = jnp.int32(0)
    x_count, z_count = zero, zero
    x_owner, z_owner = [zero] * EXTRA, [zero] * EXTRA
    for s in range(slots):
        owner = owner_s[s]
        again = zero
        for t in range(s):
            again = jnp.where(owner_s[t] == owner, 1, again)
        far = jnp.where((owner < half_base) | (owner >= half_base + half), again, 0)
        near = jnp.where((owner >= other_row) & (owner < other_row + row), again, 0)
        for e in range(EXTRA):
            x_owner[e] = jnp.where((far == 1) & (x_count == e), owner - other_half, x_owner[e])
            z_owner[e] = jnp.where((near == 1) & (z_count == e), owner - other_row, z_owner[e])
        at = jnp.where(again == 1, row_part + owner - row_base, owner)
        at = jnp.where(near == 1, z_part + jnp.minimum(z_count, EXTRA - 1), at)
        place_s[s] = jnp.where(far == 1, x_part + jnp.minimum(x_count, EXTRA - 1), at)
        x_count = x_count + far
        z_count = z_count + near
    notes = jnp.where(
        lane == count + 2 * EXTRA, jnp.where((x_count > EXTRA) | (z_count > EXTRA), 1, 0), first + last * PACK
    )
    for e in range(EXTRA):
        notes = jnp.where(lane == count + e, x_owner[e], notes)
        notes = jnp.where(lane == count + EXTRA + e, z_owner[e], notes)
    table[...] = notes

    def layer_occ(occ, x):
        spread = one_hot(iota((VOX, layer_rows), 0) == x * FACE + iota((VOX, layer_rows), 1) % FACE)
        rows = jnp.dot(occ, spread, preferred_element_type=F32)
        own = iota((slots, layer_rows), 0) == iota((slots, layer_rows), 1) // FACE
        return jnp.sum(jnp.where(own, rows, 0.0), axis=0, keepdims=True).astype(BF16)

    @pl.when(jnp.logical_not(late))
    def _():
        pl.semaphore_wait(barrier, count - row + groups - 2)

    @pl.when(late)
    def _():
        pl.semaphore_wait(barrier, count + groups - 2)

        @pl.loop(0, last_row)
        def _(i):
            pl.semaphore_signal(late_sem, inc=1, device_id={"blk": i}, device_id_type=MESH)

    def in_row(i):
        return row_base + lax.rem(row_at + i, row)

    def request(at, far):
        return pltpu.make_async_remote_copy(
            src_ref=table,
            dst_ref=(far_reqs if far else near_reqs).at[half_at],
            send_sem=rq_send.at[far * half + at],
            recv_sem=rq_recv.at[far * half + half_at],
            device_id={"blk": (other_half if far else half_base) + at},
            device_id_type=MESH,
        )

    def request_from(at, far):
        return pltpu.make_async_remote_copy(
            src_ref=table,
            dst_ref=(far_reqs if far else near_reqs).at[at],
            send_sem=rq_send.at[far * half + at],
            recv_sem=rq_recv.at[far * half + at],
            device_id={"blk": (other_half if far else half_base) + at},
            device_id_type=MESH,
        )

    def turned(part, i):
        return part * row + lax.rem(row_at + i, row)

    def request_row(part, far):
        @pl.loop(0, row)
        def _(i):
            at = turned(part, i)
            if far:
                request(at, far).start()
            else:

                @pl.when(at != half_at)
                def _():
                    request(at, far).start()

    request_row(0, 1)

    @pl.when(upper)
    def _():
        request_row(1, 1)

    request_row(0, 0)

    @pl.when(jnp.logical_not(upper) | late)
    def _():
        request_row(1, 0)

    up = lax.rem(me + 1, count)
    down = lax.rem(me + count - 1, count)

    def halo(k):
        if k < 2:
            src = feat_hbm.at[:, pl.ds((EDGE - 1) * FACE, FACE), :] if k == 0 else occ_hbm
            dst = low_layer if k == 0 else low_occ
            peer = up
        else:
            src = feat_hbm.at[:, pl.ds(0, FACE), :] if k == 2 else occ_hbm
            dst = high_layer if k == 2 else high_occ
            peer = down
        return pltpu.make_async_remote_copy(
            src_ref=src,
            dst_ref=dst,
            send_sem=halo_send.at[k],
            recv_sem=halo_recv.at[k],
            device_id={"blk": peer},
            device_id_type=MESH,
        )

    edge = me == last_row - 1

    @pl.when((me < count - 1) & jnp.logical_not(edge))
    def _():
        halo(0).start()
        halo(1).start()

    @pl.when(me > 0)
    def _():
        halo(2).start()
        halo(3).start()

    @pl.when(jnp.logical_not(late))
    def _():
        pl.semaphore_wait(late_sem, row)

    @pl.when(jnp.logical_not(upper))
    def _():
        request_row(1, 1)

    @pl.when(upper & jnp.logical_not(late))
    def _():
        request_row(1, 0)

    @pl.when(edge)
    def _():
        halo(0).start()
        halo(1).start()

    @pl.when(me == 0)
    def _():
        low_layer[...] = jnp.zeros_like(low_layer)
        low_occ[...] = jnp.zeros_like(low_occ)

    @pl.when(me == count - 1)
    def _():
        high_layer[...] = jnp.zeros_like(high_layer)
        high_occ[...] = jnp.zeros_like(high_occ)

    loads[0].wait()
    loads[1].wait()

    blocks = layer_rows // VOX
    for s in range(0, slots, blocks):
        rows = prev[s : s + blocks].reshape(layer_rows, channels)
        part = jnp.dot(rows, pweight[...], preferred_element_type=F32).astype(BF16)
        proj[s : s + blocks] = part.reshape(blocks, VOX, channels)

    near_reqs[half_at] = table[...]

    def first_to(at, far):
        return pltpu.make_async_remote_copy(
            src_ref=send_first.at[far * half + at],
            dst_ref=recv.at[me],
            send_sem=first_send.at[far * half + at],
            recv_sem=first_recv.at[far * half + half_at],
            device_id={"blk": (other_half if far else half_base) + at},
            device_id_type=MESH,
        )

    def first_from(at, far):
        return pltpu.make_async_remote_copy(
            src_ref=send_first.at[far * half + at],
            dst_ref=recv.at[(other_half if far else half_base) + at],
            send_sem=first_send.at[far * half + at],
            recv_sem=first_recv.at[far * half + at],
            device_id={"blk": (other_half if far else half_base) + at},
            device_id_type=MESH,
        )

    def row_to(i):
        return pltpu.make_async_remote_copy(
            src_ref=send_row.at[i],
            dst_ref=recv.at[row_part + row_at],
            send_sem=row_send.at[i],
            recv_sem=row_recv.at[i],
            device_id={"blk": in_row(i)},
            device_id_type=MESH,
        )

    def z_to(i):
        return pltpu.make_async_remote_copy(
            src_ref=send_z.at[i],
            dst_ref=relay_z.at[row_at],
            send_sem=z_send.at[i],
            recv_sem=z_recv.at[i],
            device_id={"blk": in_row(i)},
            device_id_type=MESH,
        )

    def x_to(at):
        return pltpu.make_async_remote_copy(
            src_ref=send_x.at[at],
            dst_ref=relay_x.at[half_at],
            send_sem=x_send.at[at],
            recv_sem=x_recv.at[half_at],
            device_id={"blk": half_base + at},
            device_id_type=MESH,
        )

    def x_from(at):
        return pltpu.make_async_remote_copy(
            src_ref=send_x.at[at],
            dst_ref=relay_x.at[at],
            send_sem=x_send.at[at],
            recv_sem=x_recv.at[at],
            device_id={"blk": half_base + at},
            device_id_type=MESH,
        )

    def relay(k):
        part, peer = ((x_part, across), (z_part, beside))[k]
        return pltpu.make_async_remote_copy(
            src_ref=relay_out.at[pl.ds(k * EXTRA, EXTRA)],
            dst_ref=recv.at[pl.ds(part, EXTRA)],
            send_sem=out_send.at[k],
            recv_sem=out_recv.at[k],
            device_id={"blk": peer},
            device_id_type=MESH,
        )

    def over_to(i):
        return pltpu.make_async_remote_copy(
            src_ref=over,
            dst_ref=overs.at[grp],
            send_sem=over_send.at[i],
            recv_sem=over_recv.at[i],
            device_id={"grp": lax.rem(grp + i, groups)},
            device_id_type=MESH,
        )

    def near_entry(peer, at):
        return jnp.sum(jnp.where(lane == at, near_reqs[peer - half_base], 0))

    def far_entry(peer, at):
        return jnp.sum(jnp.where(lane == at, far_reqs[peer - other_half], 0))

    def send_far(at):
        send_first[half + at] = proj[first_s[other_half + at]]
        first_to(at, 1).start()

    def send_across(at):
        send_x[at] = proj[last_s[other_half + at]]
        x_to(at).start()

    def send_near(at):
        send_first[at] = proj[first_s[half_base + at]]
        first_to(at, 0).start()

    def send_beside(i):
        send_z[i] = proj[last_s[other_row + lax.rem(row_at + i, row)]]
        z_to(i).start()

    def send_second(i):
        send_row[i] = proj[last_s[in_row(i)]]
        row_to(i).start()

    def others(body):
        @pl.loop(1, half)
        def _(i):
            body(lax.rem(half_at + i, half))

    for part in range(2):

        @pl.loop(0, row)
        def _(i):
            request_from(part * row + i, 1).wait_recv()

        for i in range(row):
            d = part * row + i
            wanted = far_entry(other_half + d, me)
            first_s[other_half + d] = wanted % PACK
            last_s[other_half + d] = wanted // PACK

        @pl.loop(0, row // 2)
        def _(i):
            send_far(turned(part, i))

        @pl.loop(0, row)
        def _(i):
            at = turned(part, i)

            @pl.when(at != half_at)
            def _():
                send_across(at)

        @pl.loop(row // 2, row)
        def _(i):
            send_far(turned(part, i))

    others(lambda at: request_from(at, 0).wait_recv())

    for d in range(half):
        wanted = near_entry(half_base + d, me)
        first_s[half_base + d] = wanted % PACK
        last_s[half_base + d] = wanted // PACK

    @pl.loop(1, row)
    def _(i):
        send_beside(i)

    others(send_near)

    @pl.loop(1, row)
    def _(i):
        send_second(i)

    recv[me] = proj[first_s[me]]
    recv[row_part + row_at] = proj[last_s[me]]
    relay_x[half_at] = proj[last_s[across]]
    relay_z[row_at] = proj[last_s[beside]]

    notes = near_reqs[...].reshape(half, LANES) + far_reqs[...].reshape(half, LANES)
    over[...] = jnp.sum(jnp.where(lane == count + 2 * EXTRA, notes, 0), axis=0, keepdims=True)
    for i in range(1, groups):
        over_to(i).start()

    for load in small[2:]:
        load.wait()
    occ = occ_ref[...].astype(BF16)
    volume[...] = jnp.zeros_like(volume)
    loads[2].wait()
    col = iota((layer_rows, layer_rows), 1)
    line = iota((layer_rows, layer_rows), 0)
    select_own = one_hot(col == (line % slots) * FACE + line // slots)
    spread = one_hot(iota((layer_rows, slots), 0) % slots == iota((layer_rows, slots), 1))
    nb = lax.dot_general(
        spread,
        nb_ref[...].astype(F32).astype(BF16),
        (((1,), (1,)), ((), ())),
        preferred_element_type=F32,
    ).astype(jnp.int32)
    side_rows = EDGE * slots
    scol = iota((side_rows, layer_rows), 1)
    sline = iota((side_rows, 1), 0) // slots

    def side(f, fixed, step):
        wanted = nb[:side_rows, f : f + 1]
        target = jnp.where(wanted >= 0, wanted * FACE + fixed + sline * step, -1)
        return one_hot(scol == target)

    sides = [
        side(2, (EDGE - 1) * EDGE, 1),
        side(3, 0, 1),
        side(4, EDGE - 1, EDGE),
        side(5, 0, EDGE),
    ]
    select = jnp.concatenate([select_own] + sides, axis=0)
    for x in range(EDGE):
        layer = feat[:, x * FACE : (x + 1) * FACE, :].reshape(layer_rows, channels)
        part = jnp.dot(select * layer_occ(occ, x), layer, preferred_element_type=F32).astype(BF16)
        volume[x + 1, 1 : EDGE + 1, 1 : EDGE + 1] = part[:layer_rows].reshape(
            EDGE, EDGE, slots, channels
        )
        faces = part[layer_rows:].reshape(4, EDGE, slots, channels)
        volume[x + 1, 0, 1 : EDGE + 1] = faces[0]
        volume[x + 1, EDGE + 1, 1 : EDGE + 1] = faces[1]
        volume[x + 1, 1 : EDGE + 1, 0] = faces[2]
        volume[x + 1, 1 : EDGE + 1, EDGE + 1] = faces[3]

    @pl.when(me > 0)
    def _():
        pltpu.make_async_remote_copy(
            src_ref=feat_hbm.at[:, pl.ds(0, FACE), :],
            dst_ref=low_layer,
            send_sem=halo_send.at[0],
            recv_sem=halo_recv.at[0],
            device_id={"blk": up},
            device_id_type=MESH,
        ).wait_recv()
        halo(1).wait_recv()

    @pl.when(me < count - 1)
    def _():
        halo(2).wait_recv()
        halo(3).wait_recv()

    def x_face(f, layer_ref, other_occ, x):
        wanted = nb[:, f : f + 1]
        target = jnp.where(wanted >= 0, wanted * FACE + iota((layer_rows, 1), 0) // slots, -1)
        pick = one_hot(col == target) * layer_occ(other_occ[...].astype(BF16), x)
        layer = layer_ref[...].reshape(layer_rows, channels)
        part = jnp.dot(pick, layer, preferred_element_type=F32).astype(BF16)
        return part.reshape(EDGE, EDGE, slots, channels)

    volume[0, 1 : EDGE + 1, 1 : EDGE + 1] = x_face(0, low_layer, low_occ, EDGE - 1)
    volume[EDGE + 1, 1 : EDGE + 1, 1 : EDGE + 1] = x_face(1, high_layer, high_occ, 0)

    loads[3].wait()
    scale = scale_ref[...]
    shift = shift_ref[...]

    @pl.loop(0, 1)
    def _(x):
        total = jnp.zeros((layer_rows, channels), F32)
        for tap in range(27):
            a, b, c = tap // 9, (tap // 3) % 3, tap % 3
            window = volume[x + a, b : b + EDGE, c : c + EDGE].reshape(layer_rows, channels)
            total = total + jnp.dot(window, weight[tap], preferred_element_type=F32)
        hidden = jnp.maximum(total * scale + shift, 0.0)
        for k in range(channels // LANES):
            acc[k, pl.ds(x * layer_rows, layer_rows), :] = hidden[:, k * LANES : (k + 1) * LANES]

    others(lambda at: x_from(at).wait_recv())

    @pl.loop(1, row)
    def _(i):
        z_to(i).wait_recv()

    for e in range(EXTRA):
        relay_out[e] = relay_x[far_entry(across, count + e)]
        relay_out[EXTRA + e] = relay_z[near_entry(beside, count + EXTRA + e)]
    relay(0).start()
    relay(1).start()

    @pl.loop(1, EDGE)
    def _(x):
        total = jnp.zeros((layer_rows, channels), F32)
        for tap in range(27):
            a, b, c = tap // 9, (tap // 3) % 3, tap % 3
            window = volume[x + a, b : b + EDGE, c : c + EDGE].reshape(layer_rows, channels)
            total = total + jnp.dot(window, weight[tap], preferred_element_type=F32)
        hidden = jnp.maximum(total * scale + shift, 0.0)
        for k in range(channels // LANES):
            acc[k, pl.ds(x * layer_rows, layer_rows), :] = hidden[:, k * LANES : (k + 1) * LANES]

    @pl.loop(0, slots)
    def _(s):
        mine = jnp.where(iota((VOX, VOX), 0) == iota((VOX, VOX), 1), occ_ref[pl.ds(s, 1), :], 0)
        mask[pl.ds(s * VOX, VOX), :] = jnp.dot(
            mine.astype(BF16), jnp.ones((VOX, channels), BF16), preferred_element_type=F32
        )

    for s in range(slots):
        hidden = jnp.concatenate(
            [acc[k, pl.ds(s, VOX, stride=slots), :] for k in range(channels // LANES)],
            axis=1,
        )
        base[s] = hidden * mask[s * VOX : (s + 1) * VOX, :]

    overs[grp] = over[...]
    for i in range(1, groups):
        over_to(i).wait_recv()
    over_ref[0] = jnp.sum(overs[...])

    @pl.loop(0, half)
    def _(i):
        request(i, 1).wait_send()
        first_to(i, 1).wait_send()

    others(lambda at: request(at, 0).wait_send())
    others(lambda at: first_to(at, 0).wait_send())

    others(lambda at: x_to(at).wait_send())

    @pl.loop(1, row)
    def _(i):
        row_to(i).wait_send()
        z_to(i).wait_send()

    relay(0).wait_send()
    relay(1).wait_send()
    for i in range(1, groups):
        over_to(i).wait_send()

    @pl.when(me < count - 1)
    def _():
        halo(0).wait_send()
        halo(1).wait_send()

    @pl.when(me > 0)
    def _():
        halo(2).wait_send()
        halo(3).wait_send()

    @pl.loop(0, half)
    def _(i):
        first_from(i, 1).wait_recv()

    others(lambda at: first_from(at, 0).wait_recv())

    @pl.loop(1, row)
    def _(i):
        row_to(i).wait_recv()

    relay(0).wait_recv()
    relay(1).wait_recv()

    for s in range(slots):
        moved = recv[place_s[s]].astype(F32)
        out_ref[s] = (base[s] + moved * mask[s * VOX : (s + 1) * VOX, :]).astype(BF16)


def per_device(
    features,
    occupancy,
    neighbors,
    previous,
    old_owner,
    old_slot,
    conv_weight,
    norm_scale,
    norm_shift,
    prev_weight,
):
    slots, vox, channels = features.shape
    count = lax.axis_size("blk")
    groups = lax.axis_size("grp")
    half, row = count // 2, count // 4
    hbm = pl.BlockSpec(memory_space=pl.ANY)
    volume_shape = (EDGE + 2, EDGE + 2, EDGE + 2, slots, channels)
    dma = pltpu.SemaphoreType.DMA
    return pl.pallas_call(
        functools.partial(kernel, count, groups, slots, channels),
        out_shape=[
            pltpu.VMEM(features.shape, BF16),
            pltpu.SMEM((1,), jnp.int32),
        ],
        in_specs=[hbm] * 10,
        out_specs=[
            pl.BlockSpec(memory_space=pltpu.VMEM),
            pl.BlockSpec(memory_space=pltpu.SMEM),
        ],
        scratch_shapes=[
            pltpu.SMEM((slots,), jnp.int32),
            pltpu.SMEM((slots,), jnp.int32),
            pltpu.VMEM((6, slots), jnp.int32),
            pltpu.VMEM((slots, vox), jnp.int32),
            pltpu.VMEM((1, channels), F32),
            pltpu.VMEM((1, channels), F32),
            pltpu.VMEM(features.shape, BF16),
            pltpu.VMEM(previous.shape, BF16),
            pltpu.VMEM(conv_weight.shape, BF16),
            pltpu.VMEM(prev_weight.shape, BF16),
            pltpu.VMEM(previous.shape, BF16),
            pltpu.VMEM((1, LANES), jnp.int32),
            pltpu.VMEM((half, 1, LANES), jnp.int32),
            pltpu.VMEM((half, 1, LANES), jnp.int32),
            pltpu.SMEM((count,), jnp.int32),
            pltpu.SMEM((count,), jnp.int32),
            pltpu.SMEM((slots,), jnp.int32),
            pltpu.VMEM((1, LANES), jnp.int32),
            pltpu.VMEM((groups, 1, LANES), jnp.int32),
            pltpu.VMEM((count, vox, channels), BF16),
            pltpu.VMEM((row, vox, channels), BF16),
            pltpu.VMEM((row, vox, channels), BF16),
            pltpu.VMEM((half, vox, channels), BF16),
            pltpu.VMEM((row, vox, channels), BF16),
            pltpu.VMEM((half, vox, channels), BF16),
            pltpu.VMEM((2 * EXTRA, vox, channels), BF16),
            pltpu.VMEM((count + row + 2 * EXTRA, vox, channels), BF16),
            pltpu.VMEM((slots, FACE, channels), BF16),
            pltpu.VMEM((slots, FACE, channels), BF16),
            pltpu.VMEM((slots, vox), jnp.int32),
            pltpu.VMEM((slots, vox), jnp.int32),
            pltpu.VMEM(volume_shape, BF16),
            pltpu.VMEM((channels // LANES, slots * vox, LANES), F32),
            pltpu.VMEM((slots * vox, channels), F32),
            pltpu.VMEM(features.shape, F32),
            dma((6,)),
            dma((6,)),
            dma((4,)),
            dma((4,)),
            dma((count,)),
            dma((count,)),
            dma((count,)),
            dma((count,)),
            dma((row,)),
            dma((row,)),
            dma((row,)),
            dma((row,)),
            dma((half,)),
            dma((half,)),
            dma((2,)),
            dma((2,)),
            pltpu.SemaphoreType.REGULAR,
            dma((groups,)),
            dma((groups,)),
        ],
        compiler_params=pltpu.CompilerParams(
            collective_id=0, has_side_effects=True, vmem_limit_bytes=66_000_000
        ),
        name="merge_blocks",
    )(
        old_owner[:, 0],
        old_slot,
        neighbors.T,
        norm_scale[None, :],
        norm_shift[None, :],
        features,
        previous,
        occupancy,
        conv_weight,
        prev_weight,
    )


def merge(*arrays):
    merged, over = per_device(*arrays)
    return lax.switch(over[0], [lambda: merged, lambda: merge_full(*arrays)])


def solution(mesh):
    in_specs = (
        P(("grp", "blk"), None, None),
        P(("grp", "blk"), None),
        P(("grp", "blk"), None),
        P(("grp", "blk"), None, None),
        P(("grp", "blk"), None),
        P(("grp", "blk")),
        P(),
        P(),
        P(),
        P(),
    )
    out_specs = P(("grp", "blk"), None, None)
    return jax.shard_map(
        merge, mesh=mesh, in_specs=in_specs, out_specs=out_specs, check_vma=False
    )
```

```python
import functools

import jax
import jax.numpy as jnp
from jax import lax
from jax.experimental import pallas as pl
from jax.experimental.pallas import tpu as pltpu
from jax.sharding import PartitionSpec as P

EDGE = 4
FACE = EDGE * EDGE
VOX = EDGE * FACE
CAP = 2
LANES = 128
EXTRA = 2
PACK = 1 << 16
MESH = pl.DeviceIdType.MESH
F32 = jnp.float32
BF16 = jnp.bfloat16


def iota(shape, dim):
    return lax.broadcasted_iota(jnp.int32, shape, dim)


def one_hot(hit):
    return jnp.where(hit, 1.0, 0.0).astype(BF16)


def kernel_full(
    count,
    slots,
    channels,
    owner_hbm,
    slot_hbm,
    nb_hbm,
    scale_hbm,
    shift_hbm,
    feat_hbm,
    prev_hbm,
    occ_hbm,
    w_hbm,
    pw_hbm,
    out_ref,
    owner_s,
    slot_s,
    nb_ref,
    occ_ref,
    scale_ref,
    shift_ref,
    feat,
    prev,
    weight,
    pweight,
    proj,
    table,
    reqs,
    reqs_s,
    sendbuf,
    recv,
    low_layer,
    high_layer,
    low_occ,
    high_occ,
    volume,
    acc,
    mask,
    base,
    small_sem,
    local_sem,
    halo_send,
    halo_recv,
    rq_send,
    rq_recv,
    rp_send,
    rp_recv,
):
    me = lax.axis_index("blk")
    layer_rows = FACE * slots
    barrier = pltpu.get_barrier_semaphore()

    @pl.loop(1, count)
    def _(i):
        peer = lax.rem(me + i, count)
        pl.semaphore_signal(barrier, inc=1, device_id={"blk": peer}, device_id_type=MESH)

    small = [
        pltpu.make_async_copy(owner_hbm, owner_s, small_sem.at[0]),
        pltpu.make_async_copy(slot_hbm, slot_s, small_sem.at[1]),
        pltpu.make_async_copy(occ_hbm, occ_ref, small_sem.at[2]),
        pltpu.make_async_copy(nb_hbm, nb_ref, small_sem.at[3]),
        pltpu.make_async_copy(scale_hbm, scale_ref, small_sem.at[4]),
        pltpu.make_async_copy(shift_hbm, shift_ref, small_sem.at[5]),
    ]
    for load in small:
        load.start()
    loads = [
        pltpu.make_async_copy(prev_hbm, prev, local_sem.at[0]),
        pltpu.make_async_copy(pw_hbm, pweight, local_sem.at[1]),
        pltpu.make_async_copy(feat_hbm, feat, local_sem.at[2]),
        pltpu.make_async_copy(w_hbm, weight, local_sem.at[3]),
    ]
    for load in loads:
        load.start()

    small[0].wait()
    small[1].wait()

    lane = iota((1, LANES), 1)
    first = jnp.zeros((1, LANES), jnp.int32)
    last = jnp.zeros((1, LANES), jnp.int32)
    for s in range(slots):
        last = jnp.where(lane == owner_s[s], slot_s[s], last)
        t = slots - 1 - s
        first = jnp.where(lane == owner_s[t], slot_s[t], first)
    row = iota((CAP, LANES), 0)
    table[...] = jnp.where(row == 0, first, last)

    def layer_occ(occ, x):
        spread = one_hot(iota((VOX, layer_rows), 0) == x * FACE + iota((VOX, layer_rows), 1) % FACE)
        rows = jnp.dot(occ, spread, preferred_element_type=F32)
        own = iota((slots, layer_rows), 0) == iota((slots, layer_rows), 1) // FACE
        return jnp.sum(jnp.where(own, rows, 0.0), axis=0, keepdims=True).astype(BF16)

    pl.semaphore_wait(barrier, count - 1)

    def request(i):
        return pltpu.make_async_remote_copy(
            src_ref=table,
            dst_ref=reqs.at[me],
            send_sem=rq_send.at[i],
            recv_sem=rq_recv.at[i],
            device_id={"blk": lax.rem(me + i, count)},
            device_id_type=MESH,
        )

    @pl.loop(1, count)
    def _(i):
        request(i).start()

    up = lax.rem(me + 1, count)
    down = lax.rem(me + count - 1, count)

    def halo(k):
        if k < 2:
            src = feat_hbm.at[:, pl.ds((EDGE - 1) * FACE, FACE), :] if k == 0 else occ_hbm
            dst = low_layer if k == 0 else low_occ
            peer = up
        else:
            src = feat_hbm.at[:, pl.ds(0, FACE), :] if k == 2 else occ_hbm
            dst = high_layer if k == 2 else high_occ
            peer = down
        return pltpu.make_async_remote_copy(
            src_ref=src,
            dst_ref=dst,
            send_sem=halo_send.at[k],
            recv_sem=halo_recv.at[k],
            device_id={"blk": peer},
            device_id_type=MESH,
        )

    @pl.when(me < count - 1)
    def _():
        halo(0).start()
        halo(1).start()

    @pl.when(me > 0)
    def _():
        halo(2).start()
        halo(3).start()

    @pl.when(me == 0)
    def _():
        low_layer[...] = jnp.zeros_like(low_layer)
        low_occ[...] = jnp.zeros_like(low_occ)

    @pl.when(me == count - 1)
    def _():
        high_layer[...] = jnp.zeros_like(high_layer)
        high_occ[...] = jnp.zeros_like(high_occ)

    loads[0].wait()
    loads[1].wait()

    blocks = layer_rows // VOX
    for s in range(0, slots, blocks):
        rows = prev[s : s + blocks].reshape(layer_rows, channels)
        part = jnp.dot(rows, pweight[...], preferred_element_type=F32).astype(BF16)
        proj[s : s + blocks] = part.reshape(blocks, VOX, channels)

    reqs_s_copy = pltpu.make_async_copy(reqs, reqs_s, local_sem.at[4])

    def reply(i):
        return pltpu.make_async_remote_copy(
            src_ref=sendbuf.at[i],
            dst_ref=recv.at[me],
            send_sem=rp_send.at[i],
            recv_sem=rp_recv.at[i],
            device_id={"blk": lax.rem(me + i, count)},
            device_id_type=MESH,
        )

    reqs[me] = table[...]

    @pl.loop(1, count)
    def _(i):
        request(i).wait_recv()

    reqs_s_copy.start()
    reqs_s_copy.wait()

    def far_first(k):
        step = (k + 1) // 2
        return count // 2 + step * (2 * (k % 2) - 1)

    @pl.loop(0, count - 1)
    def _(k):
        i = far_first(k)
        peer = lax.rem(me + i, count)
        sendbuf[i, 0] = proj[reqs_s[peer, 0, me]]
        sendbuf[i, 1] = proj[reqs_s[peer, 1, me]]

    @pl.loop(0, count - 1)
    def _(k):
        reply(far_first(k)).start()

    recv[me, 0] = proj[reqs_s[me, 0, me]]
    recv[me, 1] = proj[reqs_s[me, 1, me]]

    for load in small[2:]:
        load.wait()
    occ = occ_ref[...].astype(BF16)
    volume[...] = jnp.zeros_like(volume)
    loads[2].wait()
    col = iota((layer_rows, layer_rows), 1)
    line = iota((layer_rows, layer_rows), 0)
    select_own = one_hot(col == (line % slots) * FACE + line // slots)
    spread = one_hot(iota((layer_rows, slots), 0) % slots == iota((layer_rows, slots), 1))
    nb = lax.dot_general(
        spread,
        nb_ref[...].astype(F32).astype(BF16),
        (((1,), (1,)), ((), ())),
        preferred_element_type=F32,
    ).astype(jnp.int32)
    side_rows = EDGE * slots
    scol = iota((side_rows, layer_rows), 1)
    sline = iota((side_rows, 1), 0) // slots

    def side(f, fixed, step):
        wanted = nb[:side_rows, f : f + 1]
        target = jnp.where(wanted >= 0, wanted * FACE + fixed + sline * step, -1)
        return one_hot(scol == target)

    sides = [
        side(2, (EDGE - 1) * EDGE, 1),
        side(3, 0, 1),
        side(4, EDGE - 1, EDGE),
        side(5, 0, EDGE),
    ]
    select = jnp.concatenate([select_own] + sides, axis=0)
    for x in range(EDGE):
        layer = feat[:, x * FACE : (x + 1) * FACE, :].reshape(layer_rows, channels)
        part = jnp.dot(select * layer_occ(occ, x), layer, preferred_element_type=F32).astype(BF16)
        volume[x + 1, 1 : EDGE + 1, 1 : EDGE + 1] = part[:layer_rows].reshape(
            EDGE, EDGE, slots, channels
        )
        faces = part[layer_rows:].reshape(4, EDGE, slots, channels)
        volume[x + 1, 0, 1 : EDGE + 1] = faces[0]
        volume[x + 1, EDGE + 1, 1 : EDGE + 1] = faces[1]
        volume[x + 1, 1 : EDGE + 1, 0] = faces[2]
        volume[x + 1, 1 : EDGE + 1, EDGE + 1] = faces[3]

    @pl.when(me > 0)
    def _():
        pltpu.make_async_remote_copy(
            src_ref=feat_hbm.at[:, pl.ds(0, FACE), :],
            dst_ref=low_layer,
            send_sem=halo_send.at[0],
            recv_sem=halo_recv.at[0],
            device_id={"blk": up},
            device_id_type=MESH,
        ).wait_recv()
        halo(1).wait_recv()

    @pl.when(me < count - 1)
    def _():
        halo(2).wait_recv()
        halo(3).wait_recv()

    def x_face(f, layer_ref, other_occ, x):
        wanted = nb[:, f : f + 1]
        target = jnp.where(wanted >= 0, wanted * FACE + iota((layer_rows, 1), 0) // slots, -1)
        pick = one_hot(col == target) * layer_occ(other_occ[...].astype(BF16), x)
        layer = layer_ref[...].reshape(layer_rows, channels)
        part = jnp.dot(pick, layer, preferred_element_type=F32).astype(BF16)
        return part.reshape(EDGE, EDGE, slots, channels)

    volume[0, 1 : EDGE + 1, 1 : EDGE + 1] = x_face(0, low_layer, low_occ, EDGE - 1)
    volume[EDGE + 1, 1 : EDGE + 1, 1 : EDGE + 1] = x_face(1, high_layer, high_occ, 0)

    loads[3].wait()
    scale = scale_ref[...]
    shift = shift_ref[...]

    @pl.loop(0, EDGE)
    def _(x):
        total = jnp.zeros((layer_rows, channels), F32)
        for tap in range(27):
            a, b, c = tap // 9, (tap // 3) % 3, tap % 3
            window = volume[x + a, b : b + EDGE, c : c + EDGE].reshape(layer_rows, channels)
            total = total + jnp.dot(window, weight[tap], preferred_element_type=F32)
        hidden = jnp.maximum(total * scale + shift, 0.0)
        for k in range(channels // LANES):
            acc[k, pl.ds(x * layer_rows, layer_rows), :] = hidden[:, k * LANES : (k + 1) * LANES]

    @pl.loop(0, slots)
    def _(s):
        mine = jnp.where(iota((VOX, VOX), 0) == iota((VOX, VOX), 1), occ_ref[pl.ds(s, 1), :], 0)
        mask[pl.ds(s * VOX, VOX), :] = jnp.dot(
            mine.astype(BF16), jnp.ones((VOX, channels), BF16), preferred_element_type=F32
        )

    picks = []
    for s in range(slots):
        rank = jnp.int32(0)
        for t in range(s):
            rank = jnp.where(owner_s[t] == owner_s[s], 1, rank)
        picks.append(rank)
        hidden = jnp.concatenate(
            [acc[k, pl.ds(s, VOX, stride=slots), :] for k in range(channels // LANES)],
            axis=1,
        )
        base[s] = hidden * mask[s * VOX : (s + 1) * VOX, :]

    @pl.loop(1, count)
    def _(i):
        reply(i).wait_recv()

    for s in range(slots):
        moved = recv[owner_s[s], picks[s]].astype(F32)
        out_ref[s] = (base[s] + moved * mask[s * VOX : (s + 1) * VOX, :]).astype(BF16)

    @pl.loop(1, count)
    def _(i):
        request(i).wait_send()
        reply(i).wait_send()

    @pl.when(me < count - 1)
    def _():
        halo(0).wait_send()
        halo(1).wait_send()

    @pl.when(me > 0)
    def _():
        halo(2).wait_send()
        halo(3).wait_send()


def merge_full(
    features,
    occupancy,
    neighbors,
    previous,
    old_owner,
    old_slot,
    conv_weight,
    norm_scale,
    norm_shift,
    prev_weight,
):
    slots, vox, channels = features.shape
    count = lax.axis_size("blk")
    hbm = pl.BlockSpec(memory_space=pl.ANY)
    volume_shape = (EDGE + 2, EDGE + 2, EDGE + 2, slots, channels)
    dma = pltpu.SemaphoreType.DMA
    return pl.pallas_call(
        functools.partial(kernel_full, count, slots, channels),
        out_shape=pltpu.VMEM(features.shape, BF16),
        in_specs=[hbm] * 10,
        out_specs=pl.BlockSpec(memory_space=pltpu.VMEM),
        scratch_shapes=[
            pltpu.SMEM((slots,), jnp.int32),
            pltpu.SMEM((slots,), jnp.int32),
            pltpu.VMEM((6, slots), jnp.int32),
            pltpu.VMEM((slots, vox), jnp.int32),
            pltpu.VMEM((1, channels), F32),
            pltpu.VMEM((1, channels), F32),
            pltpu.VMEM(features.shape, BF16),
            pltpu.VMEM(previous.shape, BF16),
            pltpu.VMEM(conv_weight.shape, BF16),
            pltpu.VMEM(prev_weight.shape, BF16),
            pltpu.VMEM(previous.shape, BF16),
            pltpu.VMEM((CAP, LANES), jnp.int32),
            pltpu.VMEM((count, CAP, LANES), jnp.int32),
            pltpu.SMEM((count, CAP, LANES), jnp.int32),
            pltpu.VMEM((count, CAP, vox, channels), BF16),
            pltpu.VMEM((count, CAP, vox, channels), BF16),
            pltpu.VMEM((slots, FACE, channels), BF16),
            pltpu.VMEM((slots, FACE, channels), BF16),
            pltpu.VMEM((slots, vox), jnp.int32),
            pltpu.VMEM((slots, vox), jnp.int32),
            pltpu.VMEM(volume_shape, BF16),
            pltpu.VMEM((channels // LANES, slots * vox, LANES), F32),
            pltpu.VMEM((slots * vox, channels), F32),
            pltpu.VMEM(features.shape, F32),
            dma((6,)),
            dma((6,)),
            dma((4,)),
            dma((4,)),
            dma((count,)),
            dma((count,)),
            dma((count,)),
            dma((count,)),
        ],
        compiler_params=pltpu.CompilerParams(
            collective_id=1, has_side_effects=True, vmem_limit_bytes=66_000_000
        ),
        name="merge_full",
    )(
        old_owner[:, 0],
        old_slot,
        neighbors.T,
        norm_scale[None, :],
        norm_shift[None, :],
        features,
        previous,
        occupancy,
        conv_weight,
        prev_weight,
    )


def kernel(
    count,
    groups,
    slots,
    channels,
    owner_hbm,
    slot_hbm,
    nb_hbm,
    scale_hbm,
    shift_hbm,
    feat_hbm,
    prev_hbm,
    occ_hbm,
    w_hbm,
    pw_hbm,
    out_ref,
    over_ref,
    owner_s,
    slot_s,
    nb_ref,
    occ_ref,
    scale_ref,
    shift_ref,
    feat,
    prev,
    weight,
    pweight,
    proj,
    table,
    reqs,
    first_s,
    last_s,
    place_s,
    over,
    overs,
    send_first,
    send_row,
    send_z,
    send_x,
    relay_z,
    relay_x,
    relay_out,
    recv,
    low_layer,
    high_layer,
    low_occ,
    high_occ,
    volume,
    acc,
    mask,
    base,
    small_sem,
    local_sem,
    halo_send,
    halo_recv,
    rq_send,
    rq_recv,
    first_send,
    first_recv,
    row_send,
    row_recv,
    z_send,
    z_recv,
    x_send,
    x_recv,
    out_send,
    out_recv,
    late_1,
    late_2,
    over_send,
    over_recv,
):
    me = lax.axis_index("blk")
    grp = lax.axis_index("grp")
    half, row = count // 2, count // 4
    half_base = me // half * half
    row_base = me // row * row
    half_at, row_at = me - half_base, me - row_base
    other_half = half - half_base
    other_row = 2 * half_base + row - row_base
    across = lax.rem(me + half, count)
    beside = other_row + row_at
    row_part, z_part, x_part = count, count + row, count + row + EXTRA
    layer_rows = FACE * slots
    barrier = pltpu.get_barrier_semaphore()

    upper = half_base > 0
    cuts = (0, count * 5 // 8, count * 7 // 8, count)
    inside = [(me >= cuts[n]) & (me < cuts[n + 1]) for n in range(3)]
    lates = (None, late_1, late_2)

    def hello(sem, low, high):
        @pl.loop(low, high)
        def _(peer):
            @pl.when(peer != me)
            def _():
                pl.semaphore_signal(sem, inc=1, device_id={"blk": peer}, device_id_type=MESH)

    for n in range(3):

        @pl.when(inside[n])
        def _():
            hello(barrier, cuts[n], count)

    for i in range(1, groups):
        there = lax.rem(grp + i, groups)
        pl.semaphore_signal(barrier, inc=1, device_id={"grp": there}, device_id_type=MESH)

    small = [
        pltpu.make_async_copy(owner_hbm, owner_s, small_sem.at[0]),
        pltpu.make_async_copy(slot_hbm, slot_s, small_sem.at[1]),
        pltpu.make_async_copy(occ_hbm, occ_ref, small_sem.at[2]),
        pltpu.make_async_copy(nb_hbm, nb_ref, small_sem.at[3]),
        pltpu.make_async_copy(scale_hbm, scale_ref, small_sem.at[4]),
        pltpu.make_async_copy(shift_hbm, shift_ref, small_sem.at[5]),
    ]
    for load in small:
        load.start()
    loads = [
        pltpu.make_async_copy(prev_hbm, prev, local_sem.at[0]),
        pltpu.make_async_copy(pw_hbm, pweight, local_sem.at[1]),
        pltpu.make_async_copy(feat_hbm, feat, local_sem.at[2]),
        pltpu.make_async_copy(w_hbm, weight, local_sem.at[3]),
    ]
    for load in loads:
        load.start()

    small[0].wait()
    small[1].wait()

    lane = iota((1, LANES), 1)
    first = jnp.zeros((1, LANES), jnp.int32)
    last = jnp.zeros((1, LANES), jnp.int32)
    for s in range(slots):
        last = jnp.where(lane == owner_s[s], slot_s[s], last)
        t = slots - 1 - s
        first = jnp.where(lane == owner_s[t], slot_s[t], first)
    zero = jnp.int32(0)
    x_count, z_count = zero, zero
    x_owner, z_owner = [zero] * EXTRA, [zero] * EXTRA
    for s in range(slots):
        owner = owner_s[s]
        again = zero
        for t in range(s):
            again = jnp.where(owner_s[t] == owner, 1, again)
        far = jnp.where((owner < half_base) | (owner >= half_base + half), again, 0)
        near = jnp.where((owner >= other_row) & (owner < other_row + row), again, 0)
        for e in range(EXTRA):
            x_owner[e] = jnp.where((far == 1) & (x_count == e), owner - other_half, x_owner[e])
            z_owner[e] = jnp.where((near == 1) & (z_count == e), owner - other_row, z_owner[e])
        at = jnp.where(again == 1, row_part + owner - row_base, owner)
        at = jnp.where(near == 1, z_part + jnp.minimum(z_count, EXTRA - 1), at)
        place_s[s] = jnp.where(far == 1, x_part + jnp.minimum(x_count, EXTRA - 1), at)
        x_count = x_count + far
        z_count = z_count + near
    notes = jnp.where(
        lane == count + 2 * EXTRA, jnp.where((x_count > EXTRA) | (z_count > EXTRA), 1, 0), first + last * PACK
    )
    for e in range(EXTRA):
        notes = jnp.where(lane == count + e, x_owner[e], notes)
        notes = jnp.where(lane == count + EXTRA + e, z_owner[e], notes)
    table[...] = notes

    def layer_occ(occ, x):
        spread = one_hot(iota((VOX, layer_rows), 0) == x * FACE + iota((VOX, layer_rows), 1) % FACE)
        rows = jnp.dot(occ, spread, preferred_element_type=F32)
        own = iota((slots, layer_rows), 0) == iota((slots, layer_rows), 1) // FACE
        return jnp.sum(jnp.where(own, rows, 0.0), axis=0, keepdims=True).astype(BF16)

    for n in range(3):

        @pl.when(inside[n])
        def _():
            pl.semaphore_wait(barrier, cuts[n + 1] + groups - 2)
            if n:
                hello(lates[n], 0, cuts[n])

    def in_row(i):
        return row_base + lax.rem(row_at + i, row)

    def request(peer):
        return pltpu.make_async_remote_copy(
            src_ref=table,
            dst_ref=reqs.at[me],
            send_sem=rq_send.at[peer],
            recv_sem=rq_recv.at[me],
            device_id={"blk": peer},
            device_id_type=MESH,
        )

    def request_from(peer):
        return pltpu.make_async_remote_copy(
            src_ref=table,
            dst_ref=reqs.at[peer],
            send_sem=rq_send.at[peer],
            recv_sem=rq_recv.at[peer],
            device_id={"blk": peer},
            device_id_type=MESH,
        )

    def ask(low, high):
        @pl.loop(low, high)
        def _(peer):
            @pl.when(peer != me)
            def _():
                request(peer).start()

    up = lax.rem(me + 1, count)
    down = lax.rem(me + count - 1, count)

    def halo(k):
        if k < 2:
            src = feat_hbm.at[:, pl.ds((EDGE - 1) * FACE, FACE), :] if k == 0 else occ_hbm
            dst = low_layer if k == 0 else low_occ
            peer = up
        else:
            src = feat_hbm.at[:, pl.ds(0, FACE), :] if k == 2 else occ_hbm
            dst = high_layer if k == 2 else high_occ
            peer = down
        return pltpu.make_async_remote_copy(
            src_ref=src,
            dst_ref=dst,
            send_sem=halo_send.at[k],
            recv_sem=halo_recv.at[k],
            device_id={"blk": peer},
            device_id_type=MESH,
        )

    def meet(n):
        if n:

            @pl.when(me < cuts[n])
            def _():
                pl.semaphore_wait(lates[n], cuts[n + 1] - cuts[n])

            ask(cuts[n], cuts[n + 1])
        else:

            @pl.when(upper)
            def _():
                ask(0, half)
                ask(half, cuts[1])

            @pl.when(jnp.logical_not(upper))
            def _():
                ask(half, cuts[1])
                ask(0, half)

        @pl.when((me + 1 >= cuts[n]) & (me + 1 < cuts[n + 1]))
        def _():
            halo(0).start()
            halo(1).start()

    meet(0)

    @pl.when(me > 0)
    def _():
        halo(2).start()
        halo(3).start()

    @pl.when(me == 0)
    def _():
        low_layer[...] = jnp.zeros_like(low_layer)
        low_occ[...] = jnp.zeros_like(low_occ)

    @pl.when(me == count - 1)
    def _():
        high_layer[...] = jnp.zeros_like(high_layer)
        high_occ[...] = jnp.zeros_like(high_occ)

    loads[0].wait()
    loads[1].wait()

    blocks = layer_rows // VOX
    for s in range(0, slots, blocks):
        rows = prev[s : s + blocks].reshape(layer_rows, channels)
        part = jnp.dot(rows, pweight[...], preferred_element_type=F32).astype(BF16)
        proj[s : s + blocks] = part.reshape(blocks, VOX, channels)

    meet(1)
    meet(2)
    reqs[me] = table[...]

    def first_to(peer):
        return pltpu.make_async_remote_copy(
            src_ref=send_first.at[peer],
            dst_ref=recv.at[me],
            send_sem=first_send.at[peer],
            recv_sem=first_recv.at[me],
            device_id={"blk": peer},
            device_id_type=MESH,
        )

    def first_from(peer):
        return pltpu.make_async_remote_copy(
            src_ref=send_first.at[peer],
            dst_ref=recv.at[peer],
            send_sem=first_send.at[peer],
            recv_sem=first_recv.at[peer],
            device_id={"blk": peer},
            device_id_type=MESH,
        )

    def row_to(i):
        return pltpu.make_async_remote_copy(
            src_ref=send_row.at[i],
            dst_ref=recv.at[row_part + row_at],
            send_sem=row_send.at[i],
            recv_sem=row_recv.at[i],
            device_id={"blk": in_row(i)},
            device_id_type=MESH,
        )

    def z_to(i):
        return pltpu.make_async_remote_copy(
            src_ref=send_z.at[i],
            dst_ref=relay_z.at[row_at],
            send_sem=z_send.at[i],
            recv_sem=z_recv.at[i],
            device_id={"blk": in_row(i)},
            device_id_type=MESH,
        )

    def x_to(at):
        return pltpu.make_async_remote_copy(
            src_ref=send_x.at[at],
            dst_ref=relay_x.at[half_at],
            send_sem=x_send.at[at],
            recv_sem=x_recv.at[half_at],
            device_id={"blk": half_base + at},
            device_id_type=MESH,
        )

    def x_from(at):
        return pltpu.make_async_remote_copy(
            src_ref=send_x.at[at],
            dst_ref=relay_x.at[at],
            send_sem=x_send.at[at],
            recv_sem=x_recv.at[at],
            device_id={"blk": half_base + at},
            device_id_type=MESH,
        )

    def relay(k):
        part, peer = ((x_part, across), (z_part, beside))[k]
        return pltpu.make_async_remote_copy(
            src_ref=relay_out.at[pl.ds(k * EXTRA, EXTRA)],
            dst_ref=recv.at[pl.ds(part, EXTRA)],
            send_sem=out_send.at[k],
            recv_sem=out_recv.at[k],
            device_id={"blk": peer},
            device_id_type=MESH,
        )

    def over_to(i):
        return pltpu.make_async_remote_copy(
            src_ref=over,
            dst_ref=overs.at[grp],
            send_sem=over_send.at[i],
            recv_sem=over_recv.at[i],
            device_id={"grp": lax.rem(grp + i, groups)},
            device_id_type=MESH,
        )

    def entry(peer, at):
        return jnp.sum(jnp.where(lane == at, reqs[peer], 0))

    def read(peer):
        wanted = entry(peer, me)
        first_s[peer] = wanted % PACK
        last_s[peer] = wanted // PACK

    def send_first_to(peer):
        send_first[peer] = proj[first_s[peer]]
        first_to(peer).start()

    def send_across(at):
        send_x[at] = proj[last_s[other_half + at]]
        x_to(at).start()

    def send_beside(i):
        send_z[i] = proj[last_s[other_row + lax.rem(row_at + i, row)]]
        z_to(i).start()

    def send_second(i):
        send_row[i] = proj[last_s[in_row(i)]]
        row_to(i).start()

    def others(body):
        @pl.loop(1, half)
        def _(i):
            body(lax.rem(half_at + i, half))

    def serve(low, high):
        size = high - low

        def turned(i):
            return low + lax.rem(half_at + i, size)

        @pl.loop(low, high)
        def _(at):
            request_from(other_half + at).wait_recv()

        for at in range(low, high):
            read(other_half + at)

        @pl.loop(0, size // 2)
        def _(i):
            send_first_to(other_half + turned(i))

        @pl.loop(0, size)
        def _(i):
            at = turned(i)

            @pl.when(at != half_at)
            def _():
                send_across(at)

        @pl.loop(size // 2, size)
        def _(i):
            send_first_to(other_half + turned(i))

    @pl.when(upper)
    def _():
        serve(0, row)
        serve(row, half)

    @pl.when(jnp.logical_not(upper))
    def _():
        for n in range(3):
            serve(max(cuts[n], half) - half, cuts[n + 1] - half)

    others(lambda at: request_from(half_base + at).wait_recv())

    for at in range(half):
        read(half_base + at)

    @pl.loop(1, row)
    def _(i):
        send_beside(i)

    others(lambda at: send_first_to(half_base + at))

    @pl.loop(1, row)
    def _(i):
        send_second(i)

    recv[me] = proj[first_s[me]]
    recv[row_part + row_at] = proj[last_s[me]]
    relay_x[half_at] = proj[last_s[across]]
    relay_z[row_at] = proj[last_s[beside]]

    notes = reqs[...].reshape(count, LANES)
    over[...] = jnp.sum(jnp.where(lane == count + 2 * EXTRA, notes, 0), axis=0, keepdims=True)
    for i in range(1, groups):
        over_to(i).start()

    for load in small[2:]:
        load.wait()
    occ = occ_ref[...].astype(BF16)
    volume[...] = jnp.zeros_like(volume)
    loads[2].wait()
    col = iota((layer_rows, layer_rows), 1)
    line = iota((layer_rows, layer_rows), 0)
    select_own = one_hot(col == (line % slots) * FACE + line // slots)
    spread = one_hot(iota((layer_rows, slots), 0) % slots == iota((layer_rows, slots), 1))
    nb = lax.dot_general(
        spread,
        nb_ref[...].astype(F32).astype(BF16),
        (((1,), (1,)), ((), ())),
        preferred_element_type=F32,
    ).astype(jnp.int32)
    side_rows = EDGE * slots
    scol = iota((side_rows, layer_rows), 1)
    sline = iota((side_rows, 1), 0) // slots

    def side(f, fixed, step):
        wanted = nb[:side_rows, f : f + 1]
        target = jnp.where(wanted >= 0, wanted * FACE + fixed + sline * step, -1)
        return one_hot(scol == target)

    sides = [
        side(2, (EDGE - 1) * EDGE, 1),
        side(3, 0, 1),
        side(4, EDGE - 1, EDGE),
        side(5, 0, EDGE),
    ]
    select = jnp.concatenate([select_own] + sides, axis=0)
    for x in range(EDGE):
        layer = feat[:, x * FACE : (x + 1) * FACE, :].reshape(layer_rows, channels)
        part = jnp.dot(select * layer_occ(occ, x), layer, preferred_element_type=F32).astype(BF16)
        volume[x + 1, 1 : EDGE + 1, 1 : EDGE + 1] = part[:layer_rows].reshape(
            EDGE, EDGE, slots, channels
        )
        faces = part[layer_rows:].reshape(4, EDGE, slots, channels)
        volume[x + 1, 0, 1 : EDGE + 1] = faces[0]
        volume[x + 1, EDGE + 1, 1 : EDGE + 1] = faces[1]
        volume[x + 1, 1 : EDGE + 1, 0] = faces[2]
        volume[x + 1, 1 : EDGE + 1, EDGE + 1] = faces[3]

    @pl.when(me > 0)
    def _():
        pltpu.make_async_remote_copy(
            src_ref=feat_hbm.at[:, pl.ds(0, FACE), :],
            dst_ref=low_layer,
            send_sem=halo_send.at[0],
            recv_sem=halo_recv.at[0],
            device_id={"blk": up},
            device_id_type=MESH,
        ).wait_recv()
        halo(1).wait_recv()

    @pl.when(me < count - 1)
    def _():
        halo(2).wait_recv()
        halo(3).wait_recv()

    def x_face(f, layer_ref, other_occ, x):
        wanted = nb[:, f : f + 1]
        target = jnp.where(wanted >= 0, wanted * FACE + iota((layer_rows, 1), 0) // slots, -1)
        pick = one_hot(col == target) * layer_occ(other_occ[...].astype(BF16), x)
        layer = layer_ref[...].reshape(layer_rows, channels)
        part = jnp.dot(pick, layer, preferred_element_type=F32).astype(BF16)
        return part.reshape(EDGE, EDGE, slots, channels)

    volume[0, 1 : EDGE + 1, 1 : EDGE + 1] = x_face(0, low_layer, low_occ, EDGE - 1)
    volume[EDGE + 1, 1 : EDGE + 1, 1 : EDGE + 1] = x_face(1, high_layer, high_occ, 0)

    loads[3].wait()
    scale = scale_ref[...]
    shift = shift_ref[...]

    @pl.loop(0, 2)
    def _(x):
        total = jnp.zeros((layer_rows, channels), F32)
        for tap in range(27):
            a, b, c = tap // 9, (tap // 3) % 3, tap % 3
            window = volume[x + a, b : b + EDGE, c : c + EDGE].reshape(layer_rows, channels)
            total = total + jnp.dot(window, weight[tap], preferred_element_type=F32)
        hidden = jnp.maximum(total * scale + shift, 0.0)
        for k in range(channels // LANES):
            acc[k, pl.ds(x * layer_rows, layer_rows), :] = hidden[:, k * LANES : (k + 1) * LANES]

    others(lambda at: x_from(at).wait_recv())

    for e in range(EXTRA):
        relay_out[e] = relay_x[entry(across, count + e)]
    relay(0).start()

    @pl.loop(2, EDGE)
    def _(x):
        total = jnp.zeros((layer_rows, channels), F32)
        for tap in range(27):
            a, b, c = tap // 9, (tap // 3) % 3, tap % 3
            window = volume[x + a, b : b + EDGE, c : c + EDGE].reshape(layer_rows, channels)
            total = total + jnp.dot(window, weight[tap], preferred_element_type=F32)
        hidden = jnp.maximum(total * scale + shift, 0.0)
        for k in range(channels // LANES):
            acc[k, pl.ds(x * layer_rows, layer_rows), :] = hidden[:, k * LANES : (k + 1) * LANES]

    @pl.loop(1, row)
    def _(i):
        z_to(i).wait_recv()

    for e in range(EXTRA):
        relay_out[EXTRA + e] = relay_z[entry(beside, count + EXTRA + e)]
    relay(1).start()

    @pl.loop(0, slots)
    def _(s):
        mine = jnp.where(iota((VOX, VOX), 0) == iota((VOX, VOX), 1), occ_ref[pl.ds(s, 1), :], 0)
        mask[pl.ds(s * VOX, VOX), :] = jnp.dot(
            mine.astype(BF16), jnp.ones((VOX, channels), BF16), preferred_element_type=F32
        )

    for s in range(slots):
        hidden = jnp.concatenate(
            [acc[k, pl.ds(s, VOX, stride=slots), :] for k in range(channels // LANES)],
            axis=1,
        )
        base[s] = hidden * mask[s * VOX : (s + 1) * VOX, :]

    overs[grp] = over[...]
    for i in range(1, groups):
        over_to(i).wait_recv()
    over_ref[0] = jnp.sum(overs[...])

    def everyone(body):
        @pl.loop(1, count)
        def _(i):
            body(lax.rem(me + i, count))

    everyone(lambda peer: request(peer).wait_send())
    everyone(lambda peer: first_to(peer).wait_send())
    others(lambda at: x_to(at).wait_send())

    @pl.loop(1, row)
    def _(i):
        row_to(i).wait_send()
        z_to(i).wait_send()

    relay(0).wait_send()
    relay(1).wait_send()
    for i in range(1, groups):
        over_to(i).wait_send()

    @pl.when(me < count - 1)
    def _():
        halo(0).wait_send()
        halo(1).wait_send()

    @pl.when(me > 0)
    def _():
        halo(2).wait_send()
        halo(3).wait_send()

    everyone(lambda peer: first_from(peer).wait_recv())

    @pl.loop(1, row)
    def _(i):
        row_to(i).wait_recv()

    relay(0).wait_recv()
    relay(1).wait_recv()

    for s in range(slots):
        moved = recv[place_s[s]].astype(F32)
        out_ref[s] = (base[s] + moved * mask[s * VOX : (s + 1) * VOX, :]).astype(BF16)


def per_device(
    features,
    occupancy,
    neighbors,
    previous,
    old_owner,
    old_slot,
    conv_weight,
    norm_scale,
    norm_shift,
    prev_weight,
):
    slots, vox, channels = features.shape
    count = lax.axis_size("blk")
    groups = lax.axis_size("grp")
    half, row = count // 2, count // 4
    hbm = pl.BlockSpec(memory_space=pl.ANY)
    volume_shape = (EDGE + 2, EDGE + 2, EDGE + 2, slots, channels)
    dma = pltpu.SemaphoreType.DMA
    return pl.pallas_call(
        functools.partial(kernel, count, groups, slots, channels),
        out_shape=[
            pltpu.VMEM(features.shape, BF16),
            pltpu.SMEM((1,), jnp.int32),
        ],
        in_specs=[hbm] * 10,
        out_specs=[
            pl.BlockSpec(memory_space=pltpu.VMEM),
            pl.BlockSpec(memory_space=pltpu.SMEM),
        ],
        scratch_shapes=[
            pltpu.SMEM((slots,), jnp.int32),
            pltpu.SMEM((slots,), jnp.int32),
            pltpu.VMEM((6, slots), jnp.int32),
            pltpu.VMEM((slots, vox), jnp.int32),
            pltpu.VMEM((1, channels), F32),
            pltpu.VMEM((1, channels), F32),
            pltpu.VMEM(features.shape, BF16),
            pltpu.VMEM(previous.shape, BF16),
            pltpu.VMEM(conv_weight.shape, BF16),
            pltpu.VMEM(prev_weight.shape, BF16),
            pltpu.VMEM(previous.shape, BF16),
            pltpu.VMEM((1, LANES), jnp.int32),
            pltpu.VMEM((count, 1, LANES), jnp.int32),
            pltpu.SMEM((count,), jnp.int32),
            pltpu.SMEM((count,), jnp.int32),
            pltpu.SMEM((slots,), jnp.int32),
            pltpu.VMEM((1, LANES), jnp.int32),
            pltpu.VMEM((groups, 1, LANES), jnp.int32),
            pltpu.VMEM((count, vox, channels), BF16),
            pltpu.VMEM((row, vox, channels), BF16),
            pltpu.VMEM((row, vox, channels), BF16),
            pltpu.VMEM((half, vox, channels), BF16),
            pltpu.VMEM((row, vox, channels), BF16),
            pltpu.VMEM((half, vox, channels), BF16),
            pltpu.VMEM((2 * EXTRA, vox, channels), BF16),
            pltpu.VMEM((count + row + 2 * EXTRA, vox, channels), BF16),
            pltpu.VMEM((slots, FACE, channels), BF16),
            pltpu.VMEM((slots, FACE, channels), BF16),
            pltpu.VMEM((slots, vox), jnp.int32),
            pltpu.VMEM((slots, vox), jnp.int32),
            pltpu.VMEM(volume_shape, BF16),
            pltpu.VMEM((channels // LANES, slots * vox, LANES), F32),
            pltpu.VMEM((slots * vox, channels), F32),
            pltpu.VMEM(features.shape, F32),
            dma((6,)),
            dma((6,)),
            dma((4,)),
            dma((4,)),
            dma((count,)),
            dma((count,)),
            dma((count,)),
            dma((count,)),
            dma((row,)),
            dma((row,)),
            dma((row,)),
            dma((row,)),
            dma((half,)),
            dma((half,)),
            dma((2,)),
            dma((2,)),
            pltpu.SemaphoreType.REGULAR,
            pltpu.SemaphoreType.REGULAR,
            dma((groups,)),
            dma((groups,)),
        ],
        compiler_params=pltpu.CompilerParams(
            collective_id=0, has_side_effects=True, vmem_limit_bytes=66_000_000
        ),
        name="merge_blocks",
    )(
        old_owner[:, 0],
        old_slot,
        neighbors.T,
        norm_scale[None, :],
        norm_shift[None, :],
        features,
        previous,
        occupancy,
        conv_weight,
        prev_weight,
    )


def merge(*arrays):
    merged, over = per_device(*arrays)
    return lax.switch(over[0], [lambda: merged, lambda: merge_full(*arrays)])


def solution(mesh):
    in_specs = (
        P(("grp", "blk"), None, None),
        P(("grp", "blk"), None),
        P(("grp", "blk"), None),
        P(("grp", "blk"), None, None),
        P(("grp", "blk"), None),
        P(("grp", "blk")),
        P(),
        P(),
        P(),
        P(),
    )
    out_specs = P(("grp", "blk"), None, None)
    return jax.shard_map(
        merge, mesh=mesh, in_specs=in_specs, out_specs=out_specs, check_vma=False
    )
```

```python
import functools

import jax
import jax.numpy as jnp
from jax import lax
from jax.experimental import pallas as pl
from jax.experimental.pallas import tpu as pltpu
from jax.sharding import PartitionSpec as P

EDGE = 4
FACE = EDGE * EDGE
VOX = EDGE * FACE
CAP = 2
LANES = 128
EXTRA = 2
PACK = 1 << 16
MESH = pl.DeviceIdType.MESH
F32 = jnp.float32
BF16 = jnp.bfloat16


def iota(shape, dim):
    return lax.broadcasted_iota(jnp.int32, shape, dim)


def one_hot(hit):
    return jnp.where(hit, 1.0, 0.0).astype(BF16)


def kernel_full(
    count,
    slots,
    channels,
    owner_hbm,
    slot_hbm,
    nb_hbm,
    scale_hbm,
    shift_hbm,
    feat_hbm,
    prev_hbm,
    occ_hbm,
    w_hbm,
    pw_hbm,
    out_ref,
    owner_s,
    slot_s,
    nb_ref,
    occ_ref,
    scale_ref,
    shift_ref,
    feat,
    prev,
    weight,
    pweight,
    proj,
    table,
    reqs,
    reqs_s,
    sendbuf,
    recv,
    low_layer,
    high_layer,
    low_occ,
    high_occ,
    volume,
    acc,
    mask,
    base,
    small_sem,
    local_sem,
    halo_send,
    halo_recv,
    rq_send,
    rq_recv,
    rp_send,
    rp_recv,
):
    me = lax.axis_index("blk")
    layer_rows = FACE * slots
    barrier = pltpu.get_barrier_semaphore()

    @pl.loop(1, count)
    def _(i):
        peer = lax.rem(me + i, count)
        pl.semaphore_signal(barrier, inc=1, device_id={"blk": peer}, device_id_type=MESH)

    small = [
        pltpu.make_async_copy(owner_hbm, owner_s, small_sem.at[0]),
        pltpu.make_async_copy(slot_hbm, slot_s, small_sem.at[1]),
        pltpu.make_async_copy(occ_hbm, occ_ref, small_sem.at[2]),
        pltpu.make_async_copy(nb_hbm, nb_ref, small_sem.at[3]),
        pltpu.make_async_copy(scale_hbm, scale_ref, small_sem.at[4]),
        pltpu.make_async_copy(shift_hbm, shift_ref, small_sem.at[5]),
    ]
    for load in small:
        load.start()
    loads = [
        pltpu.make_async_copy(prev_hbm, prev, local_sem.at[0]),
        pltpu.make_async_copy(pw_hbm, pweight, local_sem.at[1]),
        pltpu.make_async_copy(feat_hbm, feat, local_sem.at[2]),
        pltpu.make_async_copy(w_hbm, weight, local_sem.at[3]),
    ]
    for load in loads:
        load.start()

    small[0].wait()
    small[1].wait()

    lane = iota((1, LANES), 1)
    first = jnp.zeros((1, LANES), jnp.int32)
    last = jnp.zeros((1, LANES), jnp.int32)
    for s in range(slots):
        last = jnp.where(lane == owner_s[s], slot_s[s], last)
        t = slots - 1 - s
        first = jnp.where(lane == owner_s[t], slot_s[t], first)
    row = iota((CAP, LANES), 0)
    table[...] = jnp.where(row == 0, first, last)

    def layer_occ(occ, x):
        spread = one_hot(iota((VOX, layer_rows), 0) == x * FACE + iota((VOX, layer_rows), 1) % FACE)
        rows = jnp.dot(occ, spread, preferred_element_type=F32)
        own = iota((slots, layer_rows), 0) == iota((slots, layer_rows), 1) // FACE
        return jnp.sum(jnp.where(own, rows, 0.0), axis=0, keepdims=True).astype(BF16)

    pl.semaphore_wait(barrier, count - 1)

    def request(i):
        return pltpu.make_async_remote_copy(
            src_ref=table,
            dst_ref=reqs.at[me],
            send_sem=rq_send.at[i],
            recv_sem=rq_recv.at[i],
            device_id={"blk": lax.rem(me + i, count)},
            device_id_type=MESH,
        )

    @pl.loop(1, count)
    def _(i):
        request(i).start()

    up = lax.rem(me + 1, count)
    down = lax.rem(me + count - 1, count)

    def halo(k):
        if k < 2:
            src = feat_hbm.at[:, pl.ds((EDGE - 1) * FACE, FACE), :] if k == 0 else occ_hbm
            dst = low_layer if k == 0 else low_occ
            peer = up
        else:
            src = feat_hbm.at[:, pl.ds(0, FACE), :] if k == 2 else occ_hbm
            dst = high_layer if k == 2 else high_occ
            peer = down
        return pltpu.make_async_remote_copy(
            src_ref=src,
            dst_ref=dst,
            send_sem=halo_send.at[k],
            recv_sem=halo_recv.at[k],
            device_id={"blk": peer},
            device_id_type=MESH,
        )

    @pl.when(me < count - 1)
    def _():
        halo(0).start()
        halo(1).start()

    @pl.when(me > 0)
    def _():
        halo(2).start()
        halo(3).start()

    @pl.when(me == 0)
    def _():
        low_layer[...] = jnp.zeros_like(low_layer)
        low_occ[...] = jnp.zeros_like(low_occ)

    @pl.when(me == count - 1)
    def _():
        high_layer[...] = jnp.zeros_like(high_layer)
        high_occ[...] = jnp.zeros_like(high_occ)

    loads[0].wait()
    loads[1].wait()

    blocks = layer_rows // VOX
    for s in range(0, slots, blocks):
        rows = prev[s : s + blocks].reshape(layer_rows, channels)
        part = jnp.dot(rows, pweight[...], preferred_element_type=F32).astype(BF16)
        proj[s : s + blocks] = part.reshape(blocks, VOX, channels)

    reqs_s_copy = pltpu.make_async_copy(reqs, reqs_s, local_sem.at[4])

    def reply(i):
        return pltpu.make_async_remote_copy(
            src_ref=sendbuf.at[i],
            dst_ref=recv.at[me],
            send_sem=rp_send.at[i],
            recv_sem=rp_recv.at[i],
            device_id={"blk": lax.rem(me + i, count)},
            device_id_type=MESH,
        )

    reqs[me] = table[...]

    @pl.loop(1, count)
    def _(i):
        request(i).wait_recv()

    reqs_s_copy.start()
    reqs_s_copy.wait()

    def far_first(k):
        step = (k + 1) // 2
        return count // 2 + step * (2 * (k % 2) - 1)

    @pl.loop(0, count - 1)
    def _(k):
        i = far_first(k)
        peer = lax.rem(me + i, count)
        sendbuf[i, 0] = proj[reqs_s[peer, 0, me]]
        sendbuf[i, 1] = proj[reqs_s[peer, 1, me]]

    @pl.loop(0, count - 1)
    def _(k):
        reply(far_first(k)).start()

    recv[me, 0] = proj[reqs_s[me, 0, me]]
    recv[me, 1] = proj[reqs_s[me, 1, me]]

    for load in small[2:]:
        load.wait()
    occ = occ_ref[...].astype(BF16)
    volume[...] = jnp.zeros_like(volume)
    loads[2].wait()
    col = iota((layer_rows, layer_rows), 1)
    line = iota((layer_rows, layer_rows), 0)
    select_own = one_hot(col == (line % slots) * FACE + line // slots)
    spread = one_hot(iota((layer_rows, slots), 0) % slots == iota((layer_rows, slots), 1))
    nb = lax.dot_general(
        spread,
        nb_ref[...].astype(F32).astype(BF16),
        (((1,), (1,)), ((), ())),
        preferred_element_type=F32,
    ).astype(jnp.int32)
    side_rows = EDGE * slots
    scol = iota((side_rows, layer_rows), 1)
    sline = iota((side_rows, 1), 0) // slots

    def side(f, fixed, step):
        wanted = nb[:side_rows, f : f + 1]
        target = jnp.where(wanted >= 0, wanted * FACE + fixed + sline * step, -1)
        return one_hot(scol == target)

    sides = [
        side(2, (EDGE - 1) * EDGE, 1),
        side(3, 0, 1),
        side(4, EDGE - 1, EDGE),
        side(5, 0, EDGE),
    ]
    select = jnp.concatenate([select_own] + sides, axis=0)
    for x in range(EDGE):
        layer = feat[:, x * FACE : (x + 1) * FACE, :].reshape(layer_rows, channels)
        part = jnp.dot(select * layer_occ(occ, x), layer, preferred_element_type=F32).astype(BF16)
        volume[x + 1, 1 : EDGE + 1, 1 : EDGE + 1] = part[:layer_rows].reshape(
            EDGE, EDGE, slots, channels
        )
        faces = part[layer_rows:].reshape(4, EDGE, slots, channels)
        volume[x + 1, 0, 1 : EDGE + 1] = faces[0]
        volume[x + 1, EDGE + 1, 1 : EDGE + 1] = faces[1]
        volume[x + 1, 1 : EDGE + 1, 0] = faces[2]
        volume[x + 1, 1 : EDGE + 1, EDGE + 1] = faces[3]

    @pl.when(me > 0)
    def _():
        pltpu.make_async_remote_copy(
            src_ref=feat_hbm.at[:, pl.ds(0, FACE), :],
            dst_ref=low_layer,
            send_sem=halo_send.at[0],
            recv_sem=halo_recv.at[0],
            device_id={"blk": up},
            device_id_type=MESH,
        ).wait_recv()
        halo(1).wait_recv()

    @pl.when(me < count - 1)
    def _():
        halo(2).wait_recv()
        halo(3).wait_recv()

    def x_face(f, layer_ref, other_occ, x):
        wanted = nb[:, f : f + 1]
        target = jnp.where(wanted >= 0, wanted * FACE + iota((layer_rows, 1), 0) // slots, -1)
        pick = one_hot(col == target) * layer_occ(other_occ[...].astype(BF16), x)
        layer = layer_ref[...].reshape(layer_rows, channels)
        part = jnp.dot(pick, layer, preferred_element_type=F32).astype(BF16)
        return part.reshape(EDGE, EDGE, slots, channels)

    volume[0, 1 : EDGE + 1, 1 : EDGE + 1] = x_face(0, low_layer, low_occ, EDGE - 1)
    volume[EDGE + 1, 1 : EDGE + 1, 1 : EDGE + 1] = x_face(1, high_layer, high_occ, 0)

    loads[3].wait()
    scale = scale_ref[...]
    shift = shift_ref[...]

    @pl.loop(0, EDGE)
    def _(x):
        total = jnp.zeros((layer_rows, channels), F32)
        for tap in range(27):
            a, b, c = tap // 9, (tap // 3) % 3, tap % 3
            window = volume[x + a, b : b + EDGE, c : c + EDGE].reshape(layer_rows, channels)
            total = total + jnp.dot(window, weight[tap], preferred_element_type=F32)
        hidden = jnp.maximum(total * scale + shift, 0.0)
        for k in range(channels // LANES):
            acc[k, pl.ds(x * layer_rows, layer_rows), :] = hidden[:, k * LANES : (k + 1) * LANES]

    @pl.loop(0, slots)
    def _(s):
        mine = jnp.where(iota((VOX, VOX), 0) == iota((VOX, VOX), 1), occ_ref[pl.ds(s, 1), :], 0)
        mask[pl.ds(s * VOX, VOX), :] = jnp.dot(
            mine.astype(BF16), jnp.ones((VOX, channels), BF16), preferred_element_type=F32
        )

    picks = []
    for s in range(slots):
        rank = jnp.int32(0)
        for t in range(s):
            rank = jnp.where(owner_s[t] == owner_s[s], 1, rank)
        picks.append(rank)
        hidden = jnp.concatenate(
            [acc[k, pl.ds(s, VOX, stride=slots), :] for k in range(channels // LANES)],
            axis=1,
        )
        base[s] = hidden * mask[s * VOX : (s + 1) * VOX, :]

    @pl.loop(1, count)
    def _(i):
        reply(i).wait_recv()

    for s in range(slots):
        moved = recv[owner_s[s], picks[s]].astype(F32)
        out_ref[s] = (base[s] + moved * mask[s * VOX : (s + 1) * VOX, :]).astype(BF16)

    @pl.loop(1, count)
    def _(i):
        request(i).wait_send()
        reply(i).wait_send()

    @pl.when(me < count - 1)
    def _():
        halo(0).wait_send()
        halo(1).wait_send()

    @pl.when(me > 0)
    def _():
        halo(2).wait_send()
        halo(3).wait_send()


def merge_full(
    features,
    occupancy,
    neighbors,
    previous,
    old_owner,
    old_slot,
    conv_weight,
    norm_scale,
    norm_shift,
    prev_weight,
):
    slots, vox, channels = features.shape
    count = lax.axis_size("blk")
    hbm = pl.BlockSpec(memory_space=pl.ANY)
    volume_shape = (EDGE + 2, EDGE + 2, EDGE + 2, slots, channels)
    dma = pltpu.SemaphoreType.DMA
    return pl.pallas_call(
        functools.partial(kernel_full, count, slots, channels),
        out_shape=pltpu.VMEM(features.shape, BF16),
        in_specs=[hbm] * 10,
        out_specs=pl.BlockSpec(memory_space=pltpu.VMEM),
        scratch_shapes=[
            pltpu.SMEM((slots,), jnp.int32),
            pltpu.SMEM((slots,), jnp.int32),
            pltpu.VMEM((6, slots), jnp.int32),
            pltpu.VMEM((slots, vox), jnp.int32),
            pltpu.VMEM((1, channels), F32),
            pltpu.VMEM((1, channels), F32),
            pltpu.VMEM(features.shape, BF16),
            pltpu.VMEM(previous.shape, BF16),
            pltpu.VMEM(conv_weight.shape, BF16),
            pltpu.VMEM(prev_weight.shape, BF16),
            pltpu.VMEM(previous.shape, BF16),
            pltpu.VMEM((CAP, LANES), jnp.int32),
            pltpu.VMEM((count, CAP, LANES), jnp.int32),
            pltpu.SMEM((count, CAP, LANES), jnp.int32),
            pltpu.VMEM((count, CAP, vox, channels), BF16),
            pltpu.VMEM((count, CAP, vox, channels), BF16),
            pltpu.VMEM((slots, FACE, channels), BF16),
            pltpu.VMEM((slots, FACE, channels), BF16),
            pltpu.VMEM((slots, vox), jnp.int32),
            pltpu.VMEM((slots, vox), jnp.int32),
            pltpu.VMEM(volume_shape, BF16),
            pltpu.VMEM((channels // LANES, slots * vox, LANES), F32),
            pltpu.VMEM((slots * vox, channels), F32),
            pltpu.VMEM(features.shape, F32),
            dma((6,)),
            dma((6,)),
            dma((4,)),
            dma((4,)),
            dma((count,)),
            dma((count,)),
            dma((count,)),
            dma((count,)),
        ],
        compiler_params=pltpu.CompilerParams(
            collective_id=1, has_side_effects=True, vmem_limit_bytes=66_000_000
        ),
        name="merge_full",
    )(
        old_owner[:, 0],
        old_slot,
        neighbors.T,
        norm_scale[None, :],
        norm_shift[None, :],
        features,
        previous,
        occupancy,
        conv_weight,
        prev_weight,
    )


def kernel(
    count,
    groups,
    slots,
    channels,
    owner_hbm,
    slot_hbm,
    nb_hbm,
    scale_hbm,
    shift_hbm,
    feat_hbm,
    prev_hbm,
    occ_hbm,
    w_hbm,
    pw_hbm,
    out_ref,
    over_ref,
    owner_s,
    slot_s,
    nb_ref,
    occ_ref,
    scale_ref,
    shift_ref,
    feat,
    prev,
    weight,
    pweight,
    proj,
    table,
    near_reqs,
    far_reqs,
    first_s,
    last_s,
    place_s,
    over,
    overs,
    send_first,
    send_row,
    send_z,
    send_x,
    relay_z,
    relay_x,
    relay_out,
    recv,
    low_layer,
    high_layer,
    low_occ,
    high_occ,
    volume,
    acc,
    mask,
    base,
    small_sem,
    local_sem,
    halo_send,
    halo_recv,
    rq_send,
    rq_recv,
    first_send,
    first_recv,
    row_send,
    row_recv,
    z_send,
    z_recv,
    x_send,
    x_recv,
    out_send,
    out_recv,
    late_sem,
    over_send,
    over_recv,
):
    me = lax.axis_index("blk")
    grp = lax.axis_index("grp")
    half, row = count // 2, count // 4
    half_base = me // half * half
    row_base = me // row * row
    half_at, row_at = me - half_base, me - row_base
    other_half = half - half_base
    other_row = 2 * half_base + row - row_base
    across = lax.rem(me + half, count)
    beside = other_row + row_at
    row_part, z_part, x_part = count, count + row, count + row + EXTRA
    layer_rows = FACE * slots
    barrier = pltpu.get_barrier_semaphore()

    upper = half_base > 0
    last_row = count - row
    late = me >= last_row

    def hello(peer):
        pl.semaphore_signal(barrier, inc=1, device_id={"blk": peer}, device_id_type=MESH)

    @pl.when(jnp.logical_not(late))
    def _():
        @pl.loop(1, count)
        def _(i):
            hello(lax.rem(me + i, count))

    @pl.when(late)
    def _():
        @pl.loop(1, row)
        def _(i):
            hello(row_base + lax.rem(row_at + i, row))

    for i in range(1, groups):
        there = lax.rem(grp + i, groups)
        pl.semaphore_signal(barrier, inc=1, device_id={"grp": there}, device_id_type=MESH)

    small = [
        pltpu.make_async_copy(owner_hbm, owner_s, small_sem.at[0]),
        pltpu.make_async_copy(slot_hbm, slot_s, small_sem.at[1]),
        pltpu.make_async_copy(occ_hbm, occ_ref, small_sem.at[2]),
        pltpu.make_async_copy(nb_hbm, nb_ref, small_sem.at[3]),
        pltpu.make_async_copy(scale_hbm, scale_ref, small_sem.at[4]),
        pltpu.make_async_copy(shift_hbm, shift_ref, small_sem.at[5]),
    ]
    for load in small:
        load.start()
    loads = [
        pltpu.make_async_copy(prev_hbm, prev, local_sem.at[0]),
        pltpu.make_async_copy(pw_hbm, pweight, local_sem.at[1]),
        pltpu.make_async_copy(feat_hbm, feat, local_sem.at[2]),
        pltpu.make_async_copy(w_hbm, weight, local_sem.at[3]),
    ]
    for load in loads:
        load.start()

    small[0].wait()
    small[1].wait()

    lane = iota((1, LANES), 1)
    first = jnp.zeros((1, LANES), jnp.int32)
    last = jnp.zeros((1, LANES), jnp.int32)
    for s in range(slots):
        last = jnp.where(lane == owner_s[s], slot_s[s], last)
        t = slots - 1 - s
        first = jnp.where(lane == owner_s[t], slot_s[t], first)
    zero = jnp.int32(0)
    x_count, z_count = zero, zero
    x_owner, z_owner = [zero] * EXTRA, [zero] * EXTRA
    for s in range(slots):
        owner = owner_s[s]
        again = zero
        for t in range(s):
            again = jnp.where(owner_s[t] == owner, 1, again)
        far = jnp.where((owner < half_base) | (owner >= half_base + half), again, 0)
        near = jnp.where((owner >= other_row) & (owner < other_row + row), again, 0)
        for e in range(EXTRA):
            x_owner[e] = jnp.where((far == 1) & (x_count == e), owner - other_half, x_owner[e])
            z_owner[e] = jnp.where((near == 1) & (z_count == e), owner - other_row, z_owner[e])
        at = jnp.where(again == 1, row_part + owner - row_base, owner)
        at = jnp.where(near == 1, z_part + jnp.minimum(z_count, EXTRA - 1), at)
        place_s[s] = jnp.where(far == 1, x_part + jnp.minimum(x_count, EXTRA - 1), at)
        x_count = x_count + far
        z_count = z_count + near
    notes = jnp.where(
        lane == count + 2 * EXTRA, jnp.where((x_count > EXTRA) | (z_count > EXTRA), 1, 0), first + last * PACK
    )
    for e in range(EXTRA):
        notes = jnp.where(lane == count + e, x_owner[e], notes)
        notes = jnp.where(lane == count + EXTRA + e, z_owner[e], notes)
    table[...] = notes

    def layer_occ(occ, x):
        spread = one_hot(iota((VOX, layer_rows), 0) == x * FACE + iota((VOX, layer_rows), 1) % FACE)
        rows = jnp.dot(occ, spread, preferred_element_type=F32)
        own = iota((slots, layer_rows), 0) == iota((slots, layer_rows), 1) // FACE
        return jnp.sum(jnp.where(own, rows, 0.0), axis=0, keepdims=True).astype(BF16)

    @pl.when(jnp.logical_not(late))
    def _():
        pl.semaphore_wait(barrier, count - row + groups - 2)

    @pl.when(late)
    def _():
        pl.semaphore_wait(barrier, count + groups - 2)

        @pl.loop(0, last_row)
        def _(i):
            pl.semaphore_signal(late_sem, inc=1, device_id={"blk": i}, device_id_type=MESH)

    def in_row(i):
        return row_base + lax.rem(row_at + i, row)

    def request(at, far):
        return pltpu.make_async_remote_copy(
            src_ref=table,
            dst_ref=(far_reqs if far else near_reqs).at[half_at],
            send_sem=rq_send.at[far * half + at],
            recv_sem=rq_recv.at[far * half + half_at],
            device_id={"blk": (other_half if far else half_base) + at},
            device_id_type=MESH,
        )

    def request_from(at, far):
        return pltpu.make_async_remote_copy(
            src_ref=table,
            dst_ref=(far_reqs if far else near_reqs).at[at],
            send_sem=rq_send.at[far * half + at],
            recv_sem=rq_recv.at[far * half + at],
            device_id={"blk": (other_half if far else half_base) + at},
            device_id_type=MESH,
        )

    def turned(part, i):
        return part * row + lax.rem(row_at + i, row)

    def request_row(part, far):
        @pl.loop(0, row)
        def _(i):
            at = turned(part, i)
            if far:
                request(at, far).start()
            else:

                @pl.when(at != half_at)
                def _():
                    request(at, far).start()

    request_row(0, 1)

    @pl.when(upper)
    def _():
        request_row(1, 1)

    request_row(0, 0)

    @pl.when(jnp.logical_not(upper) | late)
    def _():
        request_row(1, 0)

    up = lax.rem(me + 1, count)
    down = lax.rem(me + count - 1, count)

    def halo(k):
        if k < 2:
            src = feat_hbm.at[:, pl.ds((EDGE - 1) * FACE, FACE), :] if k == 0 else occ_hbm
            dst = low_layer if k == 0 else low_occ
            peer = up
        else:
            src = feat_hbm.at[:, pl.ds(0, FACE), :] if k == 2 else occ_hbm
            dst = high_layer if k == 2 else high_occ
            peer = down
        return pltpu.make_async_remote_copy(
            src_ref=src,
            dst_ref=dst,
            send_sem=halo_send.at[k],
            recv_sem=halo_recv.at[k],
            device_id={"blk": peer},
            device_id_type=MESH,
        )

    edge = me == last_row - 1

    @pl.when((me < count - 1) & jnp.logical_not(edge))
    def _():
        halo(0).start()
        halo(1).start()

    @pl.when(me > 0)
    def _():
        halo(2).start()
        halo(3).start()

    @pl.when(jnp.logical_not(late))
    def _():
        pl.semaphore_wait(late_sem, row)

    @pl.when(jnp.logical_not(upper))
    def _():
        request_row(1, 1)

    @pl.when(upper & jnp.logical_not(late))
    def _():
        request_row(1, 0)

    @pl.when(edge)
    def _():
        halo(0).start()
        halo(1).start()

    @pl.when(me == 0)
    def _():
        low_layer[...] = jnp.zeros_like(low_layer)
        low_occ[...] = jnp.zeros_like(low_occ)

    @pl.when(me == count - 1)
    def _():
        high_layer[...] = jnp.zeros_like(high_layer)
        high_occ[...] = jnp.zeros_like(high_occ)

    loads[0].wait()
    loads[1].wait()

    blocks = layer_rows // VOX
    for s in range(0, slots, blocks):
        rows = prev[s : s + blocks].reshape(layer_rows, channels)
        part = jnp.dot(rows, pweight[...], preferred_element_type=F32).astype(BF16)
        proj[s : s + blocks] = part.reshape(blocks, VOX, channels)

    near_reqs[half_at] = table[...]

    def first_to(at, far):
        return pltpu.make_async_remote_copy(
            src_ref=send_first.at[far * half + at],
            dst_ref=recv.at[me],
            send_sem=first_send.at[far * half + at],
            recv_sem=first_recv.at[far * half + half_at],
            device_id={"blk": (other_half if far else half_base) + at},
            device_id_type=MESH,
        )

    def first_from(at, far):
        return pltpu.make_async_remote_copy(
            src_ref=send_first.at[far * half + at],
            dst_ref=recv.at[(other_half if far else half_base) + at],
            send_sem=first_send.at[far * half + at],
            recv_sem=first_recv.at[far * half + at],
            device_id={"blk": (other_half if far else half_base) + at},
            device_id_type=MESH,
        )

    def row_to(i):
        return pltpu.make_async_remote_copy(
            src_ref=send_row.at[i],
            dst_ref=recv.at[row_part + row_at],
            send_sem=row_send.at[i],
            recv_sem=row_recv.at[i],
            device_id={"blk": in_row(i)},
            device_id_type=MESH,
        )

    def z_to(i):
        return pltpu.make_async_remote_copy(
            src_ref=send_z.at[i],
            dst_ref=relay_z.at[row_at],
            send_sem=z_send.at[i],
            recv_sem=z_recv.at[i],
            device_id={"blk": in_row(i)},
            device_id_type=MESH,
        )

    def x_to(at):
        return pltpu.make_async_remote_copy(
            src_ref=send_x.at[at],
            dst_ref=relay_x.at[half_at],
            send_sem=x_send.at[at],
            recv_sem=x_recv.at[half_at],
            device_id={"blk": half_base + at},
            device_id_type=MESH,
        )

    def x_from(at):
        return pltpu.make_async_remote_copy(
            src_ref=send_x.at[at],
            dst_ref=relay_x.at[at],
            send_sem=x_send.at[at],
            recv_sem=x_recv.at[at],
            device_id={"blk": half_base + at},
            device_id_type=MESH,
        )

    def relay(k):
        part, peer = ((x_part, across), (z_part, beside))[k]
        return pltpu.make_async_remote_copy(
            src_ref=relay_out.at[pl.ds(k * EXTRA, EXTRA)],
            dst_ref=recv.at[pl.ds(part, EXTRA)],
            send_sem=out_send.at[k],
            recv_sem=out_recv.at[k],
            device_id={"blk": peer},
            device_id_type=MESH,
        )

    def over_to(i):
        return pltpu.make_async_remote_copy(
            src_ref=over,
            dst_ref=overs.at[grp],
            send_sem=over_send.at[i],
            recv_sem=over_recv.at[i],
            device_id={"grp": lax.rem(grp + i, groups)},
            device_id_type=MESH,
        )

    def near_entry(peer, at):
        return jnp.sum(jnp.where(lane == at, near_reqs[peer - half_base], 0))

    def far_entry(peer, at):
        return jnp.sum(jnp.where(lane == at, far_reqs[peer - other_half], 0))

    def send_far(at):
        send_first[half + at] = proj[first_s[other_half + at]]
        first_to(at, 1).start()

    def send_across(at):
        send_x[at] = proj[last_s[other_half + at]]
        x_to(at).start()

    def send_near(at):
        send_first[at] = proj[first_s[half_base + at]]
        first_to(at, 0).start()

    def send_beside(i):
        send_z[i] = proj[last_s[other_row + lax.rem(row_at + i, row)]]
        z_to(i).start()

    def send_second(i):
        send_row[i] = proj[last_s[in_row(i)]]
        row_to(i).start()

    def others(body):
        @pl.loop(1, half)
        def _(i):
            body(lax.rem(half_at + i, half))

    for part in range(2):

        @pl.loop(0, row)
        def _(i):
            request_from(part * row + i, 1).wait_recv()

        for i in range(row):
            d = part * row + i
            wanted = far_entry(other_half + d, me)
            first_s[other_half + d] = wanted % PACK
            last_s[other_half + d] = wanted // PACK

        @pl.loop(0, row // 2)
        def _(i):
            send_far(turned(part, i))

        @pl.loop(0, row)
        def _(i):
            at = turned(part, i)

            @pl.when(at != half_at)
            def _():
                send_across(at)

        @pl.loop(row // 2, row)
        def _(i):
            send_far(turned(part, i))

    others(lambda at: request_from(at, 0).wait_recv())

    for d in range(half):
        wanted = near_entry(half_base + d, me)
        first_s[half_base + d] = wanted % PACK
        last_s[half_base + d] = wanted // PACK

    @pl.loop(1, row)
    def _(i):
        send_beside(i)

    others(send_near)

    @pl.loop(1, row)
    def _(i):
        send_second(i)

    recv[me] = proj[first_s[me]]
    recv[row_part + row_at] = proj[last_s[me]]
    relay_x[half_at] = proj[last_s[across]]
    relay_z[row_at] = proj[last_s[beside]]

    notes = near_reqs[...].reshape(half, LANES) + far_reqs[...].reshape(half, LANES)
    over[...] = jnp.sum(jnp.where(lane == count + 2 * EXTRA, notes, 0), axis=0, keepdims=True)
    for i in range(1, groups):
        over_to(i).start()

    for load in small[2:]:
        load.wait()
    occ = occ_ref[...].astype(BF16)
    volume[...] = jnp.zeros_like(volume)
    loads[2].wait()
    col = iota((layer_rows, layer_rows), 1)
    line = iota((layer_rows, layer_rows), 0)
    select_own = one_hot(col == (line % slots) * FACE + line // slots)
    spread = one_hot(iota((layer_rows, slots), 0) % slots == iota((layer_rows, slots), 1))
    nb = lax.dot_general(
        spread,
        nb_ref[...].astype(F32).astype(BF16),
        (((1,), (1,)), ((), ())),
        preferred_element_type=F32,
    ).astype(jnp.int32)
    side_rows = EDGE * slots
    scol = iota((side_rows, layer_rows), 1)
    sline = iota((side_rows, 1), 0) // slots

    def side(f, fixed, step):
        wanted = nb[:side_rows, f : f + 1]
        target = jnp.where(wanted >= 0, wanted * FACE + fixed + sline * step, -1)
        return one_hot(scol == target)

    sides = [
        side(2, (EDGE - 1) * EDGE, 1),
        side(3, 0, 1),
        side(4, EDGE - 1, EDGE),
        side(5, 0, EDGE),
    ]
    select = jnp.concatenate([select_own] + sides, axis=0)
    for x in range(EDGE):
        layer = feat[:, x * FACE : (x + 1) * FACE, :].reshape(layer_rows, channels)
        part = jnp.dot(select * layer_occ(occ, x), layer, preferred_element_type=F32).astype(BF16)
        volume[x + 1, 1 : EDGE + 1, 1 : EDGE + 1] = part[:layer_rows].reshape(
            EDGE, EDGE, slots, channels
        )
        faces = part[layer_rows:].reshape(4, EDGE, slots, channels)
        volume[x + 1, 0, 1 : EDGE + 1] = faces[0]
        volume[x + 1, EDGE + 1, 1 : EDGE + 1] = faces[1]
        volume[x + 1, 1 : EDGE + 1, 0] = faces[2]
        volume[x + 1, 1 : EDGE + 1, EDGE + 1] = faces[3]

    @pl.when(me > 0)
    def _():
        pltpu.make_async_remote_copy(
            src_ref=feat_hbm.at[:, pl.ds(0, FACE), :],
            dst_ref=low_layer,
            send_sem=halo_send.at[0],
            recv_sem=halo_recv.at[0],
            device_id={"blk": up},
            device_id_type=MESH,
        ).wait_recv()
        halo(1).wait_recv()

    @pl.when(me < count - 1)
    def _():
        halo(2).wait_recv()
        halo(3).wait_recv()

    def x_face(f, layer_ref, other_occ, x):
        wanted = nb[:, f : f + 1]
        target = jnp.where(wanted >= 0, wanted * FACE + iota((layer_rows, 1), 0) // slots, -1)
        pick = one_hot(col == target) * layer_occ(other_occ[...].astype(BF16), x)
        layer = layer_ref[...].reshape(layer_rows, channels)
        part = jnp.dot(pick, layer, preferred_element_type=F32).astype(BF16)
        return part.reshape(EDGE, EDGE, slots, channels)

    volume[0, 1 : EDGE + 1, 1 : EDGE + 1] = x_face(0, low_layer, low_occ, EDGE - 1)
    volume[EDGE + 1, 1 : EDGE + 1, 1 : EDGE + 1] = x_face(1, high_layer, high_occ, 0)

    loads[3].wait()
    scale = scale_ref[...]
    shift = shift_ref[...]

    @pl.loop(0, 2)
    def _(x):
        total = jnp.zeros((layer_rows, channels), F32)
        for tap in range(27):
            a, b, c = tap // 9, (tap // 3) % 3, tap % 3
            window = volume[x + a, b : b + EDGE, c : c + EDGE].reshape(layer_rows, channels)
            total = total + jnp.dot(window, weight[tap], preferred_element_type=F32)
        hidden = jnp.maximum(total * scale + shift, 0.0)
        for k in range(channels // LANES):
            acc[k, pl.ds(x * layer_rows, layer_rows), :] = hidden[:, k * LANES : (k + 1) * LANES]

    others(lambda at: x_from(at).wait_recv())

    for e in range(EXTRA):
        relay_out[e] = relay_x[far_entry(across, count + e)]
    relay(0).start()

    @pl.loop(2, EDGE)
    def _(x):
        total = jnp.zeros((layer_rows, channels), F32)
        for tap in range(27):
            a, b, c = tap // 9, (tap // 3) % 3, tap % 3
            window = volume[x + a, b : b + EDGE, c : c + EDGE].reshape(layer_rows, channels)
            total = total + jnp.dot(window, weight[tap], preferred_element_type=F32)
        hidden = jnp.maximum(total * scale + shift, 0.0)
        for k in range(channels // LANES):
            acc[k, pl.ds(x * layer_rows, layer_rows), :] = hidden[:, k * LANES : (k + 1) * LANES]

    @pl.loop(1, row)
    def _(i):
        z_to(i).wait_recv()

    for e in range(EXTRA):
        relay_out[EXTRA + e] = relay_z[near_entry(beside, count + EXTRA + e)]
    relay(1).start()

    @pl.loop(0, slots)
    def _(s):
        mine = jnp.where(iota((VOX, VOX), 0) == iota((VOX, VOX), 1), occ_ref[pl.ds(s, 1), :], 0)
        mask[pl.ds(s * VOX, VOX), :] = jnp.dot(
            mine.astype(BF16), jnp.ones((VOX, channels), BF16), preferred_element_type=F32
        )

    for s in range(slots):
        hidden = jnp.concatenate(
            [acc[k, pl.ds(s, VOX, stride=slots), :] for k in range(channels // LANES)],
            axis=1,
        )
        base[s] = hidden * mask[s * VOX : (s + 1) * VOX, :]

    overs[grp] = over[...]
    for i in range(1, groups):
        over_to(i).wait_recv()
    over_ref[0] = jnp.sum(overs[...])

    @pl.loop(0, half)
    def _(i):
        request(i, 1).wait_send()
        first_to(i, 1).wait_send()

    others(lambda at: request(at, 0).wait_send())
    others(lambda at: first_to(at, 0).wait_send())

    others(lambda at: x_to(at).wait_send())

    @pl.loop(1, row)
    def _(i):
        row_to(i).wait_send()
        z_to(i).wait_send()

    relay(0).wait_send()
    relay(1).wait_send()
    for i in range(1, groups):
        over_to(i).wait_send()

    @pl.when(me < count - 1)
    def _():
        halo(0).wait_send()
        halo(1).wait_send()

    @pl.when(me > 0)
    def _():
        halo(2).wait_send()
        halo(3).wait_send()

    @pl.loop(0, half)
    def _(i):
        first_from(i, 1).wait_recv()

    others(lambda at: first_from(at, 0).wait_recv())

    @pl.loop(1, row)
    def _(i):
        row_to(i).wait_recv()

    relay(0).wait_recv()
    relay(1).wait_recv()

    for s in range(slots):
        moved = recv[place_s[s]].astype(F32)
        out_ref[s] = (base[s] + moved * mask[s * VOX : (s + 1) * VOX, :]).astype(BF16)


def per_device(
    features,
    occupancy,
    neighbors,
    previous,
    old_owner,
    old_slot,
    conv_weight,
    norm_scale,
    norm_shift,
    prev_weight,
):
    slots, vox, channels = features.shape
    count = lax.axis_size("blk")
    groups = lax.axis_size("grp")
    half, row = count // 2, count // 4
    hbm = pl.BlockSpec(memory_space=pl.ANY)
    volume_shape = (EDGE + 2, EDGE + 2, EDGE + 2, slots, channels)
    dma = pltpu.SemaphoreType.DMA
    return pl.pallas_call(
        functools.partial(kernel, count, groups, slots, channels),
        out_shape=[
            pltpu.VMEM(features.shape, BF16),
            pltpu.SMEM((1,), jnp.int32),
        ],
        in_specs=[hbm] * 10,
        out_specs=[
            pl.BlockSpec(memory_space=pltpu.VMEM),
            pl.BlockSpec(memory_space=pltpu.SMEM),
        ],
        scratch_shapes=[
            pltpu.SMEM((slots,), jnp.int32),
            pltpu.SMEM((slots,), jnp.int32),
            pltpu.VMEM((6, slots), jnp.int32),
            pltpu.VMEM((slots, vox), jnp.int32),
            pltpu.VMEM((1, channels), F32),
            pltpu.VMEM((1, channels), F32),
            pltpu.VMEM(features.shape, BF16),
            pltpu.VMEM(previous.shape, BF16),
            pltpu.VMEM(conv_weight.shape, BF16),
            pltpu.VMEM(prev_weight.shape, BF16),
            pltpu.VMEM(previous.shape, BF16),
            pltpu.VMEM((1, LANES), jnp.int32),
            pltpu.VMEM((half, 1, LANES), jnp.int32),
            pltpu.VMEM((half, 1, LANES), jnp.int32),
            pltpu.SMEM((count,), jnp.int32),
            pltpu.SMEM((count,), jnp.int32),
            pltpu.SMEM((slots,), jnp.int32),
            pltpu.VMEM((1, LANES), jnp.int32),
            pltpu.VMEM((groups, 1, LANES), jnp.int32),
            pltpu.VMEM((count, vox, channels), BF16),
            pltpu.VMEM((row, vox, channels), BF16),
            pltpu.VMEM((row, vox, channels), BF16),
            pltpu.VMEM((half, vox, channels), BF16),
            pltpu.VMEM((row, vox, channels), BF16),
            pltpu.VMEM((half, vox, channels), BF16),
            pltpu.VMEM((2 * EXTRA, vox, channels), BF16),
            pltpu.VMEM((count + row + 2 * EXTRA, vox, channels), BF16),
            pltpu.VMEM((slots, FACE, channels), BF16),
            pltpu.VMEM((slots, FACE, channels), BF16),
            pltpu.VMEM((slots, vox), jnp.int32),
            pltpu.VMEM((slots, vox), jnp.int32),
            pltpu.VMEM(volume_shape, BF16),
            pltpu.VMEM((channels // LANES, slots * vox, LANES), F32),
            pltpu.VMEM((slots * vox, channels), F32),
            pltpu.VMEM(features.shape, F32),
            dma((6,)),
            dma((6,)),
            dma((4,)),
            dma((4,)),
            dma((count,)),
            dma((count,)),
            dma((count,)),
            dma((count,)),
            dma((row,)),
            dma((row,)),
            dma((row,)),
            dma((row,)),
            dma((half,)),
            dma((half,)),
            dma((2,)),
            dma((2,)),
            pltpu.SemaphoreType.REGULAR,
            dma((groups,)),
            dma((groups,)),
        ],
        compiler_params=pltpu.CompilerParams(
            collective_id=0, has_side_effects=True, vmem_limit_bytes=66_000_000
        ),
        name="merge_blocks",
    )(
        old_owner[:, 0],
        old_slot,
        neighbors.T,
        norm_scale[None, :],
        norm_shift[None, :],
        features,
        previous,
        occupancy,
        conv_weight,
        prev_weight,
    )


def merge(*arrays):
    merged, over = per_device(*arrays)
    return lax.switch(over[0], [lambda: merged, lambda: merge_full(*arrays)])


def solution(mesh):
    in_specs = (
        P(("grp", "blk"), None, None),
        P(("grp", "blk"), None),
        P(("grp", "blk"), None),
        P(("grp", "blk"), None, None),
        P(("grp", "blk"), None),
        P(("grp", "blk")),
        P(),
        P(),
        P(),
        P(),
    )
    out_specs = P(("grp", "blk"), None, None)
    return jax.shard_map(
        merge, mesh=mesh, in_specs=in_specs, out_specs=out_specs, check_vma=False
    )
```

```python
import functools

import jax
import jax.numpy as jnp
from jax import lax
from jax.experimental import pallas as pl
from jax.experimental.pallas import tpu as pltpu
from jax.sharding import PartitionSpec as P

EDGE = 4
FACE = EDGE * EDGE
VOX = EDGE * FACE
CAP = 2
LANES = 128
EXTRA = 2
PACK = 1 << 16
MESH = pl.DeviceIdType.MESH
F32 = jnp.float32
BF16 = jnp.bfloat16


def iota(shape, dim):
    return lax.broadcasted_iota(jnp.int32, shape, dim)


def one_hot(hit):
    return jnp.where(hit, 1.0, 0.0).astype(BF16)


def kernel_full(
    count,
    slots,
    channels,
    owner_hbm,
    slot_hbm,
    nb_hbm,
    scale_hbm,
    shift_hbm,
    feat_hbm,
    prev_hbm,
    occ_hbm,
    w_hbm,
    pw_hbm,
    out_ref,
    owner_s,
    slot_s,
    nb_ref,
    occ_ref,
    scale_ref,
    shift_ref,
    feat,
    prev,
    weight,
    pweight,
    proj,
    table,
    reqs,
    reqs_s,
    sendbuf,
    recv,
    low_layer,
    high_layer,
    low_occ,
    high_occ,
    volume,
    acc,
    mask,
    base,
    small_sem,
    local_sem,
    halo_send,
    halo_recv,
    rq_send,
    rq_recv,
    rp_send,
    rp_recv,
):
    me = lax.axis_index("blk")
    layer_rows = FACE * slots
    barrier = pltpu.get_barrier_semaphore()

    @pl.loop(1, count)
    def _(i):
        peer = lax.rem(me + i, count)
        pl.semaphore_signal(barrier, inc=1, device_id={"blk": peer}, device_id_type=MESH)

    small = [
        pltpu.make_async_copy(owner_hbm, owner_s, small_sem.at[0]),
        pltpu.make_async_copy(slot_hbm, slot_s, small_sem.at[1]),
        pltpu.make_async_copy(occ_hbm, occ_ref, small_sem.at[2]),
        pltpu.make_async_copy(nb_hbm, nb_ref, small_sem.at[3]),
        pltpu.make_async_copy(scale_hbm, scale_ref, small_sem.at[4]),
        pltpu.make_async_copy(shift_hbm, shift_ref, small_sem.at[5]),
    ]
    for load in small:
        load.start()
    loads = [
        pltpu.make_async_copy(prev_hbm, prev, local_sem.at[0]),
        pltpu.make_async_copy(pw_hbm, pweight, local_sem.at[1]),
        pltpu.make_async_copy(feat_hbm, feat, local_sem.at[2]),
        pltpu.make_async_copy(w_hbm, weight, local_sem.at[3]),
    ]
    for load in loads:
        load.start()

    small[0].wait()
    small[1].wait()

    lane = iota((1, LANES), 1)
    first = jnp.zeros((1, LANES), jnp.int32)
    last = jnp.zeros((1, LANES), jnp.int32)
    for s in range(slots):
        last = jnp.where(lane == owner_s[s], slot_s[s], last)
        t = slots - 1 - s
        first = jnp.where(lane == owner_s[t], slot_s[t], first)
    row = iota((CAP, LANES), 0)
    table[...] = jnp.where(row == 0, first, last)

    def layer_occ(occ, x):
        spread = one_hot(iota((VOX, layer_rows), 0) == x * FACE + iota((VOX, layer_rows), 1) % FACE)
        rows = jnp.dot(occ, spread, preferred_element_type=F32)
        own = iota((slots, layer_rows), 0) == iota((slots, layer_rows), 1) // FACE
        return jnp.sum(jnp.where(own, rows, 0.0), axis=0, keepdims=True).astype(BF16)

    pl.semaphore_wait(barrier, count - 1)

    def request(i):
        return pltpu.make_async_remote_copy(
            src_ref=table,
            dst_ref=reqs.at[me],
            send_sem=rq_send.at[i],
            recv_sem=rq_recv.at[i],
            device_id={"blk": lax.rem(me + i, count)},
            device_id_type=MESH,
        )

    @pl.loop(1, count)
    def _(i):
        request(i).start()

    up = lax.rem(me + 1, count)
    down = lax.rem(me + count - 1, count)

    def halo(k):
        if k < 2:
            src = feat_hbm.at[:, pl.ds((EDGE - 1) * FACE, FACE), :] if k == 0 else occ_hbm
            dst = low_layer if k == 0 else low_occ
            peer = up
        else:
            src = feat_hbm.at[:, pl.ds(0, FACE), :] if k == 2 else occ_hbm
            dst = high_layer if k == 2 else high_occ
            peer = down
        return pltpu.make_async_remote_copy(
            src_ref=src,
            dst_ref=dst,
            send_sem=halo_send.at[k],
            recv_sem=halo_recv.at[k],
            device_id={"blk": peer},
            device_id_type=MESH,
        )

    @pl.when(me < count - 1)
    def _():
        halo(0).start()
        halo(1).start()

    @pl.when(me > 0)
    def _():
        halo(2).start()
        halo(3).start()

    @pl.when(me == 0)
    def _():
        low_layer[...] = jnp.zeros_like(low_layer)
        low_occ[...] = jnp.zeros_like(low_occ)

    @pl.when(me == count - 1)
    def _():
        high_layer[...] = jnp.zeros_like(high_layer)
        high_occ[...] = jnp.zeros_like(high_occ)

    loads[0].wait()
    loads[1].wait()

    blocks = layer_rows // VOX
    for s in range(0, slots, blocks):
        rows = prev[s : s + blocks].reshape(layer_rows, channels)
        part = jnp.dot(rows, pweight[...], preferred_element_type=F32).astype(BF16)
        proj[s : s + blocks] = part.reshape(blocks, VOX, channels)

    reqs_s_copy = pltpu.make_async_copy(reqs, reqs_s, local_sem.at[4])

    def reply(i):
        return pltpu.make_async_remote_copy(
            src_ref=sendbuf.at[i],
            dst_ref=recv.at[me],
            send_sem=rp_send.at[i],
            recv_sem=rp_recv.at[i],
            device_id={"blk": lax.rem(me + i, count)},
            device_id_type=MESH,
        )

    reqs[me] = table[...]

    @pl.loop(1, count)
    def _(i):
        request(i).wait_recv()

    reqs_s_copy.start()
    reqs_s_copy.wait()

    def far_first(k):
        step = (k + 1) // 2
        return count // 2 + step * (2 * (k % 2) - 1)

    @pl.loop(0, count - 1)
    def _(k):
        i = far_first(k)
        peer = lax.rem(me + i, count)
        sendbuf[i, 0] = proj[reqs_s[peer, 0, me]]
        sendbuf[i, 1] = proj[reqs_s[peer, 1, me]]

    @pl.loop(0, count - 1)
    def _(k):
        reply(far_first(k)).start()

    recv[me, 0] = proj[reqs_s[me, 0, me]]
    recv[me, 1] = proj[reqs_s[me, 1, me]]

    for load in small[2:]:
        load.wait()
    occ = occ_ref[...].astype(BF16)
    volume[...] = jnp.zeros_like(volume)
    loads[2].wait()
    col = iota((layer_rows, layer_rows), 1)
    line = iota((layer_rows, layer_rows), 0)
    select_own = one_hot(col == (line % slots) * FACE + line // slots)
    spread = one_hot(iota((layer_rows, slots), 0) % slots == iota((layer_rows, slots), 1))
    nb = lax.dot_general(
        spread,
        nb_ref[...].astype(F32).astype(BF16),
        (((1,), (1,)), ((), ())),
        preferred_element_type=F32,
    ).astype(jnp.int32)
    side_rows = EDGE * slots
    scol = iota((side_rows, layer_rows), 1)
    sline = iota((side_rows, 1), 0) // slots

    def side(f, fixed, step):
        wanted = nb[:side_rows, f : f + 1]
        target = jnp.where(wanted >= 0, wanted * FACE + fixed + sline * step, -1)
        return one_hot(scol == target)

    sides = [
        side(2, (EDGE - 1) * EDGE, 1),
        side(3, 0, 1),
        side(4, EDGE - 1, EDGE),
        side(5, 0, EDGE),
    ]
    select = jnp.concatenate([select_own] + sides, axis=0)
    for x in range(EDGE):
        layer = feat[:, x * FACE : (x + 1) * FACE, :].reshape(layer_rows, channels)
        part = jnp.dot(select * layer_occ(occ, x), layer, preferred_element_type=F32).astype(BF16)
        volume[x + 1, 1 : EDGE + 1, 1 : EDGE + 1] = part[:layer_rows].reshape(
            EDGE, EDGE, slots, channels
        )
        faces = part[layer_rows:].reshape(4, EDGE, slots, channels)
        volume[x + 1, 0, 1 : EDGE + 1] = faces[0]
        volume[x + 1, EDGE + 1, 1 : EDGE + 1] = faces[1]
        volume[x + 1, 1 : EDGE + 1, 0] = faces[2]
        volume[x + 1, 1 : EDGE + 1, EDGE + 1] = faces[3]

    @pl.when(me > 0)
    def _():
        pltpu.make_async_remote_copy(
            src_ref=feat_hbm.at[:, pl.ds(0, FACE), :],
            dst_ref=low_layer,
            send_sem=halo_send.at[0],
            recv_sem=halo_recv.at[0],
            device_id={"blk": up},
            device_id_type=MESH,
        ).wait_recv()
        halo(1).wait_recv()

    @pl.when(me < count - 1)
    def _():
        halo(2).wait_recv()
        halo(3).wait_recv()

    def x_face(f, layer_ref, other_occ, x):
        wanted = nb[:, f : f + 1]
        target = jnp.where(wanted >= 0, wanted * FACE + iota((layer_rows, 1), 0) // slots, -1)
        pick = one_hot(col == target) * layer_occ(other_occ[...].astype(BF16), x)
        layer = layer_ref[...].reshape(layer_rows, channels)
        part = jnp.dot(pick, layer, preferred_element_type=F32).astype(BF16)
        return part.reshape(EDGE, EDGE, slots, channels)

    volume[0, 1 : EDGE + 1, 1 : EDGE + 1] = x_face(0, low_layer, low_occ, EDGE - 1)
    volume[EDGE + 1, 1 : EDGE + 1, 1 : EDGE + 1] = x_face(1, high_layer, high_occ, 0)

    loads[3].wait()
    scale = scale_ref[...]
    shift = shift_ref[...]

    @pl.loop(0, EDGE)
    def _(x):
        total = jnp.zeros((layer_rows, channels), F32)
        for tap in range(27):
            a, b, c = tap // 9, (tap // 3) % 3, tap % 3
            window = volume[x + a, b : b + EDGE, c : c + EDGE].reshape(layer_rows, channels)
            total = total + jnp.dot(window, weight[tap], preferred_element_type=F32)
        hidden = jnp.maximum(total * scale + shift, 0.0)
        for k in range(channels // LANES):
            acc[k, pl.ds(x * layer_rows, layer_rows), :] = hidden[:, k * LANES : (k + 1) * LANES]

    @pl.loop(0, slots)
    def _(s):
        mine = jnp.where(iota((VOX, VOX), 0) == iota((VOX, VOX), 1), occ_ref[pl.ds(s, 1), :], 0)
        mask[pl.ds(s * VOX, VOX), :] = jnp.dot(
            mine.astype(BF16), jnp.ones((VOX, channels), BF16), preferred_element_type=F32
        )

    picks = []
    for s in range(slots):
        rank = jnp.int32(0)
        for t in range(s):
            rank = jnp.where(owner_s[t] == owner_s[s], 1, rank)
        picks.append(rank)
        hidden = jnp.concatenate(
            [acc[k, pl.ds(s, VOX, stride=slots), :] for k in range(channels // LANES)],
            axis=1,
        )
        base[s] = hidden * mask[s * VOX : (s + 1) * VOX, :]

    @pl.loop(1, count)
    def _(i):
        reply(i).wait_recv()

    for s in range(slots):
        moved = recv[owner_s[s], picks[s]].astype(F32)
        out_ref[s] = (base[s] + moved * mask[s * VOX : (s + 1) * VOX, :]).astype(BF16)

    @pl.loop(1, count)
    def _(i):
        request(i).wait_send()
        reply(i).wait_send()

    @pl.when(me < count - 1)
    def _():
        halo(0).wait_send()
        halo(1).wait_send()

    @pl.when(me > 0)
    def _():
        halo(2).wait_send()
        halo(3).wait_send()


def merge_full(
    features,
    occupancy,
    neighbors,
    previous,
    old_owner,
    old_slot,
    conv_weight,
    norm_scale,
    norm_shift,
    prev_weight,
):
    slots, vox, channels = features.shape
    count = lax.axis_size("blk")
    hbm = pl.BlockSpec(memory_space=pl.ANY)
    volume_shape = (EDGE + 2, EDGE + 2, EDGE + 2, slots, channels)
    dma = pltpu.SemaphoreType.DMA
    return pl.pallas_call(
        functools.partial(kernel_full, count, slots, channels),
        out_shape=pltpu.VMEM(features.shape, BF16),
        in_specs=[hbm] * 10,
        out_specs=pl.BlockSpec(memory_space=pltpu.VMEM),
        scratch_shapes=[
            pltpu.SMEM((slots,), jnp.int32),
            pltpu.SMEM((slots,), jnp.int32),
            pltpu.VMEM((6, slots), jnp.int32),
            pltpu.VMEM((slots, vox), jnp.int32),
            pltpu.VMEM((1, channels), F32),
            pltpu.VMEM((1, channels), F32),
            pltpu.VMEM(features.shape, BF16),
            pltpu.VMEM(previous.shape, BF16),
            pltpu.VMEM(conv_weight.shape, BF16),
            pltpu.VMEM(prev_weight.shape, BF16),
            pltpu.VMEM(previous.shape, BF16),
            pltpu.VMEM((CAP, LANES), jnp.int32),
            pltpu.VMEM((count, CAP, LANES), jnp.int32),
            pltpu.SMEM((count, CAP, LANES), jnp.int32),
            pltpu.VMEM((count, CAP, vox, channels), BF16),
            pltpu.VMEM((count, CAP, vox, channels), BF16),
            pltpu.VMEM((slots, FACE, channels), BF16),
            pltpu.VMEM((slots, FACE, channels), BF16),
            pltpu.VMEM((slots, vox), jnp.int32),
            pltpu.VMEM((slots, vox), jnp.int32),
            pltpu.VMEM(volume_shape, BF16),
            pltpu.VMEM((channels // LANES, slots * vox, LANES), F32),
            pltpu.VMEM((slots * vox, channels), F32),
            pltpu.VMEM(features.shape, F32),
            dma((6,)),
            dma((6,)),
            dma((4,)),
            dma((4,)),
            dma((count,)),
            dma((count,)),
            dma((count,)),
            dma((count,)),
        ],
        compiler_params=pltpu.CompilerParams(
            collective_id=1, has_side_effects=True, vmem_limit_bytes=66_000_000
        ),
        name="merge_full",
    )(
        old_owner[:, 0],
        old_slot,
        neighbors.T,
        norm_scale[None, :],
        norm_shift[None, :],
        features,
        previous,
        occupancy,
        conv_weight,
        prev_weight,
    )


def kernel(
    count,
    groups,
    slots,
    channels,
    owner_hbm,
    slot_hbm,
    nb_hbm,
    scale_hbm,
    shift_hbm,
    feat_hbm,
    prev_hbm,
    occ_hbm,
    w_hbm,
    pw_hbm,
    out_ref,
    over_ref,
    owner_s,
    slot_s,
    nb_ref,
    occ_ref,
    scale_ref,
    shift_ref,
    feat,
    prev,
    weight,
    pweight,
    proj,
    table,
    near_reqs,
    far_reqs,
    first_s,
    last_s,
    place_s,
    over,
    overs,
    send_first,
    send_row,
    send_z,
    send_x,
    relay_z,
    relay_x,
    relay_out,
    recv,
    low_layer,
    high_layer,
    low_occ,
    high_occ,
    volume,
    acc,
    mask,
    base,
    small_sem,
    local_sem,
    halo_send,
    halo_recv,
    rq_send,
    rq_recv,
    first_send,
    first_recv,
    row_send,
    row_recv,
    z_send,
    z_recv,
    x_send,
    x_recv,
    out_send,
    out_recv,
    late_sem,
    over_send,
    over_recv,
):
    me = lax.axis_index("blk")
    grp = lax.axis_index("grp")
    half, row = count // 2, count // 4
    half_base = me // half * half
    row_base = me // row * row
    half_at, row_at = me - half_base, me - row_base
    other_half = half - half_base
    other_row = 2 * half_base + row - row_base
    across = lax.rem(me + half, count)
    beside = other_row + row_at
    row_part, z_part, x_part = count, count + row, count + row + EXTRA
    layer_rows = FACE * slots
    barrier = pltpu.get_barrier_semaphore()

    upper = half_base > 0
    last_row = count - row
    late = me >= last_row

    def hello(peer):
        pl.semaphore_signal(barrier, inc=1, device_id={"blk": peer}, device_id_type=MESH)

    @pl.when(jnp.logical_not(late))
    def _():
        @pl.loop(1, count)
        def _(i):
            hello(lax.rem(me + i, count))

    @pl.when(late)
    def _():
        @pl.loop(1, row)
        def _(i):
            hello(row_base + lax.rem(row_at + i, row))

    for i in range(1, groups):
        there = lax.rem(grp + i, groups)
        pl.semaphore_signal(barrier, inc=1, device_id={"grp": there}, device_id_type=MESH)

    small = [
        pltpu.make_async_copy(owner_hbm, owner_s, small_sem.at[0]),
        pltpu.make_async_copy(slot_hbm, slot_s, small_sem.at[1]),
        pltpu.make_async_copy(occ_hbm, occ_ref, small_sem.at[2]),
        pltpu.make_async_copy(nb_hbm, nb_ref, small_sem.at[3]),
        pltpu.make_async_copy(scale_hbm, scale_ref, small_sem.at[4]),
        pltpu.make_async_copy(shift_hbm, shift_ref, small_sem.at[5]),
    ]
    for load in small:
        load.start()
    loads = [
        pltpu.make_async_copy(prev_hbm, prev, local_sem.at[0]),
        pltpu.make_async_copy(pw_hbm, pweight, local_sem.at[1]),
        pltpu.make_async_copy(feat_hbm, feat, local_sem.at[2]),
        pltpu.make_async_copy(w_hbm, weight, local_sem.at[3]),
    ]
    for load in loads:
        load.start()

    small[0].wait()
    small[1].wait()

    lane = iota((1, LANES), 1)
    first = jnp.zeros((1, LANES), jnp.int32)
    last = jnp.zeros((1, LANES), jnp.int32)
    for s in range(slots):
        last = jnp.where(lane == owner_s[s], slot_s[s], last)
        t = slots - 1 - s
        first = jnp.where(lane == owner_s[t], slot_s[t], first)
    zero = jnp.int32(0)
    x_count, z_count = zero, zero
    x_owner, z_owner = [zero] * EXTRA, [zero] * EXTRA
    for s in range(slots):
        owner = owner_s[s]
        again = zero
        for t in range(s):
            again = jnp.where(owner_s[t] == owner, 1, again)
        far = jnp.where((owner < half_base) | (owner >= half_base + half), again, 0)
        near = jnp.where((owner >= other_row) & (owner < other_row + row), again, 0)
        for e in range(EXTRA):
            x_owner[e] = jnp.where((far == 1) & (x_count == e), owner - other_half, x_owner[e])
            z_owner[e] = jnp.where((near == 1) & (z_count == e), owner - other_row, z_owner[e])
        at = jnp.where(again == 1, row_part + owner - row_base, owner)
        at = jnp.where(near == 1, z_part + jnp.minimum(z_count, EXTRA - 1), at)
        place_s[s] = jnp.where(far == 1, x_part + jnp.minimum(x_count, EXTRA - 1), at)
        x_count = x_count + far
        z_count = z_count + near
    notes = jnp.where(
        lane == count + 2 * EXTRA, jnp.where((x_count > EXTRA) | (z_count > EXTRA), 1, 0), first + last * PACK
    )
    for e in range(EXTRA):
        notes = jnp.where(lane == count + e, x_owner[e], notes)
        notes = jnp.where(lane == count + EXTRA + e, z_owner[e], notes)
    table[...] = notes

    def layer_occ(occ, x):
        spread = one_hot(iota((VOX, layer_rows), 0) == x * FACE + iota((VOX, layer_rows), 1) % FACE)
        rows = jnp.dot(occ, spread, preferred_element_type=F32)
        own = iota((slots, layer_rows), 0) == iota((slots, layer_rows), 1) // FACE
        return jnp.sum(jnp.where(own, rows, 0.0), axis=0, keepdims=True).astype(BF16)

    @pl.when(jnp.logical_not(late))
    def _():
        pl.semaphore_wait(barrier, count - row + groups - 2)

    @pl.when(late)
    def _():
        pl.semaphore_wait(barrier, count + groups - 2)

        @pl.loop(0, last_row)
        def _(i):
            pl.semaphore_signal(late_sem, inc=1, device_id={"blk": i}, device_id_type=MESH)

    def in_row(i):
        return row_base + lax.rem(row_at + i, row)

    def request(at, far):
        return pltpu.make_async_remote_copy(
            src_ref=table,
            dst_ref=(far_reqs if far else near_reqs).at[half_at],
            send_sem=rq_send.at[far * half + at],
            recv_sem=rq_recv.at[far * half + half_at],
            device_id={"blk": (other_half if far else half_base) + at},
            device_id_type=MESH,
        )

    def request_from(at, far):
        return pltpu.make_async_remote_copy(
            src_ref=table,
            dst_ref=(far_reqs if far else near_reqs).at[at],
            send_sem=rq_send.at[far * half + at],
            recv_sem=rq_recv.at[far * half + at],
            device_id={"blk": (other_half if far else half_base) + at},
            device_id_type=MESH,
        )

    def turned(part, i):
        return part * row + lax.rem(row_at + i, row)

    def request_row(part, far):
        @pl.loop(0, row)
        def _(i):
            at = turned(part, i)
            if far:
                request(at, far).start()
            else:

                @pl.when(at != half_at)
                def _():
                    request(at, far).start()

    request_row(0, 1)

    @pl.when(upper)
    def _():
        request_row(1, 1)

    request_row(0, 0)

    @pl.when(jnp.logical_not(upper) | late)
    def _():
        request_row(1, 0)

    up = lax.rem(me + 1, count)
    down = lax.rem(me + count - 1, count)

    def halo(k):
        if k < 2:
            src = feat_hbm.at[:, pl.ds((EDGE - 1) * FACE, FACE), :] if k == 0 else occ_hbm
            dst = low_layer if k == 0 else low_occ
            peer = up
        else:
            src = feat_hbm.at[:, pl.ds(0, FACE), :] if k == 2 else occ_hbm
            dst = high_layer if k == 2 else high_occ
            peer = down
        return pltpu.make_async_remote_copy(
            src_ref=src,
            dst_ref=dst,
            send_sem=halo_send.at[k],
            recv_sem=halo_recv.at[k],
            device_id={"blk": peer},
            device_id_type=MESH,
        )

    edge = me == last_row - 1

    @pl.when((me < count - 1) & jnp.logical_not(edge))
    def _():
        halo(0).start()
        halo(1).start()

    @pl.when(me > 0)
    def _():
        halo(2).start()
        halo(3).start()

    @pl.when(jnp.logical_not(late))
    def _():
        pl.semaphore_wait(late_sem, row)

    @pl.when(jnp.logical_not(upper))
    def _():
        request_row(1, 1)

    @pl.when(upper & jnp.logical_not(late))
    def _():
        request_row(1, 0)

    @pl.when(edge)
    def _():
        halo(0).start()
        halo(1).start()

    @pl.when(me == 0)
    def _():
        low_layer[...] = jnp.zeros_like(low_layer)
        low_occ[...] = jnp.zeros_like(low_occ)

    @pl.when(me == count - 1)
    def _():
        high_layer[...] = jnp.zeros_like(high_layer)
        high_occ[...] = jnp.zeros_like(high_occ)

    loads[0].wait()
    loads[1].wait()

    blocks = layer_rows // VOX
    for s in range(0, slots, blocks):
        rows = prev[s : s + blocks].reshape(layer_rows, channels)
        part = jnp.dot(rows, pweight[...], preferred_element_type=F32).astype(BF16)
        proj[s : s + blocks] = part.reshape(blocks, VOX, channels)

    near_reqs[half_at] = table[...]

    def first_to(at, far):
        return pltpu.make_async_remote_copy(
            src_ref=send_first.at[far * half + at],
            dst_ref=recv.at[me],
            send_sem=first_send.at[far * half + at],
            recv_sem=first_recv.at[far * half + half_at],
            device_id={"blk": (other_half if far else half_base) + at},
            device_id_type=MESH,
        )

    def first_from(at, far):
        return pltpu.make_async_remote_copy(
            src_ref=send_first.at[far * half + at],
            dst_ref=recv.at[(other_half if far else half_base) + at],
            send_sem=first_send.at[far * half + at],
            recv_sem=first_recv.at[far * half + at],
            device_id={"blk": (other_half if far else half_base) + at},
            device_id_type=MESH,
        )

    def row_to(i):
        return pltpu.make_async_remote_copy(
            src_ref=send_row.at[i],
            dst_ref=recv.at[row_part + row_at],
            send_sem=row_send.at[i],
            recv_sem=row_recv.at[i],
            device_id={"blk": in_row(i)},
            device_id_type=MESH,
        )

    def z_to(i):
        return pltpu.make_async_remote_copy(
            src_ref=send_z.at[i],
            dst_ref=relay_z.at[row_at],
            send_sem=z_send.at[i],
            recv_sem=z_recv.at[i],
            device_id={"blk": in_row(i)},
            device_id_type=MESH,
        )

    def x_to(at):
        return pltpu.make_async_remote_copy(
            src_ref=send_x.at[at],
            dst_ref=relay_x.at[half_at],
            send_sem=x_send.at[at],
            recv_sem=x_recv.at[half_at],
            device_id={"blk": half_base + at},
            device_id_type=MESH,
        )

    def x_from(at):
        return pltpu.make_async_remote_copy(
            src_ref=send_x.at[at],
            dst_ref=relay_x.at[at],
            send_sem=x_send.at[at],
            recv_sem=x_recv.at[at],
            device_id={"blk": half_base + at},
            device_id_type=MESH,
        )

    def relay(k):
        part, peer = ((x_part, across), (z_part, beside))[k // EXTRA]
        return pltpu.make_async_remote_copy(
            src_ref=relay_out.at[k],
            dst_ref=recv.at[part + k % EXTRA],
            send_sem=out_send.at[k],
            recv_sem=out_recv.at[k],
            device_id={"blk": peer},
            device_id_type=MESH,
        )

    def over_to(i):
        return pltpu.make_async_remote_copy(
            src_ref=over,
            dst_ref=overs.at[grp],
            send_sem=over_send.at[i],
            recv_sem=over_recv.at[i],
            device_id={"grp": lax.rem(grp + i, groups)},
            device_id_type=MESH,
        )

    def near_entry(peer, at):
        return jnp.sum(jnp.where(lane == at, near_reqs[peer - half_base], 0))

    def far_entry(peer, at):
        return jnp.sum(jnp.where(lane == at, far_reqs[peer - other_half], 0))

    def send_far(at):
        send_first[half + at] = proj[first_s[other_half + at]]
        first_to(at, 1).start()

    def send_across(at):
        send_x[at] = proj[last_s[other_half + at]]
        x_to(at).start()

    def send_near(at):
        send_first[at] = proj[first_s[half_base + at]]
        first_to(at, 0).start()

    def send_beside(i):
        send_z[i] = proj[last_s[other_row + lax.rem(row_at + i, row)]]
        z_to(i).start()

    def send_second(i):
        send_row[i] = proj[last_s[in_row(i)]]
        row_to(i).start()

    def others(body):
        @pl.loop(1, half)
        def _(i):
            body(lax.rem(half_at + i, half))

    for part in range(2):

        @pl.loop(0, row)
        def _(i):
            request_from(part * row + i, 1).wait_recv()

        for i in range(row):
            d = part * row + i
            wanted = far_entry(other_half + d, me)
            first_s[other_half + d] = wanted % PACK
            last_s[other_half + d] = wanted // PACK

        @pl.loop(0, row // 2)
        def _(i):
            send_far(turned(part, i))

        @pl.loop(0, row)
        def _(i):
            at = turned(part, i)

            @pl.when(at != half_at)
            def _():
                send_across(at)

        @pl.loop(row // 2, row)
        def _(i):
            send_far(turned(part, i))

    others(lambda at: request_from(at, 0).wait_recv())

    for d in range(half):
        wanted = near_entry(half_base + d, me)
        first_s[half_base + d] = wanted % PACK
        last_s[half_base + d] = wanted // PACK

    @pl.loop(1, row)
    def _(i):
        send_beside(i)

    others(send_near)

    @pl.loop(1, row)
    def _(i):
        send_second(i)

    recv[me] = proj[first_s[me]]
    recv[row_part + row_at] = proj[last_s[me]]
    relay_x[half_at] = proj[last_s[across]]
    relay_z[row_at] = proj[last_s[beside]]

    notes = near_reqs[...].reshape(half, LANES) + far_reqs[...].reshape(half, LANES)
    over[...] = jnp.sum(jnp.where(lane == count + 2 * EXTRA, notes, 0), axis=0, keepdims=True)
    for i in range(1, groups):
        over_to(i).start()

    for load in small[2:]:
        load.wait()
    occ = occ_ref[...].astype(BF16)
    volume[...] = jnp.zeros_like(volume)
    loads[2].wait()
    col = iota((layer_rows, layer_rows), 1)
    line = iota((layer_rows, layer_rows), 0)
    select_own = one_hot(col == (line % slots) * FACE + line // slots)
    spread = one_hot(iota((layer_rows, slots), 0) % slots == iota((layer_rows, slots), 1))
    nb = lax.dot_general(
        spread,
        nb_ref[...].astype(F32).astype(BF16),
        (((1,), (1,)), ((), ())),
        preferred_element_type=F32,
    ).astype(jnp.int32)
    side_rows = EDGE * slots
    scol = iota((side_rows, layer_rows), 1)
    sline = iota((side_rows, 1), 0) // slots

    def side(f, fixed, step):
        wanted = nb[:side_rows, f : f + 1]
        target = jnp.where(wanted >= 0, wanted * FACE + fixed + sline * step, -1)
        return one_hot(scol == target)

    sides = [
        side(2, (EDGE - 1) * EDGE, 1),
        side(3, 0, 1),
        side(4, EDGE - 1, EDGE),
        side(5, 0, EDGE),
    ]
    select = jnp.concatenate([select_own] + sides, axis=0)
    for x in range(EDGE):
        layer = feat[:, x * FACE : (x + 1) * FACE, :].reshape(layer_rows, channels)
        part = jnp.dot(select * layer_occ(occ, x), layer, preferred_element_type=F32).astype(BF16)
        volume[x + 1, 1 : EDGE + 1, 1 : EDGE + 1] = part[:layer_rows].reshape(
            EDGE, EDGE, slots, channels
        )
        faces = part[layer_rows:].reshape(4, EDGE, slots, channels)
        volume[x + 1, 0, 1 : EDGE + 1] = faces[0]
        volume[x + 1, EDGE + 1, 1 : EDGE + 1] = faces[1]
        volume[x + 1, 1 : EDGE + 1, 0] = faces[2]
        volume[x + 1, 1 : EDGE + 1, EDGE + 1] = faces[3]

    @pl.when(me > 0)
    def _():
        pltpu.make_async_remote_copy(
            src_ref=feat_hbm.at[:, pl.ds(0, FACE), :],
            dst_ref=low_layer,
            send_sem=halo_send.at[0],
            recv_sem=halo_recv.at[0],
            device_id={"blk": up},
            device_id_type=MESH,
        ).wait_recv()
        halo(1).wait_recv()

    @pl.when(me < count - 1)
    def _():
        halo(2).wait_recv()
        halo(3).wait_recv()

    def x_face(f, layer_ref, other_occ, x):
        wanted = nb[:, f : f + 1]
        target = jnp.where(wanted >= 0, wanted * FACE + iota((layer_rows, 1), 0) // slots, -1)
        pick = one_hot(col == target) * layer_occ(other_occ[...].astype(BF16), x)
        layer = layer_ref[...].reshape(layer_rows, channels)
        part = jnp.dot(pick, layer, preferred_element_type=F32).astype(BF16)
        return part.reshape(EDGE, EDGE, slots, channels)

    volume[0, 1 : EDGE + 1, 1 : EDGE + 1] = x_face(0, low_layer, low_occ, EDGE - 1)
    volume[EDGE + 1, 1 : EDGE + 1, 1 : EDGE + 1] = x_face(1, high_layer, high_occ, 0)

    loads[3].wait()
    scale = scale_ref[...]
    shift = shift_ref[...]

    @pl.loop(0, 1)
    def _(x):
        total = jnp.zeros((layer_rows, channels), F32)
        for tap in range(27):
            a, b, c = tap // 9, (tap // 3) % 3, tap % 3
            window = volume[x + a, b : b + EDGE, c : c + EDGE].reshape(layer_rows, channels)
            total = total + jnp.dot(window, weight[tap], preferred_element_type=F32)
        hidden = jnp.maximum(total * scale + shift, 0.0)
        for k in range(channels // LANES):
            acc[k, pl.ds(x * layer_rows, layer_rows), :] = hidden[:, k * LANES : (k + 1) * LANES]

    others(lambda at: x_from(at).wait_recv())

    @pl.loop(1, row)
    def _(i):
        z_to(i).wait_recv()

    for e in range(EXTRA):
        relay_out[e] = relay_x[far_entry(across, count + e)]
        relay_out[EXTRA + e] = relay_z[near_entry(beside, count + EXTRA + e)]
    for e in range(2 * EXTRA):
        relay(e).start()

    @pl.loop(1, EDGE)
    def _(x):
        total = jnp.zeros((layer_rows, channels), F32)
        for tap in range(27):
            a, b, c = tap // 9, (tap // 3) % 3, tap % 3
            window = volume[x + a, b : b + EDGE, c : c + EDGE].reshape(layer_rows, channels)
            total = total + jnp.dot(window, weight[tap], preferred_element_type=F32)
        hidden = jnp.maximum(total * scale + shift, 0.0)
        for k in range(channels // LANES):
            acc[k, pl.ds(x * layer_rows, layer_rows), :] = hidden[:, k * LANES : (k + 1) * LANES]

    @pl.loop(0, slots)
    def _(s):
        mine = jnp.where(iota((VOX, VOX), 0) == iota((VOX, VOX), 1), occ_ref[pl.ds(s, 1), :], 0)
        mask[pl.ds(s * VOX, VOX), :] = jnp.dot(
            mine.astype(BF16), jnp.ones((VOX, channels), BF16), preferred_element_type=F32
        )

    for s in range(slots):
        hidden = jnp.concatenate(
            [acc[k, pl.ds(s, VOX, stride=slots), :] for k in range(channels // LANES)],
            axis=1,
        )
        base[s] = hidden * mask[s * VOX : (s + 1) * VOX, :]

    overs[grp] = over[...]
    for i in range(1, groups):
        over_to(i).wait_recv()
    over_ref[0] = jnp.sum(overs[...])

    @pl.loop(0, half)
    def _(i):
        request(i, 1).wait_send()
        first_to(i, 1).wait_send()

    others(lambda at: request(at, 0).wait_send())
    others(lambda at: first_to(at, 0).wait_send())

    others(lambda at: x_to(at).wait_send())

    @pl.loop(1, row)
    def _(i):
        row_to(i).wait_send()
        z_to(i).wait_send()

    for e in range(2 * EXTRA):
        relay(e).wait_send()
    for i in range(1, groups):
        over_to(i).wait_send()

    @pl.when(me < count - 1)
    def _():
        halo(0).wait_send()
        halo(1).wait_send()

    @pl.when(me > 0)
    def _():
        halo(2).wait_send()
        halo(3).wait_send()

    @pl.loop(0, half)
    def _(i):
        first_from(i, 1).wait_recv()

    others(lambda at: first_from(at, 0).wait_recv())

    @pl.loop(1, row)
    def _(i):
        row_to(i).wait_recv()

    for e in range(2 * EXTRA):
        relay(e).wait_recv()

    for s in range(slots):
        moved = recv[place_s[s]].astype(F32)
        out_ref[s] = (base[s] + moved * mask[s * VOX : (s + 1) * VOX, :]).astype(BF16)


def per_device(
    features,
    occupancy,
    neighbors,
    previous,
    old_owner,
    old_slot,
    conv_weight,
    norm_scale,
    norm_shift,
    prev_weight,
):
    slots, vox, channels = features.shape
    count = lax.axis_size("blk")
    groups = lax.axis_size("grp")
    half, row = count // 2, count // 4
    hbm = pl.BlockSpec(memory_space=pl.ANY)
    volume_shape = (EDGE + 2, EDGE + 2, EDGE + 2, slots, channels)
    dma = pltpu.SemaphoreType.DMA
    return pl.pallas_call(
        functools.partial(kernel, count, groups, slots, channels),
        out_shape=[
            pltpu.VMEM(features.shape, BF16),
            pltpu.SMEM((1,), jnp.int32),
        ],
        in_specs=[hbm] * 10,
        out_specs=[
            pl.BlockSpec(memory_space=pltpu.VMEM),
            pl.BlockSpec(memory_space=pltpu.SMEM),
        ],
        scratch_shapes=[
            pltpu.SMEM((slots,), jnp.int32),
            pltpu.SMEM((slots,), jnp.int32),
            pltpu.VMEM((6, slots), jnp.int32),
            pltpu.VMEM((slots, vox), jnp.int32),
            pltpu.VMEM((1, channels), F32),
            pltpu.VMEM((1, channels), F32),
            pltpu.VMEM(features.shape, BF16),
            pltpu.VMEM(previous.shape, BF16),
            pltpu.VMEM(conv_weight.shape, BF16),
            pltpu.VMEM(prev_weight.shape, BF16),
            pltpu.VMEM(previous.shape, BF16),
            pltpu.VMEM((1, LANES), jnp.int32),
            pltpu.VMEM((half, 1, LANES), jnp.int32),
            pltpu.VMEM((half, 1, LANES), jnp.int32),
            pltpu.SMEM((count,), jnp.int32),
            pltpu.SMEM((count,), jnp.int32),
            pltpu.SMEM((slots,), jnp.int32),
            pltpu.VMEM((1, LANES), jnp.int32),
            pltpu.VMEM((groups, 1, LANES), jnp.int32),
            pltpu.VMEM((count, vox, channels), BF16),
            pltpu.VMEM((row, vox, channels), BF16),
            pltpu.VMEM((row, vox, channels), BF16),
            pltpu.VMEM((half, vox, channels), BF16),
            pltpu.VMEM((row, vox, channels), BF16),
            pltpu.VMEM((half, vox, channels), BF16),
            pltpu.VMEM((2 * EXTRA, vox, channels), BF16),
            pltpu.VMEM((count + row + 2 * EXTRA, vox, channels), BF16),
            pltpu.VMEM((slots, FACE, channels), BF16),
            pltpu.VMEM((slots, FACE, channels), BF16),
            pltpu.VMEM((slots, vox), jnp.int32),
            pltpu.VMEM((slots, vox), jnp.int32),
            pltpu.VMEM(volume_shape, BF16),
            pltpu.VMEM((channels // LANES, slots * vox, LANES), F32),
            pltpu.VMEM((slots * vox, channels), F32),
            pltpu.VMEM(features.shape, F32),
            dma((6,)),
            dma((6,)),
            dma((4,)),
            dma((4,)),
            dma((count,)),
            dma((count,)),
            dma((count,)),
            dma((count,)),
            dma((row,)),
            dma((row,)),
            dma((row,)),
            dma((row,)),
            dma((half,)),
            dma((half,)),
            dma((2 * EXTRA,)),
            dma((2 * EXTRA,)),
            pltpu.SemaphoreType.REGULAR,
            dma((groups,)),
            dma((groups,)),
        ],
        compiler_params=pltpu.CompilerParams(
            collective_id=0, has_side_effects=True, vmem_limit_bytes=66_000_000
        ),
        name="merge_blocks",
    )(
        old_owner[:, 0],
        old_slot,
        neighbors.T,
        norm_scale[None, :],
        norm_shift[None, :],
        features,
        previous,
        occupancy,
        conv_weight,
        prev_weight,
    )


def merge(*arrays):
    merged, over = per_device(*arrays)
    return lax.switch(over[0], [lambda: merged, lambda: merge_full(*arrays)])


def solution(mesh):
    in_specs = (
        P(("grp", "blk"), None, None),
        P(("grp", "blk"), None),
        P(("grp", "blk"), None),
        P(("grp", "blk"), None, None),
        P(("grp", "blk"), None),
        P(("grp", "blk")),
        P(),
        P(),
        P(),
        P(),
    )
    out_specs = P(("grp", "blk"), None, None)
    return jax.shard_map(
        merge, mesh=mesh, in_specs=in_specs, out_specs=out_specs, check_vma=False
    )
```
